32 devices in a mesh: dp: 16 (over z, y, core), tensor: 2 (over x).
Axes of the slice: x: 2, y: 2, z: 4, core: 2. Of those that a mesh axis runs over, the one named last changes fastest.
Arguments:
- tokens: bfloat16 [8192, 1024], P('dp'), may hold values from -6 to 6
- clip_lengths: int32 [16, 3], P('dp'), may hold values from 0 to 512, as said below
- attn_gain: float32 [1024], replicated, may hold values from 0.5 to 1.5
- attn_shift: float32 [1024], replicated, may hold values from -3 to 3
- qkv_weight: bfloat16 [3, 1024, 1024], P(None, None, 'tensor'), may hold values from -0.1875 to 0.1875
- qv_bias: float32 [2, 1024], P(None, 'tensor'), may hold values from -0.3 to 0.3
- out_weight: bfloat16 [1024, 1024], P('tensor'), may hold values from -4 to 4
- out_bias: float32 [1024], replicated, may hold values from -3 to 3
- mlp_gain: float32 [1024], replicated, may hold values from 0.5 to 1.5
- mlp_shift: float32 [1024], replicated, may hold values from -3 to 3
- up_weight: bfloat16 [1024, 4096], P(None, 'tensor'), may hold values from -0.1875 to 0.1875
- up_bias: float32 [4096], P('tensor'), may hold values from -3 to 3
- down_weight: bfloat16 [4096, 1024], P('tensor'), may hold values from -0.09375 to 0.09375
- down_bias: float32 [1024], replicated, may hold values from -3 to 3
- cotangent: bfloat16 [8192, 1024], P('dp'), may hold values from -6 to 6
Outputs:
- layer_output: bfloat16 [8192, 1024], P('dp')
- grad_tokens: bfloat16 [8192, 1024], P('dp')
- grad_attn_gain: float32 [1024], replicated
- grad_attn_shift: float32 [1024], replicated
- grad_qkv_weight: float32 [3, 1024, 1024], P(None, None, 'tensor')
- grad_qv_bias: float32 [2, 1024], P(None, 'tensor')
- grad_out_weight: float32 [1024, 1024], P('tensor')
- grad_out_bias: float32 [1024], replicated
- grad_mlp_gain: float32 [1024], replicated
- grad_mlp_shift: float32 [1024], replicated
- grad_up_weight: float32 [1024, 4096], P(None, 'tensor')
- grad_up_bias: float32 [4096], P('tensor')
- grad_down_weight: float32 [4096, 1024], P('tensor')
- grad_down_bias: float32 [1024], replicated
The draws below stay inside these ranges and needn't reach their ends.
Inputs may be any that keep to these rules, and one draw needn't show every extreme that they name: `clip_lengths`: row g lists the clips packed, in order, from the first of data group g's 512 rows; the rows after them are padding. In a quarter of the data groups (at least one), chosen by the seed, one clip fills all 512 rows; every other data group holds one clip of 341 to 426 tokens. Unused entries are 0.
All inputs are finite; a program needn't handle non-finite values.
Results may differ from the reference program's by a relative error of at most 0.012.
Values may be sent and summed in bfloat16 or wider, within the bound.
A program may use at most 192 MiB of HBM per device.

```python
from functools import partial
import jax
import jax.numpy as jnp
from jax import lax

D = 1024
H = 16
HS = 64
FF = 4096
TOK_DEV = 512
SLOTS = 3
TOKENS = 8192
N_DP = 16


def draw_clip_lengths(key, part):
    group_total = TOKENS // TOK_DEV
    group_order = jax.random.permutation(jax.random.fold_in(key, 11), group_total)
    long_group = group_order < max(1, group_total // 4)
    short_clip = jax.random.randint(jax.random.fold_in(key, 12), (group_total,), 2 * TOK_DEV // 3, 5 * TOK_DEV // 6 + 1)
    first_len = jnp.where(long_group, TOK_DEV, short_clip.astype(jnp.int32)).astype(jnp.int32)
    return jnp.zeros((group_total, SLOTS), jnp.int32).at[:, 0].set(first_len)


def steps_of(stream_key, shape, shards, smallest, high):
    factor_of, own = 1.0, jax.random.fold_in(stream_key, 6)
    for axis_at, parts in shards:
        steps = jnp.exp(jax.random.uniform(jax.random.fold_in(own, axis_at), (parts,), jnp.float32, smallest / len(shards), high / len(shards)))
        factor_of = factor_of * jnp.repeat(steps, shape[axis_at] // parts).reshape([-1 if axis == axis_at else 1 for axis in range(len(shape))])
    return factor_of


def gaussian(own_key, extent, scale, bound, cuts=(), held_as=jnp.bfloat16):
    result = scale * jax.random.normal(own_key, extent, jnp.float32)
    if cuts:
        result = result * steps_of(own_key, extent, cuts, -0.22, 0.18)
    return jnp.clip(result, -bound, bound).astype(held_as)


def setup_inputs(seed: int = 0) -> dict:
    splits = jax.random.split(jax.random.key(seed), 16)
    return {
        "tokens": gaussian(splits[0], (TOKENS, D), 1.0, 6.0, ((0, 16),)),
        "clip_lengths": draw_clip_lengths(jax.random.fold_in(splits[15], 71), 0),
        "attn_gain": jnp.clip(1.0 + 0.1 * jax.random.normal(splits[2], (D,), jnp.float32), 0.5, 1.5),
        "attn_shift": gaussian(splits[3], (D,), 0.3, 3.0, (), jnp.float32),
        "qkv_weight": gaussian(splits[4], (3, D, D), D ** -0.5, 0.1875, ((2, 2),)),
        "qv_bias": gaussian(splits[5], (2, D), 0.03, 0.3, ((1, 2),), jnp.float32),
        "out_weight": gaussian(splits[6], (D, D), (max(1, 4 * D // (3 * TOK_DEV))) ** -0.5, 4.0, ((0, 2),)),
        "out_bias": gaussian(splits[7], (D,), 0.3, 3.0, (), jnp.float32),
        "mlp_gain": jnp.clip(1.0 + 0.1 * jax.random.normal(splits[8], (D,), jnp.float32), 0.5, 1.5),
        "mlp_shift": gaussian(splits[9], (D,), 0.3, 3.0, (), jnp.float32),
        "up_weight": gaussian(splits[10], (D, FF), D ** -0.5, 0.1875, ((1, 2),)),
        "up_bias": gaussian(splits[11], (FF,), 0.3, 3.0, ((0, 2),), jnp.float32),
        "down_weight": gaussian(splits[12], (FF, D), FF ** -0.5, 0.09375, ((0, 2),)),
        "down_bias": gaussian(splits[13], (D,), 0.3, 3.0, (), jnp.float32),
        "cotangent": gaussian(splits[14], (TOKENS, D), 1.0, 6.0, ((0, 16),)),
    }


eps_norm = 1e-06
neg_big = -1e+30

@jax.custom_vjp
def low(v):
    return lax.optimization_barrier(v.astype(jnp.bfloat16)).astype(jnp.float32)

@jax.custom_vjp
def low_back(v):
    return v

def low_keep(v):
    return (low(v), None)

def low_pass(kept, grad):
    return (grad,)

def back_keep(v):
    return (v, None)

def back_low(kept, grad):
    return (low(grad),)
low.defvjp(low_keep, low_pass)
low_back.defvjp(back_keep, back_low)

def matmul(left_side, right_side):
    return jnp.dot(left_side, right_side, precision=lax.Precision.HIGHEST, preferred_element_type=jnp.float32)

def layer_norm(rows_in, gain, shift):
    row_mean = lax.optimization_barrier(jnp.mean(rows_in, axis=-1, keepdims=True))
    centred = rows_in - row_mean
    variance = lax.optimization_barrier(jnp.mean(centred * centred, axis=-1, keepdims=True))
    return centred * lax.rsqrt(variance + eps_norm) * gain + shift

def segment_rows(lengths):
    clip_ends = jnp.cumsum(lengths).astype(jnp.int32)
    row_index = jnp.arange(TOK_DEV, dtype=jnp.int32)
    return lax.optimization_barrier(jnp.sum((row_index[:, None] >= clip_ends[None, :]).astype(jnp.int32), axis=1))

def head_attention(queries, keys_in, values_in, same_clip):
    products = low_back(matmul(queries, keys_in.T))
    scores = jnp.where(same_clip, products * HS ** (-0.5), neg_big)
    row_max = lax.optimization_barrier(jnp.max(scores, axis=1, keepdims=True))
    weights = jnp.exp(scores - row_max)
    probabilities = weights / lax.optimization_barrier(jnp.sum(weights, axis=1, keepdims=True))
    return matmul(low(probabilities), values_in)

def group_attention(queries, keys_in, values_in, lengths):
    segments = segment_rows(lengths)
    same_clip = segments[:, None] == segments[None, :]
    head_fn = jax.checkpoint(head_attention)
    query_heads = queries.reshape(TOK_DEV, H, HS).transpose(1, 0, 2)
    key_heads = keys_in.reshape(TOK_DEV, H, HS).transpose(1, 0, 2)
    value_heads = values_in.reshape(TOK_DEV, H, HS).transpose(1, 0, 2)
    mapped = lax.map(lambda triple: head_fn(triple[0], triple[1], triple[2], same_clip), (query_heads, key_heads, value_heads))
    return mapped.transpose(1, 0, 2).reshape(TOK_DEV, D)

def forward(lengths, inputs, attn_gain, attn_shift, qkv_weight, qv_bias, out_weight, out_bias, mlp_gain, mlp_shift, up_weight, up_bias, down_weight, down_bias):
    first_low = low(layer_norm(inputs, attn_gain, attn_shift))
    queries = low(low_back(matmul(first_low, qkv_weight[0]) + qv_bias[0]))
    keys_in = low(low_back(matmul(first_low, qkv_weight[1])))
    values_in = low(low_back(matmul(first_low, qkv_weight[2]) + qv_bias[1]))
    group_fn = jax.checkpoint(group_attention)
    attended = lax.map(lambda quad: group_fn(quad[0], quad[1], quad[2], quad[3]), (queries.reshape(N_DP, TOK_DEV, D), keys_in.reshape(N_DP, TOK_DEV, D), values_in.reshape(N_DP, TOK_DEV, D), lengths))
    attended = low(low_back(attended.reshape(TOKENS, D)))
    resid = inputs + low_back(matmul(attended, out_weight)) + out_bias
    second_low = low(layer_norm(resid, mlp_gain, mlp_shift))
    pre_act = low_back(matmul(second_low, up_weight) + up_bias)
    hidden = low(jax.nn.gelu(pre_act, approximate=False))
    return resid + matmul(hidden, down_weight) + down_bias

def reference(tokens, clip_lengths, attn_gain, attn_shift, qkv_weight, qv_bias, out_weight, out_bias, mlp_gain, mlp_shift, up_weight, up_bias, down_weight, down_bias, cotangent):
    primals = (tokens.astype(jnp.float32), attn_gain, attn_shift, qkv_weight.astype(jnp.float32), qv_bias, out_weight.astype(jnp.float32), out_bias, mlp_gain, mlp_shift, up_weight.astype(jnp.float32), up_bias, down_weight.astype(jnp.float32), down_bias)
    output, pull_back = jax.vjp(partial(forward, clip_lengths), *primals)
    gradients = pull_back(cotangent.astype(jnp.float32))
    return (output.astype(jnp.bfloat16), gradients[0].astype(jnp.bfloat16), gradients[1], gradients[2], gradients[3], gradients[4], gradients[5], gradients[6], gradients[7], gradients[8], gradients[9], gradients[10], gradients[11], gradients[12])
```

```python
import jax
import jax.numpy as jnp
from jax import lax
from jax.experimental import pallas as pl
from jax.experimental.pallas import tpu as pltpu

MESH = pl.DeviceIdType.MESH
bf16, f32 = jnp.bfloat16, jnp.float32
CELL = 16
NSA = 6
STAGES = 6


def place():
    at = lax.axis_index("dp")
    base = (at // CELL) * CELL
    inner = at - base
    z = inner // 4
    y = (inner // 2) % 2
    core = inner % 2
    return base, z, y, core


class Summer:
    def __init__(self, loc_a, loc_b, bufs, out_a, out_b, sems):
        self.loc_a, self.loc_b = loc_a, loc_b
        (self.a1, self.a2, self.a3, self.b1, self.b2, self.b3) = bufs
        self.out_a, self.out_b = out_a, out_b
        self.as_, self.ar_, self.bs_, self.br_, self.ls_ = sems
        self.na = loc_a.shape[0]
        self.nb = loc_b.shape[0]
        self.ha = loc_a.shape[1] // 2
        self.hb = loc_b.shape[1] // 2
        base, z, y, core = place()
        self.y, self.core = y, core
        self.outer = jnp.logical_or(z == 0, z == 3)
        self.mid = jnp.logical_not(self.outer)
        self.mine = jnp.where(z >= 2, 1, 0)
        across = 3 - z
        toward = jnp.where(z < 2, 1 - z, 5 - z)
        tensor = lax.axis_index("tensor")

        def dev(zz, yy, cc):
            return (base + zz * 4 + yy * 2 + cc, tensor)

        self.to_sib = dev(z, y, 1 - core)
        self.to_y = dev(z, 1 - y, core)
        self.to_x = None
        self.to_mid = dev(across, y, core)
        self.to_z = dev(toward, y, core)

    def la(self, i, h):
        return self.loc_a.at[i, pl.ds(pl.multiple_of(h * self.ha, self.ha), self.ha), :]

    def lb(self, i, h):
        return self.loc_b.at[i, pl.ds(pl.multiple_of(h * self.hb, self.hb), self.hb), :]

    def oa(self, i, h, core):
        return self.out_a.at[i, core, pl.ds(pl.multiple_of(h * self.ha, self.ha), self.ha), :]

    def ob(self, i, h, core):
        w = self.loc_b.shape[2]
        return self.out_b.at[
            i,
            pl.ds(pl.multiple_of(h * self.hb, self.hb), self.hb),
            pl.ds(pl.multiple_of(core * w, w), w),
        ]

    def ca(self, i, kind, recv, src, dst, to):
        return pltpu.make_async_remote_copy(
            src, dst, self.as_.at[i, kind], self.ar_.at[i, recv], device_id=to, device_id_type=MESH
        )

    def cb(self, i, kind, recv, src, dst, to):
        return pltpu.make_async_remote_copy(
            src, dst, self.bs_.at[i, kind], self.br_.at[i, recv], device_id=to, device_id_type=MESH
        )

    def a_y(self, i):
        return self.ca(i, 0, 0, self.la(i, 1 - self.y), self.a1.at[i], self.to_y)

    def a_in(self, i):
        return self.ca(i, 1, 1, self.la(i, self.y), self.a2.at[i], self.to_z)

    def a_mid(self, i):
        return self.ca(i, 1, 2, self.la(i, self.y), self.a3.at[i], self.to_mid)

    def a_out(self, i):
        return self.ca(i, 2, 3, self.a2.at[i], self.oa(i, self.y, self.core), self.to_z)

    def a_done(self, i, kind, recv, src, to):
        return self.ca(i, kind, recv, src, self.oa(i, self.y, self.core), to)

    def a_keep(self, i):
        return pltpu.make_async_copy(self.a2.at[i], self.oa(i, self.y, self.core), self.ls_.at[0, i])

    def a_fwd(self, i):
        o = self.oa(i, 1 - self.y, self.core)
        return self.ca(i, 5, 6, o, o, self.to_sib)

    def step_a(self, i, stage):
        y = self.y
        if stage == 0:
            self.a_y(i).start()
        elif stage == 1:
            self.a_y(i).wait_recv()
            v = self.la(i, y)
            v[...] = (v[...].astype(f32) + self.a1[i].astype(f32)).astype(bf16)

            @pl.when(self.outer)
            def _():
                self.a_in(i).start()
        elif stage == 2:
            @pl.when(self.mid)
            def _():
                self.a_in(i).wait_recv()
                v = self.la(i, y)
                v[...] = (v[...].astype(f32) + self.a2[i].astype(f32)).astype(bf16)
                self.a_mid(i).start()
        elif stage == 3:
            @pl.when(self.mid)
            def _():
                self.a_mid(i).wait_recv()
                self.a2[i] = (self.la(i, y)[...].astype(f32) + self.a3[i].astype(f32)).astype(bf16)
                self.a_out(i).start()
                src = self.a2.at[i]
                self.a_done(i, 3, 4, src, self.to_y).start()
                self.a_done(i, 4, 5, src, self.to_sib).start()
                self.a_keep(i).start()
        elif stage == 4:
            @pl.when(self.outer)
            def _():
                self.a_out(i).wait_recv()
                src = self.oa(i, y, self.core)
                self.a_done(i, 3, 4, src, self.to_y).start()
                self.a_done(i, 4, 5, src, self.to_sib).start()
        elif stage == 5:
            self.a_done(i, 3, 4, self.oa(i, y, self.core), self.to_y).wait_recv()
            self.a_fwd(i).start()

    def end_a(self, i):
        src = self.a2.at[i]
        self.a_y(i).wait_send()
        self.a_in(i).wait_send()

        @pl.when(self.mid)
        def _():
            self.a_out(i).wait_send()
            self.a_keep(i).wait()

        self.a_done(i, 3, 4, src, self.to_y).wait_send()
        self.a_done(i, 4, 5, src, self.to_sib).wait_send()
        self.a_fwd(i).wait_send()
        self.a_done(i, 4, 5, src, self.to_sib).wait_recv()
        self.a_fwd(i).wait_recv()

    def b_in(self, i):
        return self.cb(i, 0, 0, self.loc_b.at[i], self.b1.at[i], self.to_z)

    def b_mid(self, i):
        return self.cb(i, 0, 1, self.lb(i, 1 - self.mine), self.b2.at[i], self.to_mid)

    def b_y(self, i):
        return self.cb(i, 1, 2, self.lb(i, self.mine), self.b3.at[i], self.to_y)

    def fin_b(self, i):
        return self.b1.at[i, pl.ds(0, self.hb), :]

    def b_done(self, i, kind, recv, src, h, to):
        return self.cb(i, kind, recv, src, self.ob(i, h, self.core), to)

    def b_keep(self, i):
        return pltpu.make_async_copy(
            self.fin_b(i), self.ob(i, self.mine, self.core), self.ls_.at[1, i]
        )

    def step_b(self, i, stage):
        mine, core = self.mine, self.core
        if stage == 0:
            @pl.when(self.outer)
            def _():
                self.b_in(i).start()
        elif stage == 1:
            @pl.when(self.mid)
            def _():
                self.b_in(i).wait_recv()
                self.loc_b[i] = (self.loc_b[i].astype(f32) + self.b1[i].astype(f32)).astype(bf16)
                self.b_mid(i).start()
        elif stage == 2:
            @pl.when(self.mid)
            def _():
                self.b_mid(i).wait_recv()
                v = self.lb(i, mine)
                v[...] = (v[...].astype(f32) + self.b2[i].astype(f32)).astype(bf16)
                self.b_y(i).start()
        elif stage == 3:
            @pl.when(self.mid)
            def _():
                self.b_y(i).wait_recv()
                fin = self.fin_b(i)
                fin[...] = (self.lb(i, mine)[...].astype(f32) + self.b3[i].astype(f32)).astype(bf16)
                self.b_done(i, 2, 4, fin, mine, self.to_mid).start()
                self.b_done(i, 3, 3, fin, mine, self.to_z).start()
                self.b_done(i, 4, 5, fin, mine, self.to_sib).start()
                self.b_keep(i).start()
        elif stage == 4:
            @pl.when(self.mid)
            def _():
                o = self.ob(i, 1 - mine, core)
                self.b_done(i, 2, 4, o, 1 - mine, self.to_mid).wait_recv()
                self.b_done(i, 5, 4, o, 1 - mine, self.to_z).start()
                self.b_done(i, 6, 6, o, 1 - mine, self.to_sib).start()

            @pl.when(self.outer)
            def _():
                o = self.ob(i, mine, core)
                self.b_done(i, 3, 3, o, mine, self.to_z).wait_recv()
                self.b_done(i, 4, 5, o, mine, self.to_sib).start()
        elif stage == 5:
            @pl.when(self.outer)
            def _():
                o = self.ob(i, 1 - mine, core)
                self.b_done(i, 5, 4, o, 1 - mine, self.to_z).wait_recv()
                self.b_done(i, 6, 6, o, 1 - mine, self.to_sib).start()

    def end_b(self, i):
        fin = self.fin_b(i)
        mine = self.mine

        @pl.when(self.outer)
        def _():
            self.b_in(i).wait_send()

        @pl.when(self.mid)
        def _():
            self.b_mid(i).wait_send()
            self.b_y(i).wait_send()
            self.b_done(i, 2, 4, fin, mine, self.to_mid).wait_send()
            self.b_done(i, 3, 3, fin, mine, self.to_z).wait_send()
            self.b_done(i, 5, 4, fin, mine, self.to_z).wait_send()
            self.b_keep(i).wait()

        self.b_done(i, 4, 5, fin, mine, self.to_sib).wait_send()
        self.b_done(i, 6, 6, fin, mine, self.to_sib).wait_send()
        self.b_done(i, 4, 5, fin, mine, self.to_sib).wait_recv()
        self.b_done(i, 6, 6, fin, mine, self.to_sib).wait_recv()

    def step(self, t):
        for stage in range(STAGES):
            i = t - stage

            @pl.when(jnp.logical_and(i >= 0, i < self.na))
            def _():
                self.step_a(i, stage)

            @pl.when(jnp.logical_and(i >= 0, i < self.nb))
            def _():
                self.step_b(i, stage)

    def steps(self, lo, hi):
        def body(t, _):
            self.step(t)
            return 0

        lax.fori_loop(lo, hi, body, 0)

    def end(self):
        def body_a(i, _):
            self.end_a(i)
            return 0

        def body_b(i, _):
            self.end_b(i)
            return 0

        lax.fori_loop(0, self.na, body_a, 0)
        lax.fori_loop(0, self.nb, body_b, 0)


def scratch_of(na, ra, wa, nb, rb, wb):
    return [
        pltpu.VMEM((na, ra // 2, wa), bf16),
        pltpu.VMEM((na, ra // 2, wa), bf16),
        pltpu.VMEM((na, ra // 2, wa), bf16),
        pltpu.VMEM((nb, rb, wb), bf16),
        pltpu.VMEM((nb, rb // 2, wb), bf16),
        pltpu.VMEM((nb, rb // 2, wb), bf16),
        pltpu.SemaphoreType.DMA((na, 6)),
        pltpu.SemaphoreType.DMA((na, 7)),
        pltpu.SemaphoreType.DMA((nb, 7)),
        pltpu.SemaphoreType.DMA((nb, 7)),
        pltpu.SemaphoreType.DMA((2, max(na, nb))),
    ]


def sum_kernel(in_a, in_b, out_a, out_b, loc_a, loc_b, a1, a2, a3, b1, b2, b3, as_, ar_, bs_, br_, ls_, lsem):
    ca = pltpu.make_async_copy(in_a, loc_a, lsem.at[0])
    cb = pltpu.make_async_copy(in_b, loc_b, lsem.at[1])
    ca.start()
    cb.start()
    s = Summer(loc_a, loc_b, (a1, a2, a3, b1, b2, b3), out_a, out_b, (as_, ar_, bs_, br_, ls_))
    ca.wait()
    cb.wait()
    s.steps(0, max(s.na, s.nb) + STAGES - 1)
    s.end()


def group_sum(in_a, in_b):
    na, ra, wa = in_a.shape
    nb, rb, wb = in_b.shape
    return pl.pallas_call(
        sum_kernel,
        out_shape=(
            jax.ShapeDtypeStruct((na, 2, ra, wa), bf16),
            jax.ShapeDtypeStruct((nb, rb, 2 * wb), bf16),
        ),
        in_specs=[pl.BlockSpec(memory_space=pl.ANY)] * 2,
        out_specs=[pl.BlockSpec(memory_space=pl.ANY)] * 2,
        scratch_shapes=[pltpu.VMEM(in_a.shape, bf16), pltpu.VMEM(in_b.shape, bf16)]
        + scratch_of(na, ra, wa, nb, rb, wb)
        + [pltpu.SemaphoreType.DMA((2,))],
        compiler_params=pltpu.CompilerParams(has_side_effects=True, vmem_limit_bytes=56 << 20),
        name="group_sum",
    )(in_a, in_b)

from jax.sharding import PartitionSpec as P

HS = 64


eps_norm = 1e-06
neg_big = -1e30


def matmul(left_side, right_side):
    return jnp.dot(left_side, right_side, preferred_element_type=jnp.float32)


def contract_rows(left_side, right_side):
    return lax.dot_general(
        left_side, right_side, (((0,), (0,)), ((), ())), preferred_element_type=jnp.float32
    )


def contract_cols(left_side, right_side):
    return lax.dot_general(
        left_side, right_side, (((1,), (1,)), ((), ())), preferred_element_type=jnp.float32
    )


def norm_forward(rows_in, gain, shift):
    row_mean = jnp.mean(rows_in, axis=-1, keepdims=True)
    centred = rows_in - row_mean
    variance = jnp.mean(centred * centred, axis=-1, keepdims=True)
    norm_scale = lax.rsqrt(variance + eps_norm)
    normed = centred * norm_scale
    return (normed, norm_scale, normed * gain + shift)


def norm_backward(grad_rows, normed, norm_scale, gain):
    grad_normed = grad_rows * gain
    mean_one = jnp.mean(grad_normed, axis=-1, keepdims=True)
    mean_two = jnp.mean(grad_normed * normed, axis=-1, keepdims=True)
    grad_in = norm_scale * (grad_normed - mean_one - normed * mean_two)
    return (grad_in, jnp.sum(grad_rows * normed, axis=0), jnp.sum(grad_rows, axis=0))


def gelu_parts(pre_act):
    normal_cdf = 0.5 * (1.0 + jax.scipy.special.erf(pre_act * 0.7071067811865476))
    normal_pdf = jnp.exp(-0.5 * pre_act * pre_act) * 0.3989422804014327
    return (pre_act * normal_cdf, normal_cdf + pre_act * normal_pdf)


def segment_rows(clip_lengths, length):
    first = clip_lengths[0, 0]
    second = first + clip_lengths[0, 1]
    clip_ends = jnp.stack([first, second, second + clip_lengths[0, 2]])
    row_index = jnp.arange(length, dtype=jnp.int32)
    return jnp.sum((row_index[:, None] >= clip_ends[None, :]).astype(jnp.int32), axis=1)


def attention_forward(queries, keys_low, values_low, segments, block_rows):
    length, head_count, head_width = queries.shape
    inv_scale = head_width ** (-0.5)
    block_count = length // block_rows

    def one_block(inputs):
        query_block, seg_block = inputs
        products = jnp.einsum(
            "qhd,khd->hqk", query_block, keys_low, preferred_element_type=jnp.float32
        )
        same_clip = seg_block[:, None] == segments[None, :]
        scores = jnp.where(same_clip[None], products * inv_scale, neg_big)
        row_max = jnp.max(scores, axis=2, keepdims=True)
        weights = jnp.exp(scores - row_max)
        row_total = jnp.sum(weights, axis=2, keepdims=True)
        weights_low = (weights / row_total).astype(jnp.bfloat16)
        attended = jnp.einsum(
            "hqk,khd->qhd", weights_low, values_low, preferred_element_type=jnp.float32
        )
        return (attended, (row_max + jnp.log(row_total))[:, :, 0])

    attended, log_totals = lax.map(
        one_block,
        (
            queries.reshape(block_count, block_rows, head_count, head_width),
            segments.reshape(block_count, block_rows),
        ),
    )
    return (attended.reshape(length, head_count * head_width), log_totals)


def attention_backward(
    queries, keys_low, values_low, segments, log_totals, grad_attended, block_rows
):
    length, head_count, head_width = queries.shape
    inv_scale = head_width ** (-0.5)
    block_count = length // block_rows

    def one_block(carried, inputs):
        grad_keys, grad_values = carried
        query_block, seg_block, total_block, grad_block = inputs
        products = jnp.einsum(
            "qhd,khd->hqk", query_block, keys_low, preferred_element_type=jnp.float32
        )
        same_clip = seg_block[:, None] == segments[None, :]
        scores = jnp.where(same_clip[None], products * inv_scale, neg_big)
        probabilities = jnp.exp(scores - total_block[:, :, None])
        grad_probs = jnp.einsum(
            "qhd,khd->hqk", grad_block, values_low, preferred_element_type=jnp.float32
        )
        row_inner = jnp.sum(probabilities * grad_probs, axis=2, keepdims=True)
        grad_scores = (probabilities * (grad_probs - row_inner) * inv_scale).astype(jnp.bfloat16)
        grad_queries = jnp.einsum(
            "hqk,khd->qhd", grad_scores, keys_low, preferred_element_type=jnp.float32
        )
        grad_keys = grad_keys + jnp.einsum(
            "hqk,qhd->khd", grad_scores, query_block, preferred_element_type=jnp.float32
        )
        grad_values = grad_values + jnp.einsum(
            "hqk,qhd->khd",
            probabilities.astype(jnp.bfloat16),
            grad_block,
            preferred_element_type=jnp.float32,
        )
        return ((grad_keys, grad_values), grad_queries)

    zero_grads = jnp.zeros((length, head_count, head_width), jnp.float32)
    shape_four = (block_count, block_rows, head_count, head_width)
    (grad_keys, grad_values), grad_queries = lax.scan(
        one_block,
        (zero_grads, zero_grads),
        (
            queries.reshape(shape_four),
            segments.reshape(block_count, block_rows),
            log_totals,
            grad_attended.reshape(shape_four),
        ),
    )
    flat_shape = (length, head_count * head_width)
    return (
        grad_queries.reshape(flat_shape),
        grad_keys.reshape(flat_shape),
        grad_values.reshape(flat_shape),
    )


def over_tensor(part):
    low = part.astype(jnp.bfloat16)
    other = lax.ppermute(low, "tensor", [(0, 1), (1, 0)])
    return low.astype(jnp.float32) + other.astype(jnp.float32)


def from_sibling(value):
    count = lax.axis_size("dp")
    return lax.ppermute(value, "dp", [(i, i ^ 1) for i in range(count)])


def pair_rows(value):
    core = lax.axis_index("dp") % 2
    other = from_sibling(value)
    first = jnp.where(core == 0, value, other)
    return jnp.concatenate([first, jnp.where(core == 0, other, value)], axis=0)


def pair_cols(value, pieces):
    core = lax.axis_index("dp") % 2
    rows, cols = value.shape
    halves = value.reshape(rows, pieces, 2, cols // pieces // 2)
    mine = jnp.where(core == 0, halves[:, :, 0], halves[:, :, 1])
    other = from_sibling(jnp.where(core == 0, halves[:, :, 1], halves[:, :, 0]))
    first = jnp.where(core == 0, mine, other)
    return jnp.concatenate([first, jnp.where(core == 0, other, mine)], axis=0)


def local(
    tokens,
    clip_lengths,
    attn_gain,
    attn_shift,
    qkv_weight,
    qv_bias,
    out_weight,
    out_bias,
    mlp_gain,
    mlp_shift,
    up_weight,
    up_bias,
    down_weight,
    down_bias,
    cotangent,
):
    length = tokens.shape[0]
    local_cols = qkv_weight.shape[2]
    head_count = local_cols // HS
    block_rows = min(512, length)
    segments = segment_rows(clip_lengths, length)
    inputs = tokens.astype(jnp.float32)
    normed_one, scale_one, shifted_one = norm_forward(inputs, attn_gain, attn_shift)
    first_low = shifted_one.astype(jnp.bfloat16)
    head_shape = (length, head_count, HS)
    queries = (
        (matmul(first_low, qkv_weight[0]) + qv_bias[0]).astype(jnp.bfloat16).reshape(head_shape)
    )
    keys_low = matmul(first_low, qkv_weight[1]).astype(jnp.bfloat16).reshape(head_shape)
    values_low = (
        (matmul(first_low, qkv_weight[2]) + qv_bias[1]).astype(jnp.bfloat16).reshape(head_shape)
    )
    attended, log_totals = attention_forward(queries, keys_low, values_low, segments, block_rows)
    attended_low = attended.astype(jnp.bfloat16)
    attn_part = matmul(attended_low, out_weight)
    attn_sum = over_tensor(attn_part)
    resid = inputs + attn_sum + out_bias
    normed_two, scale_two, shifted_two = norm_forward(resid, mlp_gain, mlp_shift)
    second_low = shifted_two.astype(jnp.bfloat16)
    pre_act = matmul(second_low, up_weight) + up_bias
    activated, gelu_slope = gelu_parts(pre_act)
    hidden_low = activated.astype(jnp.bfloat16)
    mlp_part = matmul(hidden_low, down_weight)
    mlp_sum = over_tensor(mlp_part)
    layer_output = (resid + mlp_sum + down_bias).astype(jnp.bfloat16)
    grad_hidden = contract_cols(cotangent, down_weight)
    grad_pre = (grad_hidden * gelu_slope).astype(jnp.bfloat16)
    up_bias_grad = jnp.sum(grad_pre.astype(jnp.float32), axis=0)
    back_part = contract_cols(grad_pre, up_weight)
    second_part = back_part
    pieces = hidden_low.shape[1] // 512
    pair_hidden = pair_cols(hidden_low, pieces)
    pair_pre = pair_cols(grad_pre, pieces)
    pair_cot = pair_rows(cotangent)
    pair_second = pair_rows(second_low)
    down_grad = jnp.einsum("rph,rd->phd", pair_hidden, pair_cot, preferred_element_type=jnp.float32)
    up_grad = jnp.einsum("rd,rph->pdh", pair_second, pair_pre, preferred_element_type=jnp.float32)
    second_sum = over_tensor(second_part)
    norm_two_grad, mlp_gain_grad, mlp_shift_grad = norm_backward(
        second_sum, normed_two, scale_two, mlp_gain
    )
    cot_full = cotangent.astype(jnp.float32)
    resid_grad = cot_full + norm_two_grad
    out_bias_grad = jnp.sum(resid_grad, axis=0)
    down_bias_grad = jnp.sum(cot_full, axis=0)
    branch_low = resid_grad.astype(jnp.bfloat16)
    out_grad = jnp.einsum(
        "rph,rd->phd", pair_cols(attended_low, 1), pair_rows(branch_low), preferred_element_type=jnp.float32
    )
    grad_attended = contract_cols(branch_low, out_weight).astype(jnp.bfloat16).reshape(head_shape)
    grad_queries, grad_keys, grad_values = attention_backward(
        queries, keys_low, values_low, segments, log_totals, grad_attended, block_rows
    )
    query_low = grad_queries.astype(jnp.bfloat16)
    key_low = grad_keys.astype(jnp.bfloat16)
    value_low = grad_values.astype(jnp.bfloat16)
    qv_grad = jnp.stack(
        [
            jnp.sum(query_low.astype(jnp.float32), axis=0),
            jnp.sum(value_low.astype(jnp.float32), axis=0),
        ]
    )
    pair_first = pair_rows(first_low)
    qkv_grad = jnp.concatenate(
        [
            jnp.einsum("rd,rph->pdh", pair_first, pair_cols(v, 1), preferred_element_type=jnp.float32)
            for v in (query_low, key_low, value_low)
        ]
    )
    back_part = (
        contract_cols(query_low, qkv_weight[0])
        + contract_cols(key_low, qkv_weight[1])
        + contract_cols(value_low, qkv_weight[2])
    )
    first_part = back_part
    first_sum = over_tensor(first_part)
    norm_one_grad, attn_gain_grad, attn_shift_grad = norm_backward(
        first_sum, normed_one, scale_one, attn_gain
    )
    grad_tokens = (resid_grad + norm_one_grad).astype(jnp.bfloat16)
    in_a = jnp.concatenate([down_grad, out_grad]).astype(jnp.bfloat16)
    in_b = jnp.concatenate([up_grad, qkv_grad]).astype(jnp.bfloat16)
    na, ra, wa = in_a.shape
    nb, rb, wb = in_b.shape
    sum_a, sum_b = group_sum(in_a.reshape(na * 2, ra // 2, wa), in_b.reshape(nb * 2, rb // 2, wb))
    groups = lax.axis_size("dp")
    if groups > CELL:
        cells = [[k * CELL + i for k in range(groups // CELL)] for i in range(CELL)]
        sum_a, sum_b = lax.psum(
            (sum_a.astype(f32), sum_b.astype(f32)), "dp", axis_index_groups=cells
        )
    sum_a = sum_a.reshape(na, 2, 2, ra // 2, wa).transpose(0, 2, 1, 3, 4).reshape(na, 2 * ra, wa)
    sum_b = sum_b.reshape(nb, rb, 2 * wb)
    down_flat = sum_a[: na - 1].reshape(-1, wa).astype(jnp.float32)
    out_flat = sum_a[na - 1].astype(jnp.float32)
    up_flat = sum_b[: nb - 3].transpose(1, 0, 2).reshape(rb, -1).astype(jnp.float32)
    qkv_flat = sum_b[nb - 3 :].astype(jnp.float32)
    (
        attn_gain_sum,
        attn_shift_sum,
        qv_sum,
        out_bias_sum,
        mlp_gain_sum,
        mlp_shift_sum,
        up_bias_sum,
        down_bias_sum,
    ) = lax.psum(
        (
            attn_gain_grad,
            attn_shift_grad,
            qv_grad,
            out_bias_grad,
            mlp_gain_grad,
            mlp_shift_grad,
            up_bias_grad,
            down_bias_grad,
        ),
        "dp",
    )
    return (
        layer_output,
        grad_tokens,
        attn_gain_sum,
        attn_shift_sum,
        qkv_flat.reshape(qkv_weight.shape),
        qv_sum,
        out_flat.reshape(out_weight.shape),
        out_bias_sum,
        mlp_gain_sum,
        mlp_shift_sum,
        up_flat.reshape(up_weight.shape),
        up_bias_sum,
        down_flat.reshape(down_weight.shape),
        down_bias_sum,
    )


def solution(mesh):
    placed = (
        P("dp", None),
        P("dp", None),
        P(),
        P(),
        P(None, None, "tensor"),
        P(None, "tensor"),
        P("tensor", None),
        P(),
        P(),
        P(),
        P(None, "tensor"),
        P("tensor"),
        P("tensor", None),
        P(),
        P("dp", None),
    )
    return jax.shard_map(
        local,
        mesh=mesh,
        in_specs=placed,
        out_specs=(
            P("dp", None),
            P("dp", None),
            P(),
            P(),
            P(None, None, "tensor"),
            P(None, "tensor"),
            P("tensor", None),
            P(),
            P(),
            P(),
            P(None, "tensor"),
            P("tensor"),
            P("tensor", None),
            P(),
        ),
        check_vma=False,
    )
```

```python
import jax
import jax.numpy as jnp
from jax import lax
from jax.experimental import pallas as pl
from jax.experimental.pallas import tpu as pltpu
from jax.sharding import PartitionSpec as P

MESH = pl.DeviceIdType.MESH
bf16, f32 = jnp.bfloat16, jnp.float32
CELL = 16
STAGES = 6


def place():
    at = lax.axis_index("dp")
    base = (at // CELL) * CELL
    inner = at - base
    z = inner // 4
    y = (inner // 2) % 2
    core = inner % 2
    return base, z, y, core


class Summer:
    def __init__(self, loc_a, loc_b, bufs, out_a, out_b, sems):
        self.loc_a, self.loc_b = loc_a, loc_b
        (self.a1, self.a2, self.a3, self.b1, self.b2, self.b3) = bufs
        self.out_a, self.out_b = out_a, out_b
        self.as_, self.ar_, self.bs_, self.br_, self.ls_ = sems
        self.na = loc_a.shape[0]
        self.nb = loc_b.shape[0]
        self.ha = loc_a.shape[1] // 2
        self.hb = loc_b.shape[1] // 2
        base, z, y, core = place()
        self.y, self.core = y, core
        self.outer = jnp.logical_or(z == 0, z == 3)
        self.mid = jnp.logical_not(self.outer)
        self.mine = jnp.where(z >= 2, 1, 0)
        across = 3 - z
        toward = jnp.where(z < 2, 1 - z, 5 - z)
        tensor = lax.axis_index("tensor")

        def dev(zz, yy, cc):
            return (base + zz * 4 + yy * 2 + cc, tensor)

        self.to_sib = dev(z, y, 1 - core)
        self.to_y = dev(z, 1 - y, core)
        self.to_mid = dev(across, y, core)
        self.to_z = dev(toward, y, core)

    def la(self, i, h):
        return self.loc_a.at[i, pl.ds(pl.multiple_of(h * self.ha, self.ha), self.ha), :]

    def lb(self, i, h):
        return self.loc_b.at[i, pl.ds(pl.multiple_of(h * self.hb, self.hb), self.hb), :]

    def oa(self, i, h, core):
        at = lax.rem(i, 2) * 2 * self.ha + h * self.ha
        return self.out_a.at[i // 2, core, pl.ds(pl.multiple_of(at, self.ha), self.ha), :]

    def ob(self, i, h, core):
        w = self.loc_b.shape[2]
        at = lax.rem(i, 2) * 2 * self.hb + h * self.hb
        return self.out_b.at[
            i // 2,
            pl.ds(pl.multiple_of(at, self.hb), self.hb),
            pl.ds(pl.multiple_of(core * w, w), w),
        ]

    def ca(self, i, kind, recv, src, dst, to):
        return pltpu.make_async_remote_copy(
            src, dst, self.as_.at[i, kind], self.ar_.at[i, recv], device_id=to, device_id_type=MESH
        )

    def cb(self, i, kind, recv, src, dst, to):
        return pltpu.make_async_remote_copy(
            src, dst, self.bs_.at[i, kind], self.br_.at[i, recv], device_id=to, device_id_type=MESH
        )

    def a_y(self, i):
        return self.ca(i, 0, 0, self.la(i, 1 - self.y), self.a1.at[i], self.to_y)

    def a_in(self, i):
        return self.ca(i, 1, 1, self.la(i, self.y), self.a2.at[i], self.to_z)

    def a_mid(self, i):
        return self.ca(i, 1, 2, self.la(i, self.y), self.a3.at[i], self.to_mid)

    def a_out(self, i):
        return self.ca(i, 2, 3, self.a2.at[i], self.oa(i, self.y, self.core), self.to_z)

    def a_done(self, i, kind, recv, src, to):
        return self.ca(i, kind, recv, src, self.oa(i, self.y, self.core), to)

    def a_keep(self, i):
        return pltpu.make_async_copy(self.a2.at[i], self.oa(i, self.y, self.core), self.ls_.at[0, i])

    def a_fwd(self, i):
        o = self.oa(i, 1 - self.y, self.core)
        return self.ca(i, 5, 6, o, o, self.to_sib)

    def step_a(self, i, stage):
        y = self.y
        if stage == 0:
            self.a_y(i).start()
        elif stage == 1:
            self.a_y(i).wait_recv()
            v = self.la(i, y)
            v[...] = (v[...].astype(f32) + self.a1[i].astype(f32)).astype(bf16)

            @pl.when(self.outer)
            def _():
                self.a_in(i).start()
        elif stage == 2:
            @pl.when(self.mid)
            def _():
                self.a_in(i).wait_recv()
                v = self.la(i, y)
                v[...] = (v[...].astype(f32) + self.a2[i].astype(f32)).astype(bf16)
                self.a_mid(i).start()
        elif stage == 3:
            @pl.when(self.mid)
            def _():
                self.a_mid(i).wait_recv()
                self.a2[i] = (self.la(i, y)[...].astype(f32) + self.a3[i].astype(f32)).astype(bf16)
                self.a_out(i).start()
                src = self.a2.at[i]
                self.a_done(i, 3, 4, src, self.to_y).start()
                self.a_done(i, 4, 5, src, self.to_sib).start()
                self.a_keep(i).start()
        elif stage == 4:
            @pl.when(self.outer)
            def _():
                self.a_out(i).wait_recv()
                src = self.oa(i, y, self.core)
                self.a_done(i, 3, 4, src, self.to_y).start()
                self.a_done(i, 4, 5, src, self.to_sib).start()
        elif stage == 5:
            self.a_done(i, 3, 4, self.oa(i, y, self.core), self.to_y).wait_recv()
            self.a_fwd(i).start()

    def end_a(self, i):
        src = self.a2.at[i]
        self.a_y(i).wait_send()
        self.a_in(i).wait_send()

        @pl.when(self.mid)
        def _():
            self.a_out(i).wait_send()
            self.a_keep(i).wait()

        self.a_done(i, 3, 4, src, self.to_y).wait_send()
        self.a_done(i, 4, 5, src, self.to_sib).wait_send()
        self.a_fwd(i).wait_send()
        self.a_done(i, 4, 5, src, self.to_sib).wait_recv()
        self.a_fwd(i).wait_recv()

    def b_in(self, i):
        return self.cb(i, 0, 0, self.loc_b.at[i], self.b1.at[i], self.to_z)

    def b_mid(self, i):
        return self.cb(i, 0, 1, self.lb(i, 1 - self.mine), self.b2.at[i], self.to_mid)

    def b_y(self, i):
        return self.cb(i, 1, 2, self.lb(i, self.mine), self.b3.at[i], self.to_y)

    def fin_b(self, i):
        return self.b1.at[i, pl.ds(0, self.hb), :]

    def b_done(self, i, kind, recv, src, h, to):
        return self.cb(i, kind, recv, src, self.ob(i, h, self.core), to)

    def b_keep(self, i):
        return pltpu.make_async_copy(
            self.fin_b(i), self.ob(i, self.mine, self.core), self.ls_.at[1, i]
        )

    def step_b(self, i, stage):
        mine, core = self.mine, self.core
        if stage == 0:
            @pl.when(self.outer)
            def _():
                self.b_in(i).start()
        elif stage == 1:
            @pl.when(self.mid)
            def _():
                self.b_in(i).wait_recv()
                self.loc_b[i] = (self.loc_b[i].astype(f32) + self.b1[i].astype(f32)).astype(bf16)
                self.b_mid(i).start()
        elif stage == 2:
            @pl.when(self.mid)
            def _():
                self.b_mid(i).wait_recv()
                v = self.lb(i, mine)
                v[...] = (v[...].astype(f32) + self.b2[i].astype(f32)).astype(bf16)
                self.b_y(i).start()
        elif stage == 3:
            @pl.when(self.mid)
            def _():
                self.b_y(i).wait_recv()
                fin = self.fin_b(i)
                fin[...] = (self.lb(i, mine)[...].astype(f32) + self.b3[i].astype(f32)).astype(bf16)
                self.b_done(i, 2, 4, fin, mine, self.to_mid).start()
                self.b_done(i, 3, 3, fin, mine, self.to_z).start()
                self.b_done(i, 4, 5, fin, mine, self.to_sib).start()
                self.b_keep(i).start()
        elif stage == 4:
            @pl.when(self.mid)
            def _():
                o = self.ob(i, 1 - mine, core)
                self.b_done(i, 2, 4, o, 1 - mine, self.to_mid).wait_recv()
                self.b_done(i, 5, 4, o, 1 - mine, self.to_z).start()
                self.b_done(i, 6, 6, o, 1 - mine, self.to_sib).start()

            @pl.when(self.outer)
            def _():
                o = self.ob(i, mine, core)
                self.b_done(i, 3, 3, o, mine, self.to_z).wait_recv()
                self.b_done(i, 4, 5, o, mine, self.to_sib).start()
        elif stage == 5:
            @pl.when(self.outer)
            def _():
                o = self.ob(i, 1 - mine, core)
                self.b_done(i, 5, 4, o, 1 - mine, self.to_z).wait_recv()
                self.b_done(i, 6, 6, o, 1 - mine, self.to_sib).start()

    def end_b(self, i):
        fin = self.fin_b(i)
        mine = self.mine

        @pl.when(self.outer)
        def _():
            self.b_in(i).wait_send()

        @pl.when(self.mid)
        def _():
            self.b_mid(i).wait_send()
            self.b_y(i).wait_send()
            self.b_done(i, 2, 4, fin, mine, self.to_mid).wait_send()
            self.b_done(i, 3, 3, fin, mine, self.to_z).wait_send()
            self.b_done(i, 5, 4, fin, mine, self.to_z).wait_send()
            self.b_keep(i).wait()

        self.b_done(i, 4, 5, fin, mine, self.to_sib).wait_send()
        self.b_done(i, 6, 6, fin, mine, self.to_sib).wait_send()
        self.b_done(i, 4, 5, fin, mine, self.to_sib).wait_recv()
        self.b_done(i, 6, 6, fin, mine, self.to_sib).wait_recv()

    def step(self, t):
        for stage in range(STAGES):
            i = t - stage

            @pl.when(jnp.logical_and(i >= 0, i < self.na))
            def _():
                self.step_a(i, stage)

            @pl.when(jnp.logical_and(i >= 0, i < self.nb))
            def _():
                self.step_b(i, stage)

    def steps(self, lo, hi):
        def body(t, _):
            self.step(t)
            return 0

        lax.fori_loop(lo, hi, body, 0)

    def end(self):
        def body_a(i, _):
            self.end_a(i)
            return 0

        def body_b(i, _):
            self.end_b(i)
            return 0

        lax.fori_loop(0, self.na, body_a, 0)
        lax.fori_loop(0, self.nb, body_b, 0)


def scratch_of(na, ra, wa, nb, rb, wb):
    return [
        pltpu.VMEM((na, ra // 2, wa), bf16),
        pltpu.VMEM((na, ra // 2, wa), bf16),
        pltpu.VMEM((na, ra // 2, wa), bf16),
        pltpu.VMEM((nb, rb, wb), bf16),
        pltpu.VMEM((nb, rb // 2, wb), bf16),
        pltpu.VMEM((nb, rb // 2, wb), bf16),
        pltpu.SemaphoreType.DMA((na, 6)),
        pltpu.SemaphoreType.DMA((na, 7)),
        pltpu.SemaphoreType.DMA((nb, 7)),
        pltpu.SemaphoreType.DMA((nb, 7)),
        pltpu.SemaphoreType.DMA((2, max(na, nb))),
    ]


def split_rows(value):
    rows, cols = value.shape
    return jnp.sum(value.reshape(rows // 8, 8, cols), axis=0)


def erf(value):
    x = jnp.clip(value, -4.0, 4.0)
    x2 = x * x
    top = -2.72614225801306e-10
    for c in (
        2.77068142495902e-08,
        -2.10102402082508e-06,
        -5.69250639462346e-05,
        -7.34990630326855e-04,
        -2.95459980854025e-03,
        -1.60960333262415e-02,
    ):
        top = top * x2 + c
    low = -1.45660718464996e-05
    for c in (
        -2.13374055278905e-04,
        -1.68282697438203e-03,
        -7.37332916720468e-03,
        -1.42647390514189e-02,
    ):
        low = low * x2 + c
    return x * top / low


def gelu_parts(u):
    cdf = 0.5 * (1.0 + erf(u * 0.7071067811865476))
    pdf = jnp.exp(-0.5 * u * u) * 0.3989422804014327
    return u * cdf, cdf + u * pdf


def normed(rows_in):
    centred = rows_in - jnp.mean(rows_in, axis=-1, keepdims=True)
    scale = lax.rsqrt(jnp.mean(centred * centred, axis=-1, keepdims=True) + 1e-06)
    return centred * scale, scale


def mm(left, right):
    return jnp.dot(left, right, preferred_element_type=f32)


def mm_tn(left, right):
    return lax.dot_general(left, right, (((0,), (0,)), ((), ())), preferred_element_type=f32)


def mm_nt(left, right):
    return lax.dot_general(left, right, (((1,), (1,)), ((), ())), preferred_element_type=f32)


LINKS = {
    "w": 4, "c": 1, "o": 4, "osib": 2, "h2t": 4, "act": 4, "pre": 4, "x0": 4, "x1": 4, "x2": 4,
    "dyb": 1, "h1t": 1, "dqkv": 6, "small": 5,
}
LINK_AT = {}
for _name, _count in LINKS.items():
    LINK_AT[_name] = sum(LINKS[n] for n in LINK_AT)
N_LINKS = sum(LINKS.values())


def layer_kernel(
    clip, again, ashift, qvb, outb, mgain, mshift, upb, downb,
    tok_h, wqkv_h, wout_h, wup_h, wdown_h, cot_h,
    lo_h, gt_h, out_a, out_b, small_h,
    tok, wqkv, wout, wup, wdown, cpair, hid, h1t, q, k, v, o_own, o_peer, o_sib, y1, h2t,
    act, pre, act_sib, pre_sib, xs0, xs1, xr0, xr1, dy1, dob, scr0, scr1, small, small_r, sums,
    loc_a, loc_b, a1, a2, a3, b1, b2, b3,
    as_, ar_, bs_, br_, ls_, lsem, ssem, rsem,
):
    rows = tok.shape[0]
    width = tok.shape[1]
    sm = Summer(loc_a, loc_b, (a1, a2, a3, b1, b2, b3), out_a, out_b, (as_, ar_, bs_, br_, ls_))
    base, z, y, core = place()
    t = lax.axis_index("tensor")
    to_x = (lax.axis_index("dp"), 1 - t)
    to_sib, to_y = sm.to_sib, sm.to_y

    def rc(name, i, src, dst, to):
        at = LINK_AT[name] + i
        return pltpu.make_async_remote_copy(
            src, dst, ssem.at[at], rsem.at[at], device_id=to, device_id_type=MESH
        )

    def cols(i, n=128):
        return pl.ds(pl.multiple_of(i * n, n), n)

    def loop(n, body):
        def wrapped(i, _):
            body(i)
            return 0

        lax.fori_loop(0, n, wrapped, 0)

    def load(i, src, dst):
        return pltpu.make_async_copy(src, dst, lsem.at[i])

    loads = [
        load(0, tok_h, tok),
        load(1, wqkv_h, wqkv),
        load(2, wout_h, wout.at[t]),
        load(3, wup_h, wup),
        load(4, cot_h, cpair.at[0]),
        load(5, wdown_h, wdown),
    ]
    quarter = 2 * y + core
    part = wout_h.shape[0] // 4

    def rows_of(i):
        return pl.ds(pl.multiple_of(i * part, part), part)

    def w_at(i):
        return wout.at[1 - t, rows_of(i), :]

    w_out = rc("w", 0, wout_h.at[rows_of(quarter), :], wout.at[t, rows_of(quarter), :], to_x)
    w_in = rc("w", 0, wout_h.at[rows_of(quarter), :], w_at(quarter), to_x)
    w_y = rc("w", 1, w_at(quarter), w_at(quarter), to_y)
    w_s0 = rc("w", 2, w_at(quarter), w_at(quarter), to_sib)
    other = 2 * (1 - y) + core
    w_s1 = rc("w", 3, w_at(other), w_at(other), to_sib)
    c_out = rc("c", 0, cot_h, cpair.at[1], to_sib)
    loads[0].start()
    loads[1].start()
    w_out.start()
    for item in loads[2:]:
        item.start()
    c_out.start()

    loads[0].wait()
    tile = 64

    def norm_one(i):
        r = pl.ds(pl.multiple_of(i * tile, tile), tile)
        n1, _ = normed(tok[r, :].astype(f32))
        hid[r, :] = (n1 * again[...] + ashift[...]).astype(bf16)

    loop(rows // tile, norm_one)
    loads[1].wait()
    heads_w = q.shape[1]
    lane = lax.broadcasted_iota(jnp.int32, (1, 128), 1)

    def half_of(value, e):
        keep = (lane < 64) if e == 0 else (lane >= 64)
        return jnp.where(keep, value.astype(f32), 0.0).astype(bf16)

    end0 = clip[0, 0]
    end1 = end0 + clip[0, 1]
    end2 = end1 + clip[0, 2]

    def seg_of(index):
        one = lambda e: (index >= e).astype(jnp.int32)
        return one(end0) + one(end1) + one(end2)

    key_seg = seg_of(lax.broadcasted_iota(jnp.int32, (1, rows), 1))
    sub = 32

    def softmax_rows(i):
        r = pl.ds(pl.multiple_of(i * sub, sub), sub)
        row_seg = seg_of(lax.broadcasted_iota(jnp.int32, (sub, 1), 0) + i * sub)
        s = jnp.where(row_seg == key_seg, scr0[r, :], -1e30)
        w = jnp.exp(s - jnp.max(s, axis=1, keepdims=True))
        return r, w * (1.0 / jnp.sum(w, axis=1, keepdims=True))

    def make_qkv(g):
        c4 = cols(g, 256)
        h = hid[...]
        q[:, c4] = ((mm(h, wqkv[0, :, c4]) + qvb[pl.ds(0, 1), c4]).astype(bf16) * 0.125).astype(bf16)
        k[:, c4] = mm(h, wqkv[1, :, c4]).astype(bf16)
        v[:, c4] = (mm(h, wqkv[2, :, c4]) + qvb[pl.ds(1, 1), c4]).astype(bf16)

    def o_send(pr):
        return rc("o", pr, o_own.at[:, cols(pr)], o_peer.at[:, cols(pr)], to_x)

    def osib_send(pr):
        m = lax.rem(pr, 2)
        return rc("osib", m, o_own.at[:, cols(pr)], o_sib.at[:, cols(m)], to_sib)

    def attend(pr):
        c2 = cols(pr)
        total = None
        for e in range(2):
            scr0[...] = mm_nt(half_of(q[:, c2], e), k[:, c2])

            def soft(i):
                r, p = softmax_rows(i)
                xs0[r, pl.ds(0, rows)] = p.astype(bf16)

            loop(rows // sub, soft)
            term = mm(xs0[:, pl.ds(0, rows)], half_of(v[:, c2], e))
            total = term if total is None else total + term
        o_own[:, c2] = total.astype(bf16)
        o_send(pr).start()

        @pl.when(pr // 2 == 1 - core)
        def _():
            osib_send(pr).start()

    def group_of_heads(g):
        make_qkv(g)
        attend(2 * g)
        attend(2 * g + 1)

    loop(heads_w // 256, group_of_heads)

    w_in.wait_recv()
    w_y.start()
    w_s0.start()
    loads[2].wait()
    nrow = 128

    def own_part(i):
        r = pl.ds(pl.multiple_of(i * nrow, nrow), nrow)
        y1[r, :] = mm(o_own[r, :], wout[t])

    loop(rows // nrow, own_part)
    w_y.wait_recv()
    w_s1.start()
    w_s0.wait_recv()
    w_s1.wait_recv()
    w_y.wait_send()
    w_s0.wait_send()
    w_s1.wait_send()
    for pr in range(4):
        o_send(pr).wait_recv()

    def h2t_send(i):
        return rc("h2t", i, h2t.at[0, :, cols(i, nrow)], h2t.at[1, :, cols(i, nrow)], to_sib)

    def norm_two(i):
        r = pl.ds(pl.multiple_of(i * nrow, nrow), nrow)
        x = tok[r, :].astype(f32)
        y = x + (y1[r, :] + mm(o_peer[r, :], wout[1 - t])) + outb[...]
        y1[r, :] = y
        n2, _ = normed(y)
        h2 = (n2 * mgain[...] + mshift[...]).astype(bf16)
        hid_two[r, :] = h2
        h2t[0, :, cols(i, nrow)] = h2.T
        h2t_send(i).start()

    hid_two = xs1
    loop(rows // nrow, norm_two)

    loads[3].wait()
    loads[4].wait()
    loads[5].wait()
    c_out.wait_recv()

    def act_send(j):
        c4 = cols(2 * j + 1 - core, 256)
        return rc("act", j, act.at[:, c4], act_sib.at[j], to_sib)

    def pre_send(j):
        c4 = cols(2 * j + 1 - core, 256)
        return rc("pre", j, pre.at[:, c4], pre_sib.at[j], to_sib)

    def hidden(piece):
        c4 = cols(piece, 256)
        half = pl.ds(0, 256)
        scr0[:, half] = mm(hid_two[...], wup[:, c4]) + upb[:, c4]
        scr1[:, half] = mm_nt(cpair[0], wdown[c4, :])

        def slope(i, total):
            r = pl.ds(pl.multiple_of(i * tile, tile), tile)
            a, d = gelu_parts(scr0[r, half])
            du = (scr1[r, half] * d).astype(bf16)
            act[r, c4] = a.astype(bf16)
            pre[r, c4] = du
            return total + split_rows(du.astype(f32))

        total = lax.fori_loop(0, rows // tile, slope, jnp.zeros((8, 256), f32))
        row = 6 + piece // 4
        small[pl.ds(row, 1), cols(lax.rem(piece, 4), 256)] = jnp.sum(total, axis=0, keepdims=True)

    def chunk(j):
        hidden(2 * j + 1 - core)
        act_send(j).start()
        pre_send(j).start()
        hidden(2 * j + core)
        mine = cols(2 * j + core, 256)
        act_send(j).wait_recv()
        for n in range(width // 512):
            wide = pl.ds(n * 512, 512)
            block = mm_tn(act[:, mine], cpair[0, :, wide]) + mm_tn(act_sib[j], cpair[1, :, wide])
            low = block.astype(bf16)
            loc_a[2 * j, :, wide] = low[:128]
            loc_a[2 * j + 1, :, wide] = low[128:]
        pre_send(j).wait_recv()
        for m in range(2):
            high = pl.ds(m * 512, 512)
            loc_b[2 * j + m] = (
                mm(h2t[0, high, :], pre[:, mine]) + mm(h2t[1, high, :], pre_sib[j])
            ).astype(bf16)

    def first_wait():
        for i in range(4):
            h2t_send(i).wait_recv()

    first_wait()
    chunk(0)
    sm.step(0)
    chunk(1)
    chunk(2)
    sm.step(1)
    chunk(3)

    def x_send(name, n, src, dst):
        return rc(name, n, src.at[:, cols(n, 256)], dst.at[:, cols(n, 256)], to_x)

    def back_two(n):
        xs0[:, cols(n, 256)] = mm_nt(pre[...], wup[cols(n, 256), :]).astype(bf16)
        x_send("x0", n, xs0, xr0).start()

    loop(width // 256, back_two)
    sm.step(2)

    def forward_two(n):
        xs1[:, cols(n, 256)] = mm(act[...], wdown[:, cols(n, 256)]).astype(bf16)
        x_send("x1", n, xs1, xr1).start()

    loop(width // 256, forward_two)

    def turn_first(i):
        r = pl.ds(pl.multiple_of(i * nrow, nrow), nrow)
        h1t[0, :, cols(i, nrow)] = hid[r, :].T

    loop(rows // nrow, turn_first)
    h1t_out = rc("h1t", 0, h1t.at[0], h1t.at[1], to_sib)
    h1t_out.start()

    def cot_sum(i, total):
        r = pl.ds(pl.multiple_of(i * tile, tile), tile)
        return total + split_rows(cpair[0, r, :].astype(f32))

    total = lax.fori_loop(0, rows // tile, cot_sum, jnp.zeros((8, width), f32))
    small[pl.ds(8, 1), :] = jnp.sum(total, axis=0, keepdims=True)
    sm.step(3)
    sm.step(4)

    for n in range(4):
        x_send("x0", n, xs0, xr0).wait_recv()
    sums[...] = jnp.zeros_like(sums)
    back = 32
    dyb = xr0

    def norm_two_back(i):
        r = pl.ds(pl.multiple_of(i * back, back), back)
        g = xs0[r, :].astype(f32) + xr0[r, :].astype(f32)
        n2, r2 = normed(y1[r, :])
        gn = g * n2
        sums[0] += split_rows(gn)
        sums[1] += split_rows(g)
        e2 = g * mgain[...]
        m1 = jnp.mean(e2, axis=-1, keepdims=True)
        m2 = jnp.mean(e2 * n2, axis=-1, keepdims=True)
        d = cpair[0, r, :].astype(f32) + r2 * (e2 - m1 - n2 * m2)
        sums[2] += split_rows(d)
        dy1[r, :] = d
        dyb[r, :] = d.astype(bf16)

    loop(rows // back, norm_two_back)
    dyb_out = rc("dyb", 0, dyb, wout.at[1 - t], to_sib)
    dyb_out.start()
    for i, row in enumerate((4, 5, 3)):
        small[pl.ds(row, 1), :] = jnp.sum(sums[i], axis=0, keepdims=True)
    for n in range(4):
        x_send("x0", n, xs0, xr0).wait_send()

    def back_heads(n):
        dob[:, cols(n, 256)] = mm_nt(dyb[...], wout[t, cols(n, 256), :]).astype(bf16)

    loop(heads_w // 256, back_heads)
    sm.step(5)
    osib_send(0).wait_recv()
    osib_send(1).wait_recv()
    dyb_out.wait_recv()
    for n in range(width // 512):
        wide = pl.ds(n * 512, 512)
        low = (
            mm_tn(o_own[:, cols(core, 256)], dyb[:, wide]) + mm_tn(o_sib[...], wout[1 - t, :, wide])
        ).astype(bf16)
        loc_a[8, :, wide] = low[:128]
        loc_a[9, :, wide] = low[128:]

    def dqkv_send(w, m, src, pr):
        return rc("dqkv", 2 * w + m, src.at[:, cols(pr)], act_sib.at[w, :, cols(m)], to_sib)

    def attend_back(pr):
        c2 = cols(pr)
        p_at, ds_at = pl.ds(0, rows), pl.ds(rows, rows)
        dq = dk = dv = None
        for e in range(2):
            q_e, do_e = half_of(q[:, c2], e), half_of(dob[:, c2], e)
            scr0[...] = mm_nt(q_e, k[:, c2])
            scr1[...] = mm_nt(do_e, v[:, c2])

            def soft(i):
                r, p = softmax_rows(i)
                dp = scr1[r, :]
                inner = jnp.sum(p * dp, axis=1, keepdims=True)
                xs0[r, p_at] = p.astype(bf16)
                xs0[r, ds_at] = (p * (dp - inner)).astype(bf16)

            loop(rows // sub, soft)
            terms = (
                mm(xs0[:, ds_at], half_of(k[:, c2], e)) * 0.125,
                mm_tn(xs0[:, ds_at], q_e),
                mm_tn(xs0[:, p_at], do_e),
            )
            dq, dk, dv = terms if dq is None else (dq + terms[0], dk + terms[1], dv + terms[2])
        q[:, c2] = dq.astype(bf16)
        k[:, c2] = dk.astype(bf16)
        v[:, c2] = dv.astype(bf16)
        small[pl.ds(2, 1), c2] = jnp.sum(q[:, c2].astype(f32), axis=0, keepdims=True)
        small[pl.ds(2, 1), cols(pr + 4)] = jnp.sum(v[:, c2].astype(f32), axis=0, keepdims=True)

    def theirs(m):
        pr = 2 * (1 - core) + m
        attend_back(pr)
        for w, src in enumerate((q, k, v)):
            dqkv_send(w, m, src, pr).start()

    loop(2, theirs)
    sm.step(6)

    def ours(m):
        attend_back(2 * core + m)

    loop(2, ours)
    sm.step(7)
    h1t_out.wait_recv()
    for w, src in enumerate((q, k, v)):
        for m in range(2):
            dqkv_send(w, m, src, m).wait_recv()
        for m in range(2):
            high = pl.ds(m * 512, 512)
            loc_b[8 + 2 * w + m] = (
                mm(h1t[0, high, :], src[:, cols(core, 256)]) + mm(h1t[1, high, :], act_sib[w])
            ).astype(bf16)
    sm.step(8)

    for n in range(4):
        x_send("x1", n, xs1, xr1).wait_recv()

    def finish(i):
        r = pl.ds(pl.multiple_of(i * tile, tile), tile)
        hid[r, :] = (
            y1[r, :] + (xs1[r, :].astype(f32) + xr1[r, :].astype(f32)) + downb[...]
        ).astype(bf16)

    loop(rows // tile, finish)
    lo_out = load(6, hid, lo_h)
    lo_out.start()

    last = wdown.at[pl.ds(0, rows), :]

    def back_one(n):
        c4 = cols(n, 256)
        xs0[:, c4] = (
            mm_nt(q[...], wqkv[0, c4, :]) + mm_nt(k[...], wqkv[1, c4, :]) + mm_nt(v[...], wqkv[2, c4, :])
        ).astype(bf16)
        x_send("x2", n, xs0, last).start()

    loop(width // 256, back_one)
    sm.step(9)
    sm.step(10)
    for n in range(4):
        x_send("x2", n, xs0, last).wait_recv()
    sums[...] = jnp.zeros_like(sums)

    def norm_one_back(i):
        r = pl.ds(pl.multiple_of(i * back, back), back)
        g = xs0[r, :].astype(f32) + wdown[r, :].astype(f32)
        n1, r1 = normed(tok[r, :].astype(f32))
        gn = g * n1
        sums[0] += split_rows(gn)
        sums[1] += split_rows(g)
        e1 = g * again[...]
        m1 = jnp.mean(e1, axis=-1, keepdims=True)
        m2 = jnp.mean(e1 * n1, axis=-1, keepdims=True)
        tok[r, :] = (dy1[r, :] + r1 * (e1 - m1 - n1 * m2)).astype(bf16)

    loop(rows // back, norm_one_back)
    gt_out = load(7, tok, gt_h)
    gt_out.start()
    for i, row in enumerate((0, 1)):
        small[pl.ds(row, 1), :] = jnp.sum(sums[i], axis=0, keepdims=True)

    def small_rc(i, src, to):
        return rc("small", i, src, small_r.at[i], to)

    small_sib = small_rc(0, small, to_sib)
    small_y = small_rc(1, small_r.at[0], to_y)
    small_in = small_rc(2, small_r.at[1], sm.to_z)
    small_mid = small_rc(3, small_r.at[2], sm.to_mid)
    small_out = small_rc(4, small_r.at[3], sm.to_z)
    small_sib.start()
    sm.step(11)
    small_sib.wait_recv()
    small_r[0] += small[...]
    small_y.start()
    sm.step(12)
    small_y.wait_recv()
    small_r[1] += small_r[0]

    @pl.when(sm.outer)
    def _():
        small_in.start()

    sm.step(13)

    @pl.when(sm.mid)
    def _():
        small_in.wait_recv()
        small_r[2] += small_r[1]
        small_mid.start()

    sm.step(14)

    @pl.when(sm.mid)
    def _():
        small_mid.wait_recv()
        small_r[3] += small_r[2]
        small_out.start()

    sm.steps(15, max(sm.na, sm.nb) + STAGES - 1)

    @pl.when(sm.outer)
    def _():
        small_out.wait_recv()

    keep = load(8, small_r.at[jnp.where(sm.outer, 4, 3)], small_h)
    keep.start()

    sm.end()
    w_out.wait_send()
    c_out.wait_send()
    h1t_out.wait_send()
    dyb_out.wait_send()
    for i in range(4):
        o_send(i).wait_send()
        h2t_send(i).wait_send()
        act_send(i).wait_send()
        pre_send(i).wait_send()
        x_send("x1", i, xs1, xr1).wait_send()
        x_send("x2", i, xs0, last).wait_send()
    for m in range(2):
        osib_send(m).wait_send()
        for w, src in enumerate((q, k, v)):
            dqkv_send(w, m, src, m).wait_send()
    small_sib.wait_send()
    small_y.wait_send()

    @pl.when(sm.outer)
    def _():
        small_in.wait_send()

    @pl.when(sm.mid)
    def _():
        small_mid.wait_send()
        small_out.wait_send()

    lo_out.wait()
    gt_out.wait()
    keep.wait()


def layer(clip, vectors, tokens, wqkv, wout, wup, wdown, cot):
    rows, width = tokens.shape
    heads_w = wqkv.shape[2]
    hidden = wup.shape[1]
    big = pl.BlockSpec(memory_space=pl.ANY)
    small = pl.BlockSpec(memory_space=pltpu.VMEM)
    na, nb = 10, 14
    vm = lambda *shape: pltpu.VMEM(shape, bf16)
    vf = lambda *shape: pltpu.VMEM(shape, f32)
    return pl.pallas_call(
        layer_kernel,
        out_shape=(
            jax.ShapeDtypeStruct((rows, width), bf16),
            jax.ShapeDtypeStruct((rows, width), bf16),
            jax.ShapeDtypeStruct((na // 2, 2, 256, width), bf16),
            jax.ShapeDtypeStruct((nb // 2, width, heads_w), bf16),
            jax.ShapeDtypeStruct((16, width), f32),
        ),
        in_specs=[pl.BlockSpec(memory_space=pltpu.SMEM)] + [small] * len(vectors) + [big] * 6,
        out_specs=[big] * 5,
        scratch_shapes=[
            vm(rows, width),
            vm(*wqkv.shape),
            vm(2, *wout.shape),
            vm(*wup.shape),
            vm(*wdown.shape),
            vm(2, rows, width),
            vm(rows, width),
            vm(2, width, rows),
            vm(rows, heads_w),
            vm(rows, heads_w),
            vm(rows, heads_w),
            vm(rows, heads_w),
            vm(rows, heads_w),
            vm(rows, 256),
            vf(rows, width),
            vm(2, width, rows),
            vm(rows, hidden),
            vm(rows, hidden),
            vm(4, rows, 256),
            vm(4, rows, 256),
            vm(rows, width),
            vm(rows, width),
            vm(rows, width),
            vm(rows, width),
            vf(rows, width),
            vm(rows, heads_w),
            vf(rows, rows),
            vf(rows, rows),
            vf(16, width),
            vf(5, 16, width),
            vf(3, 8, width),
            vm(na, 128, width),
            vm(nb, 512, 256),
        ]
        + scratch_of(na, 128, width, nb, 512, 256)
        + [
            pltpu.SemaphoreType.DMA((9,)),
            pltpu.SemaphoreType.DMA((N_LINKS,)),
            pltpu.SemaphoreType.DMA((N_LINKS,)),
        ],
        compiler_params=pltpu.CompilerParams(has_side_effects=True, vmem_limit_bytes=VMEM_BYTES),
        name="layer",
    )(clip, *vectors, tokens, wqkv, wout, wup, wdown, cot)


VMEM_BYTES = 60 << 20


def widen_kernel(a_in, b_in, s_in, down, out, up, qkv, ag, ash, qv, ob, mg, ms, ub, db):
    down[...] = a_in[pl.ds(0, 4)].astype(f32)
    out[...] = a_in[4].astype(f32)
    for j in range(4):
        up[:, pl.ds(j * 512, 512)] = b_in[j].astype(f32)
    qkv[...] = b_in[pl.ds(4, 3)].astype(f32)

    @pl.when(pl.program_id(0) == 0)
    def _():
        for ref, row in ((ag, 0), (ash, 1), (ob, 3), (mg, 4), (ms, 5), (db, 8)):
            ref[...] = s_in[pl.ds(row, 1), :]
        qv[pl.ds(0, 1), :] = s_in[pl.ds(2, 1), pl.ds(0, 512)]
        qv[pl.ds(1, 1), :] = s_in[pl.ds(2, 1), pl.ds(512, 512)]
        ub[:, pl.ds(0, 1024)] = s_in[pl.ds(6, 1), :]
        ub[:, pl.ds(1024, 1024)] = s_in[pl.ds(7, 1), :]


def widen(sum_a, sum_b, small):
    steps = 8
    a = sum_a.reshape(5, 512, 1024)
    whole = lambda *shape: pl.BlockSpec(shape, lambda i: (0,) * len(shape))
    got = pl.pallas_call(
        widen_kernel,
        grid=(steps,),
        in_specs=[
            pl.BlockSpec((5, 512 // steps, 1024), lambda i: (0, i, 0)),
            pl.BlockSpec((7, 1024 // steps, 512), lambda i: (0, i, 0)),
            whole(16, 1024),
        ],
        out_specs=[
            pl.BlockSpec((4, 512 // steps, 1024), lambda i: (0, i, 0)),
            pl.BlockSpec((512 // steps, 1024), lambda i: (i, 0)),
            pl.BlockSpec((1024 // steps, 2048), lambda i: (i, 0)),
            pl.BlockSpec((3, 1024 // steps, 512), lambda i: (0, i, 0)),
            whole(1, 1024), whole(1, 1024), whole(2, 512), whole(1, 1024),
            whole(1, 1024), whole(1, 1024), whole(1, 2048), whole(1, 1024),
        ],
        out_shape=[
            jax.ShapeDtypeStruct((4, 512, 1024), f32),
            jax.ShapeDtypeStruct((512, 1024), f32),
            jax.ShapeDtypeStruct((1024, 2048), f32),
            jax.ShapeDtypeStruct((3, 1024, 512), f32),
        ]
        + [
            jax.ShapeDtypeStruct(s, f32)
            for s in ((1, 1024), (1, 1024), (2, 512), (1, 1024), (1, 1024), (1, 1024), (1, 2048), (1, 1024))
        ],
        compiler_params=pltpu.CompilerParams(vmem_limit_bytes=40 << 20),
        name="widen",
    )(a, sum_b, small)
    down, out, up, qkv, ag, ash, qv, ob, mg, ms, ub, db = got
    flat = lambda v: v.reshape(-1)
    return (
        flat(ag), flat(ash), qkv, qv, out, flat(ob), flat(mg), flat(ms), up, flat(ub),
        down.reshape(2048, 1024), flat(db),
    )


def local(
    tokens, clip_lengths, attn_gain, attn_shift, qkv_weight, qv_bias, out_weight, out_bias,
    mlp_gain, mlp_shift, up_weight, up_bias, down_weight, down_bias, cotangent,
):
    row = lambda v: v.reshape(1, -1)
    vectors = (
        row(attn_gain), row(attn_shift), qv_bias, row(out_bias), row(mlp_gain), row(mlp_shift),
        row(up_bias), row(down_bias),
    )
    layer_output, grad_tokens, sum_a, sum_b, small = layer(
        clip_lengths, vectors, tokens, qkv_weight, out_weight, up_weight, down_weight, cotangent
    )
    groups = lax.axis_size("dp")
    if groups > CELL:
        cells = [[k * CELL + i for k in range(groups // CELL)] for i in range(CELL)]
        wide = (sum_a.astype(f32), sum_b.astype(f32), small)
        sum_a, sum_b, small = lax.psum(wide, "dp", axis_index_groups=cells)
    return (layer_output, grad_tokens, *widen(sum_a, sum_b, small))


def solution(mesh):
    placed = (
        P("dp", None), P("dp", None), P(), P(), P(None, None, "tensor"), P(None, "tensor"),
        P("tensor", None), P(), P(), P(), P(None, "tensor"), P("tensor"), P("tensor", None), P(),
        P("dp", None),
    )
    return jax.shard_map(
        local,
        mesh=mesh,
        in_specs=placed,
        out_specs=(
            P("dp", None), P("dp", None), P(), P(), P(None, None, "tensor"), P(None, "tensor"),
            P("tensor", None), P(), P(), P(), P(None, "tensor"), P("tensor"), P("tensor", None), P(),
        ),
        check_vma=False,
    )
```

```python
import jax
import jax.numpy as jnp
from jax import lax
from jax.experimental import pallas as pl
from jax.experimental.pallas import tpu as pltpu
from jax.sharding import PartitionSpec as P

MESH = pl.DeviceIdType.MESH
bf16, f32 = jnp.bfloat16, jnp.float32
CELL = 16
STAGES = 6


def place():
    at = lax.axis_index("dp")
    base = (at // CELL) * CELL
    inner = at - base
    z = inner // 4
    y = (inner // 2) % 2
    core = inner % 2
    return base, z, y, core


class Summer:
    def __init__(self, loc_a, loc_b, bufs, out_a, out_b, sems):
        self.loc_a, self.loc_b = loc_a, loc_b
        (self.a1, self.a2, self.a3, self.b1, self.b2, self.b3) = bufs
        self.out_a, self.out_b = out_a, out_b
        self.as_, self.ar_, self.bs_, self.br_, self.ls_ = sems
        self.na = loc_a.shape[0]
        self.nb = loc_b.shape[0]
        self.ha = loc_a.shape[1] // 2
        self.hb = loc_b.shape[1] // 2
        base, z, y, core = place()
        self.y, self.core = y, core
        self.outer = jnp.logical_or(z == 0, z == 3)
        self.mid = jnp.logical_not(self.outer)
        self.mine = jnp.where(z >= 2, 1, 0)
        across = 3 - z
        toward = jnp.where(z < 2, 1 - z, 5 - z)
        tensor = lax.axis_index("tensor")

        def dev(zz, yy, cc):
            return (base + zz * 4 + yy * 2 + cc, tensor)

        self.to_sib = dev(z, y, 1 - core)
        self.to_y = dev(z, 1 - y, core)
        self.to_mid = dev(across, y, core)
        self.to_z = dev(toward, y, core)

    def la(self, i, h):
        return self.loc_a.at[i, pl.ds(pl.multiple_of(h * self.ha, self.ha), self.ha), :]

    def lb(self, i, h):
        return self.loc_b.at[i, pl.ds(pl.multiple_of(h * self.hb, self.hb), self.hb), :]

    def oa(self, i, h, core):
        at = lax.rem(i, 2) * 2 * self.ha + h * self.ha
        return self.out_a.at[i // 2, core, pl.ds(pl.multiple_of(at, self.ha), self.ha), :]

    def ob(self, i, h, core):
        w = self.loc_b.shape[2]
        at = lax.rem(i, 2) * 2 * self.hb + h * self.hb
        return self.out_b.at[
            i // 2,
            pl.ds(pl.multiple_of(at, self.hb), self.hb),
            pl.ds(pl.multiple_of(core * w, w), w),
        ]

    def ca(self, i, kind, recv, src, dst, to):
        return pltpu.make_async_remote_copy(
            src, dst, self.as_.at[i, kind], self.ar_.at[i, recv], device_id=to, device_id_type=MESH
        )

    def cb(self, i, kind, recv, src, dst, to):
        return pltpu.make_async_remote_copy(
            src, dst, self.bs_.at[i, kind], self.br_.at[i, recv], device_id=to, device_id_type=MESH
        )

    def a_y(self, i):
        return self.ca(i, 0, 0, self.la(i, 1 - self.y), self.a1.at[i], self.to_y)

    def a_in(self, i):
        return self.ca(i, 1, 1, self.la(i, self.y), self.a2.at[i], self.to_z)

    def a_mid(self, i):
        return self.ca(i, 1, 2, self.la(i, self.y), self.a3.at[i], self.to_mid)

    def a_out(self, i):
        return self.ca(i, 2, 3, self.a2.at[i], self.oa(i, self.y, self.core), self.to_z)

    def a_done(self, i, kind, recv, src, to):
        return self.ca(i, kind, recv, src, self.oa(i, self.y, self.core), to)

    def a_keep(self, i):
        return pltpu.make_async_copy(self.a2.at[i], self.oa(i, self.y, self.core), self.ls_.at[0, i])

    def a_fwd(self, i):
        o = self.oa(i, 1 - self.y, self.core)
        return self.ca(i, 5, 6, o, o, self.to_sib)

    def step_a(self, i, stage):
        y = self.y
        if stage == 0:
            self.a_y(i).start()
        elif stage == 1:
            self.a_y(i).wait_recv()
            v = self.la(i, y)
            v[...] = (v[...].astype(f32) + self.a1[i].astype(f32)).astype(bf16)

            @pl.when(self.outer)
            def _():
                self.a_in(i).start()
        elif stage == 2:
            @pl.when(self.mid)
            def _():
                self.a_in(i).wait_recv()
                v = self.la(i, y)
                v[...] = (v[...].astype(f32) + self.a2[i].astype(f32)).astype(bf16)
                self.a_mid(i).start()
        elif stage == 3:
            @pl.when(self.mid)
            def _():
                self.a_mid(i).wait_recv()
                self.a2[i] = (self.la(i, y)[...].astype(f32) + self.a3[i].astype(f32)).astype(bf16)
                self.a_out(i).start()
                src = self.a2.at[i]
                self.a_done(i, 3, 4, src, self.to_y).start()
                self.a_done(i, 4, 5, src, self.to_sib).start()
                self.a_keep(i).start()
        elif stage == 4:
            @pl.when(self.outer)
            def _():
                self.a_out(i).wait_recv()
                src = self.oa(i, y, self.core)
                self.a_done(i, 3, 4, src, self.to_y).start()
                self.a_done(i, 4, 5, src, self.to_sib).start()
        elif stage == 5:
            self.a_done(i, 3, 4, self.oa(i, y, self.core), self.to_y).wait_recv()
            self.a_fwd(i).start()

    def end_a(self, i):
        src = self.a2.at[i]
        self.a_y(i).wait_send()
        self.a_in(i).wait_send()

        @pl.when(self.mid)
        def _():
            self.a_out(i).wait_send()
            self.a_keep(i).wait()

        self.a_done(i, 3, 4, src, self.to_y).wait_send()
        self.a_done(i, 4, 5, src, self.to_sib).wait_send()
        self.a_fwd(i).wait_send()
        self.a_done(i, 4, 5, src, self.to_sib).wait_recv()
        self.a_fwd(i).wait_recv()

    def b_in(self, i):
        return self.cb(i, 0, 0, self.loc_b.at[i], self.b1.at[i], self.to_z)

    def b_mid(self, i):
        return self.cb(i, 0, 1, self.lb(i, 1 - self.mine), self.b2.at[i], self.to_mid)

    def b_y(self, i):
        return self.cb(i, 1, 2, self.lb(i, self.mine), self.b3.at[i], self.to_y)

    def fin_b(self, i):
        return self.b1.at[i, pl.ds(0, self.hb), :]

    def b_done(self, i, kind, recv, src, h, to):
        return self.cb(i, kind, recv, src, self.ob(i, h, self.core), to)

    def b_keep(self, i):
        return pltpu.make_async_copy(
            self.fin_b(i), self.ob(i, self.mine, self.core), self.ls_.at[1, i]
        )

    def step_b(self, i, stage):
        mine, core = self.mine, self.core
        if stage == 0:
            @pl.when(self.outer)
            def _():
                self.b_in(i).start()
        elif stage == 1:
            @pl.when(self.mid)
            def _():
                self.b_in(i).wait_recv()
                self.loc_b[i] = (self.loc_b[i].astype(f32) + self.b1[i].astype(f32)).astype(bf16)
                self.b_mid(i).start()
        elif stage == 2:
            @pl.when(self.mid)
            def _():
                self.b_mid(i).wait_recv()
                v = self.lb(i, mine)
                v[...] = (v[...].astype(f32) + self.b2[i].astype(f32)).astype(bf16)
                self.b_y(i).start()
        elif stage == 3:
            @pl.when(self.mid)
            def _():
                self.b_y(i).wait_recv()
                fin = self.fin_b(i)
                fin[...] = (self.lb(i, mine)[...].astype(f32) + self.b3[i].astype(f32)).astype(bf16)
                self.b_done(i, 2, 4, fin, mine, self.to_mid).start()
                self.b_done(i, 3, 3, fin, mine, self.to_z).start()
                self.b_done(i, 4, 5, fin, mine, self.to_sib).start()
                self.b_keep(i).start()
        elif stage == 4:
            @pl.when(self.mid)
            def _():
                o = self.ob(i, 1 - mine, core)
                self.b_done(i, 2, 4, o, 1 - mine, self.to_mid).wait_recv()
                self.b_done(i, 5, 4, o, 1 - mine, self.to_z).start()
                self.b_done(i, 6, 6, o, 1 - mine, self.to_sib).start()

            @pl.when(self.outer)
            def _():
                o = self.ob(i, mine, core)
                self.b_done(i, 3, 3, o, mine, self.to_z).wait_recv()
                self.b_done(i, 4, 5, o, mine, self.to_sib).start()
        elif stage == 5:
            @pl.when(self.outer)
            def _():
                o = self.ob(i, 1 - mine, core)
                self.b_done(i, 5, 4, o, 1 - mine, self.to_z).wait_recv()
                self.b_done(i, 6, 6, o, 1 - mine, self.to_sib).start()

    def end_b(self, i):
        fin = self.fin_b(i)
        mine = self.mine

        @pl.when(self.outer)
        def _():
            self.b_in(i).wait_send()

        @pl.when(self.mid)
        def _():
            self.b_mid(i).wait_send()
            self.b_y(i).wait_send()
            self.b_done(i, 2, 4, fin, mine, self.to_mid).wait_send()
            self.b_done(i, 3, 3, fin, mine, self.to_z).wait_send()
            self.b_done(i, 5, 4, fin, mine, self.to_z).wait_send()
            self.b_keep(i).wait()

        self.b_done(i, 4, 5, fin, mine, self.to_sib).wait_send()
        self.b_done(i, 6, 6, fin, mine, self.to_sib).wait_send()
        self.b_done(i, 4, 5, fin, mine, self.to_sib).wait_recv()
        self.b_done(i, 6, 6, fin, mine, self.to_sib).wait_recv()

    def step(self, t):
        for stage in range(STAGES):
            i = t - stage

            @pl.when(jnp.logical_and(i >= 0, i < self.na))
            def _():
                self.step_a(i, stage)

            @pl.when(jnp.logical_and(i >= 0, i < self.nb))
            def _():
                self.step_b(i, stage)

    def steps(self, lo, hi):
        def body(t, _):
            self.step(t)
            return 0

        lax.fori_loop(lo, hi, body, 0)

    def end(self):
        def body_a(i, _):
            self.end_a(i)
            return 0

        def body_b(i, _):
            self.end_b(i)
            return 0

        lax.fori_loop(0, self.na, body_a, 0)
        lax.fori_loop(0, self.nb, body_b, 0)


def scratch_of(na, ra, wa, nb, rb, wb):
    return [
        pltpu.VMEM((na, ra // 2, wa), bf16),
        pltpu.VMEM((na, ra // 2, wa), bf16),
        pltpu.VMEM((na, ra // 2, wa), bf16),
        pltpu.VMEM((nb, rb, wb), bf16),
        pltpu.VMEM((nb, rb // 2, wb), bf16),
        pltpu.VMEM((nb, rb // 2, wb), bf16),
        pltpu.SemaphoreType.DMA((na, 6)),
        pltpu.SemaphoreType.DMA((na, 7)),
        pltpu.SemaphoreType.DMA((nb, 7)),
        pltpu.SemaphoreType.DMA((nb, 7)),
        pltpu.SemaphoreType.DMA((2, max(na, nb))),
    ]


def split_rows(value):
    rows, cols = value.shape
    return jnp.sum(value.reshape(rows // 8, 8, cols), axis=0)


def erf(value):
    x = jnp.clip(value, -4.0, 4.0)
    x2 = x * x
    top = -2.72614225801306e-10
    for c in (
        2.77068142495902e-08,
        -2.10102402082508e-06,
        -5.69250639462346e-05,
        -7.34990630326855e-04,
        -2.95459980854025e-03,
        -1.60960333262415e-02,
    ):
        top = top * x2 + c
    low = -1.45660718464996e-05
    for c in (
        -2.13374055278905e-04,
        -1.68282697438203e-03,
        -7.37332916720468e-03,
        -1.42647390514189e-02,
    ):
        low = low * x2 + c
    return x * top / low


def gelu_parts(u):
    cdf = 0.5 * (1.0 + erf(u * 0.7071067811865476))
    pdf = jnp.exp(-0.5 * u * u) * 0.3989422804014327
    return u * cdf, cdf + u * pdf


def normed(rows_in):
    centred = rows_in - jnp.mean(rows_in, axis=-1, keepdims=True)
    scale = lax.rsqrt(jnp.mean(centred * centred, axis=-1, keepdims=True) + 1e-06)
    return centred * scale, scale


def mm(left, right):
    return jnp.dot(left, right, preferred_element_type=f32)


def mm_tn(left, right):
    return lax.dot_general(left, right, (((0,), (0,)), ((), ())), preferred_element_type=f32)


def mm_nt(left, right):
    return lax.dot_general(left, right, (((1,), (1,)), ((), ())), preferred_element_type=f32)


LINKS = {
    "w": 4, "c": 1, "o": 4, "osib": 2, "h2t": 4, "act": 4, "pre": 4, "x0": 4, "x1": 4, "x2": 4,
    "dyb": 1, "h1t": 1, "dqkv": 6, "small": 5,
}
LINK_AT = {}
for _name, _count in LINKS.items():
    LINK_AT[_name] = sum(LINKS[n] for n in LINK_AT)
N_LINKS = sum(LINKS.values())


def layer_kernel(
    clip, again, ashift, qvb, outb, mgain, mshift, upb, downb,
    tok_h, wqkv_h, wout_h, wup_h, wdown_h, cot_h,
    lo_h, gt_h, out_a, out_b, small_h,
    tok, wqkv, wout, wup, wdown, cpair, hid, q, k, v, o_own, o_peer, o_sib, y1, h2t,
    act, pre, act_sib, pre_sib, xs0, xs1, xr0, xr1, dy1, dob, small, small_r, sums,
    loc_a, loc_b, a1, a2, a3, b1, b2, b3,
    as_, ar_, bs_, br_, ls_, lsem, ssem, rsem,
):
    rows = tok.shape[0]
    width = tok.shape[1]
    sm = Summer(loc_a, loc_b, (a1, a2, a3, b1, b2, b3), out_a, out_b, (as_, ar_, bs_, br_, ls_))
    base, z, y, core = place()
    t = lax.axis_index("tensor")
    to_x = (lax.axis_index("dp"), 1 - t)
    to_sib, to_y = sm.to_sib, sm.to_y

    def rc(name, i, src, dst, to):
        at = LINK_AT[name] + i
        return pltpu.make_async_remote_copy(
            src, dst, ssem.at[at], rsem.at[at], device_id=to, device_id_type=MESH
        )

    def cols(i, n=128):
        return pl.ds(pl.multiple_of(i * n, n), n)

    def loop(n, body, unroll=False):
        def wrapped(i, _):
            body(i)
            return 0

        lax.fori_loop(0, n, wrapped, 0, unroll=unroll)

    def load(i, src, dst):
        return pltpu.make_async_copy(src, dst, lsem.at[i])

    loads = [
        load(0, tok_h, tok),
        load(1, wqkv_h, wqkv),
        load(2, wout_h, wout.at[t]),
        load(3, wup_h, wup),
        load(4, cot_h, cpair.at[0]),
        load(5, wdown_h, wdown),
    ]
    quarter = 2 * y + core
    part = wout_h.shape[0] // 4

    def rows_of(i):
        return pl.ds(pl.multiple_of(i * part, part), part)

    def w_at(i):
        return wout.at[1 - t, rows_of(i), :]

    w_out = rc("w", 0, wout_h.at[rows_of(quarter), :], wout.at[t, rows_of(quarter), :], to_x)
    w_in = rc("w", 0, wout_h.at[rows_of(quarter), :], w_at(quarter), to_x)
    w_y = rc("w", 1, w_at(quarter), w_at(quarter), to_y)
    w_s0 = rc("w", 2, w_at(quarter), w_at(quarter), to_sib)
    other = 2 * (1 - y) + core
    w_s1 = rc("w", 3, w_at(other), w_at(other), to_sib)
    c_out = rc("c", 0, cot_h, cpair.at[1], to_sib)
    loads[0].start()
    loads[1].start()
    w_out.start()
    for item in loads[2:]:
        item.start()
    c_out.start()

    loads[0].wait()
    tile = 64

    def norm_one(i):
        r = pl.ds(pl.multiple_of(i * tile, tile), tile)
        n1, _ = normed(tok[r, :].astype(f32))
        hid[r, :] = (n1 * again[...] + ashift[...]).astype(bf16)

    loop(rows // tile, norm_one, True)
    loads[1].wait()
    heads_w = q.shape[1]
    lane = lax.broadcasted_iota(jnp.int32, (1, 128), 1)

    def half_of(value, e):
        keep = (lane < 64) if e == 0 else (lane >= 64)
        return jnp.where(keep, value.astype(f32), 0.0).astype(bf16)

    end0 = clip[0, 0]
    end1 = end0 + clip[0, 1]
    end2 = end1 + clip[0, 2]

    def seg_of(index):
        one = lambda e: (index >= e).astype(jnp.int32)
        return one(end0) + one(end1) + one(end2)

    key_seg = seg_of(lax.broadcasted_iota(jnp.int32, (1, rows), 1))
    def same_clip(at, count):
        return seg_of(lax.broadcasted_iota(jnp.int32, (count, 1), 0) + at) == key_seg

    def softmax(products, same):
        s = jnp.where(same, products, -1e30)
        w = jnp.exp(s - jnp.max(s, axis=1, keepdims=True))
        return w * (1.0 / jnp.sum(w, axis=1, keepdims=True))

    def make_qkv(g):
        c4 = cols(g, 256)
        h = hid[...]
        q[:, c4] = ((mm(h, wqkv[0, :, c4]) + qvb[pl.ds(0, 1), c4]).astype(bf16) * 0.125).astype(bf16)
        k[:, c4] = mm(h, wqkv[1, :, c4]).astype(bf16)
        v[:, c4] = (mm(h, wqkv[2, :, c4]) + qvb[pl.ds(1, 1), c4]).astype(bf16)

    def o_send(pr):
        return rc("o", pr, o_own.at[:, cols(pr)], o_peer.at[:, cols(pr)], to_x)

    def osib_send(pr):
        m = lax.rem(pr, 2)
        return rc("osib", m, o_own.at[:, cols(pr)], o_sib.at[:, cols(m)], to_sib)

    def attend(pr):
        c2 = cols(pr)
        keys = k[:, c2]
        values = [half_of(v[:, c2], e) for e in range(2)]
        for at in range(0, rows, 256):
            r = pl.ds(at, 256)
            same = same_clip(at, 256)
            total = None
            for e in range(2):
                p = softmax(mm_nt(half_of(q[r, c2], e), keys), same)
                term = mm(p.astype(bf16), values[e])
                total = term if total is None else total + term
            o_own[r, c2] = total.astype(bf16)
        o_send(pr).start()

        @pl.when(pr // 2 == 1 - core)
        def _():
            osib_send(pr).start()

    def group_of_heads(g):
        make_qkv(g)
        attend(2 * g)
        attend(2 * g + 1)

    loop(heads_w // 256, group_of_heads)

    w_in.wait_recv()
    w_y.start()
    w_s0.start()
    loads[2].wait()
    nrow = 128

    def own_part(i):
        r = pl.ds(pl.multiple_of(i * nrow, nrow), nrow)
        y1[r, :] = mm(o_own[r, :], wout[t])

    loop(rows // nrow, own_part, True)
    w_y.wait_recv()
    w_s1.start()
    w_s0.wait_recv()
    w_s1.wait_recv()
    w_y.wait_send()
    w_s0.wait_send()
    w_s1.wait_send()
    for pr in range(4):
        o_send(pr).wait_recv()

    def peer_part(i):
        r = pl.ds(pl.multiple_of(i * nrow, nrow), nrow)
        dy1[r, :] = mm(o_peer[r, :], wout[1 - t])

    loop(rows // nrow, peer_part, True)

    def h2t_send(i):
        return rc("h2t", i, h2t.at[0, :, cols(i, nrow)], h2t.at[1, :, cols(i, nrow)], to_sib)

    def norm_two(i):
        r = pl.ds(pl.multiple_of(i * nrow, nrow), nrow)
        x = tok[r, :].astype(f32)
        y = x + (y1[r, :] + dy1[r, :]) + outb[...]
        y1[r, :] = y
        n2, _ = normed(y)
        h2 = (n2 * mgain[...] + mshift[...]).astype(bf16)
        hid_two[r, :] = h2
        h2t[0, :, cols(i, nrow)] = h2.T
        h2t_send(i).start()

    hid_two = xs1
    loop(rows // nrow, norm_two, True)

    loads[3].wait()
    loads[4].wait()
    loads[5].wait()
    c_out.wait_recv()

    def act_send(j):
        c4 = cols(2 * j + 1 - core, 256)
        return rc("act", j, act.at[:, c4], act_sib.at[j], to_sib)

    def pre_send(j):
        c4 = cols(2 * j + 1 - core, 256)
        return rc("pre", j, pre.at[:, c4], pre_sib.at[j], to_sib)

    def hidden(piece):
        c4 = cols(piece, 256)
        a, d = gelu_parts(mm(hid_two[...], wup[:, c4]) + upb[:, c4])
        du = (mm_nt(cpair[0], wdown[c4, :]) * d).astype(bf16)
        act[:, c4] = a.astype(bf16)
        pre[:, c4] = du
        total = split_rows(du.astype(f32))
        row = 6 + piece // 4
        small[pl.ds(row, 1), cols(lax.rem(piece, 4), 256)] = jnp.sum(total, axis=0, keepdims=True)

    def chunk(j):
        hidden(2 * j + 1 - core)
        act_send(j).start()
        pre_send(j).start()
        hidden(2 * j + core)
        mine = cols(2 * j + core, 256)
        act_send(j).wait_recv()
        for n in range(width // 512):
            wide = pl.ds(n * 512, 512)
            block = mm_tn(act[:, mine], cpair[0, :, wide]) + mm_tn(act_sib[j], cpair[1, :, wide])
            low = block.astype(bf16)
            loc_a[2 * j, :, wide] = low[:128]
            loc_a[2 * j + 1, :, wide] = low[128:]
        pre_send(j).wait_recv()
        for m in range(2):
            high = pl.ds(m * 512, 512)
            loc_b[2 * j + m] = (
                mm(h2t[0, high, :], pre[:, mine]) + mm(h2t[1, high, :], pre_sib[j])
            ).astype(bf16)

    def first_wait():
        for i in range(4):
            h2t_send(i).wait_recv()

    first_wait()
    chunk(0)
    sm.step(0)
    chunk(1)
    chunk(2)
    sm.step(1)
    chunk(3)

    def x_send(name, n, src, dst):
        return rc(name, n, src.at[:, cols(n, 256)], dst.at[:, cols(n, 256)], to_x)

    def back_two(n):
        xs0[:, cols(n, 256)] = mm_nt(pre[...], wup[cols(n, 256), :]).astype(bf16)
        x_send("x0", n, xs0, xr0).start()

    loop(width // 256, back_two)
    sm.step(2)

    def forward_two(n):
        xs1[:, cols(n, 256)] = mm(act[...], wdown[:, cols(n, 256)]).astype(bf16)
        x_send("x1", n, xs1, xr1).start()

    loop(width // 256, forward_two)

    for i in range(4):
        h2t_send(i).wait_send()
    h1t = h2t

    def turn_first(i):
        r = pl.ds(pl.multiple_of(i * nrow, nrow), nrow)
        h1t[0, :, cols(i, nrow)] = hid[r, :].T

    loop(rows // nrow, turn_first, True)
    h1t_out = rc("h1t", 0, h1t.at[0], h1t.at[1], to_sib)

    def cot_sum(i, total):
        r = pl.ds(pl.multiple_of(i * tile, tile), tile)
        return total + split_rows(cpair[0, r, :].astype(f32))

    total = lax.fori_loop(0, rows // tile, cot_sum, jnp.zeros((8, width), f32), unroll=True)
    small[pl.ds(8, 1), :] = jnp.sum(total, axis=0, keepdims=True)
    sm.step(3)
    sm.step(4)

    for n in range(4):
        x_send("x0", n, xs0, xr0).wait_recv()
    sums[...] = jnp.zeros_like(sums)
    back = 128
    dyb = xr0

    def norm_two_back(i):
        r = pl.ds(pl.multiple_of(i * back, back), back)
        g = xs0[r, :].astype(f32) + xr0[r, :].astype(f32)
        n2, r2 = normed(y1[r, :])
        gn = g * n2
        sums[0] += split_rows(gn)
        sums[1] += split_rows(g)
        e2 = g * mgain[...]
        m1 = jnp.mean(e2, axis=-1, keepdims=True)
        m2 = jnp.mean(e2 * n2, axis=-1, keepdims=True)
        d = cpair[0, r, :].astype(f32) + r2 * (e2 - m1 - n2 * m2)
        sums[2] += split_rows(d)
        dy1[r, :] = d
        dyb[r, :] = d.astype(bf16)

    loop(rows // back, norm_two_back)
    dyb_out = rc("dyb", 0, dyb, wout.at[1 - t], to_sib)
    dyb_out.start()
    for i, row in enumerate((4, 5, 3)):
        small[pl.ds(row, 1), :] = jnp.sum(sums[i], axis=0, keepdims=True)
    for n in range(4):
        x_send("x0", n, xs0, xr0).wait_send()

    def back_heads(n):
        dob[:, cols(n, 256)] = mm_nt(dyb[...], wout[t, cols(n, 256), :]).astype(bf16)

    loop(heads_w // 256, back_heads)
    sm.step(5)
    osib_send(0).wait_recv()
    osib_send(1).wait_recv()
    dyb_out.wait_recv()
    h1t_out.start()
    for n in range(width // 512):
        wide = pl.ds(n * 512, 512)
        low = (
            mm_tn(o_own[:, cols(core, 256)], dyb[:, wide]) + mm_tn(o_sib[...], wout[1 - t, :, wide])
        ).astype(bf16)
        loc_a[8, :, wide] = low[:128]
        loc_a[9, :, wide] = low[128:]

    def dqkv_send(w, m, src, pr):
        return rc("dqkv", 2 * w + m, src.at[:, cols(pr)], act_sib.at[w, :, cols(m)], to_sib)

    def attend_back(pr):
        c2 = cols(pr)
        same = same_clip(0, rows)
        dq = dk = dv = None
        for e in range(2):
            q_e, do_e = half_of(q[:, c2], e), half_of(dob[:, c2], e)
            p = softmax(mm_nt(q_e, k[:, c2]), same)
            dp = mm_nt(do_e, v[:, c2])
            ds = (p * (dp - jnp.sum(p * dp, axis=1, keepdims=True))).astype(bf16)
            terms = (
                mm(ds, half_of(k[:, c2], e)) * 0.125,
                mm_tn(ds, q_e),
                mm_tn(p.astype(bf16), do_e),
            )
            dq, dk, dv = terms if dq is None else (dq + terms[0], dk + terms[1], dv + terms[2])
        q[:, c2] = dq.astype(bf16)
        k[:, c2] = dk.astype(bf16)
        v[:, c2] = dv.astype(bf16)
        small[pl.ds(2, 1), c2] = jnp.sum(q[:, c2].astype(f32), axis=0, keepdims=True)
        small[pl.ds(2, 1), cols(pr + 4)] = jnp.sum(v[:, c2].astype(f32), axis=0, keepdims=True)

    def theirs(m):
        pr = 2 * (1 - core) + m
        attend_back(pr)
        for w, src in enumerate((q, k, v)):
            dqkv_send(w, m, src, pr).start()

    loop(2, theirs)
    sm.step(6)

    def ours(m):
        attend_back(2 * core + m)

    loop(2, ours)
    sm.step(7)
    h1t_out.wait_recv()
    for w, src in enumerate((q, k, v)):
        for m in range(2):
            dqkv_send(w, m, src, m).wait_recv()
        for m in range(2):
            high = pl.ds(m * 512, 512)
            loc_b[8 + 2 * w + m] = (
                mm(h1t[0, high, :], src[:, cols(core, 256)]) + mm(h1t[1, high, :], act_sib[w])
            ).astype(bf16)
    sm.step(8)

    for n in range(4):
        x_send("x1", n, xs1, xr1).wait_recv()

    def finish(i):
        r = pl.ds(pl.multiple_of(i * tile, tile), tile)
        hid[r, :] = (
            y1[r, :] + (xs1[r, :].astype(f32) + xr1[r, :].astype(f32)) + downb[...]
        ).astype(bf16)

    loop(rows // tile, finish, True)
    lo_out = load(6, hid, lo_h)
    lo_out.start()

    last = wdown.at[pl.ds(0, rows), :]

    def back_one(n):
        c4 = cols(n, 256)
        xs0[:, c4] = (
            mm_nt(q[...], wqkv[0, c4, :]) + mm_nt(k[...], wqkv[1, c4, :]) + mm_nt(v[...], wqkv[2, c4, :])
        ).astype(bf16)
        x_send("x2", n, xs0, last).start()

    loop(width // 256, back_one)
    sm.step(9)
    sm.step(10)
    for n in range(4):
        x_send("x2", n, xs0, last).wait_recv()
    sums[...] = jnp.zeros_like(sums)

    def norm_one_back(i):
        r = pl.ds(pl.multiple_of(i * back, back), back)
        g = xs0[r, :].astype(f32) + wdown[r, :].astype(f32)
        n1, r1 = normed(tok[r, :].astype(f32))
        gn = g * n1
        sums[0] += split_rows(gn)
        sums[1] += split_rows(g)
        e1 = g * again[...]
        m1 = jnp.mean(e1, axis=-1, keepdims=True)
        m2 = jnp.mean(e1 * n1, axis=-1, keepdims=True)
        tok[r, :] = (dy1[r, :] + r1 * (e1 - m1 - n1 * m2)).astype(bf16)

    loop(rows // back, norm_one_back)
    gt_out = load(7, tok, gt_h)
    gt_out.start()
    for i, row in enumerate((0, 1)):
        small[pl.ds(row, 1), :] = jnp.sum(sums[i], axis=0, keepdims=True)

    def small_rc(i, src, to):
        return rc("small", i, src, small_r.at[i], to)

    small_sib = small_rc(0, small, to_sib)
    small_y = small_rc(1, small_r.at[0], to_y)
    small_in = small_rc(2, small_r.at[1], sm.to_z)
    small_mid = small_rc(3, small_r.at[2], sm.to_mid)
    small_out = small_rc(4, small_r.at[3], sm.to_z)
    small_sib.start()
    sm.step(11)
    small_sib.wait_recv()
    small_r[0] += small[...]
    small_y.start()
    sm.step(12)
    small_y.wait_recv()
    small_r[1] += small_r[0]

    @pl.when(sm.outer)
    def _():
        small_in.start()

    sm.step(13)

    @pl.when(sm.mid)
    def _():
        small_in.wait_recv()
        small_r[2] += small_r[1]
        small_mid.start()

    sm.step(14)

    @pl.when(sm.mid)
    def _():
        small_mid.wait_recv()
        small_r[3] += small_r[2]
        small_out.start()

    sm.steps(15, max(sm.na, sm.nb) + STAGES - 1)

    @pl.when(sm.outer)
    def _():
        small_out.wait_recv()

    keep = load(8, small_r.at[jnp.where(sm.outer, 4, 3)], small_h)
    keep.start()

    sm.end()
    w_out.wait_send()
    c_out.wait_send()
    h1t_out.wait_send()
    dyb_out.wait_send()
    for i in range(4):
        o_send(i).wait_send()
        act_send(i).wait_send()
        pre_send(i).wait_send()
        x_send("x1", i, xs1, xr1).wait_send()
        x_send("x2", i, xs0, last).wait_send()
    for m in range(2):
        osib_send(m).wait_send()
        for w, src in enumerate((q, k, v)):
            dqkv_send(w, m, src, m).wait_send()
    small_sib.wait_send()
    small_y.wait_send()

    @pl.when(sm.outer)
    def _():
        small_in.wait_send()

    @pl.when(sm.mid)
    def _():
        small_mid.wait_send()
        small_out.wait_send()

    lo_out.wait()
    gt_out.wait()
    keep.wait()


def layer(clip, vectors, tokens, wqkv, wout, wup, wdown, cot):
    rows, width = tokens.shape
    heads_w = wqkv.shape[2]
    hidden = wup.shape[1]
    big = pl.BlockSpec(memory_space=pl.ANY)
    small = pl.BlockSpec(memory_space=pltpu.VMEM)
    na, nb = 10, 14
    vm = lambda *shape: pltpu.VMEM(shape, bf16)
    vf = lambda *shape: pltpu.VMEM(shape, f32)
    return pl.pallas_call(
        layer_kernel,
        out_shape=(
            jax.ShapeDtypeStruct((rows, width), bf16),
            jax.ShapeDtypeStruct((rows, width), bf16),
            jax.ShapeDtypeStruct((na // 2, 2, 256, width), bf16),
            jax.ShapeDtypeStruct((nb // 2, width, heads_w), bf16),
            jax.ShapeDtypeStruct((16, width), f32),
        ),
        in_specs=[pl.BlockSpec(memory_space=pltpu.SMEM)] + [small] * len(vectors) + [big] * 6,
        out_specs=[big] * 5,
        scratch_shapes=[
            vm(rows, width),
            vm(*wqkv.shape),
            vm(2, *wout.shape),
            vm(*wup.shape),
            vm(*wdown.shape),
            vm(2, rows, width),
            vm(rows, width),
            vm(rows, heads_w),
            vm(rows, heads_w),
            vm(rows, heads_w),
            vm(rows, heads_w),
            vm(rows, heads_w),
            vm(rows, 256),
            vf(rows, width),
            vm(2, width, rows),
            vm(rows, hidden),
            vm(rows, hidden),
            vm(4, rows, 256),
            vm(4, rows, 256),
            vm(rows, width),
            vm(rows, width),
            vm(rows, width),
            vm(rows, width),
            vf(rows, width),
            vm(rows, heads_w),
            vf(16, width),
            vf(5, 16, width),
            vf(3, 8, width),
            vm(na, 128, width),
            vm(nb, 512, 256),
        ]
        + scratch_of(na, 128, width, nb, 512, 256)
        + [
            pltpu.SemaphoreType.DMA((9,)),
            pltpu.SemaphoreType.DMA((N_LINKS,)),
            pltpu.SemaphoreType.DMA((N_LINKS,)),
        ],
        compiler_params=pltpu.CompilerParams(has_side_effects=True, vmem_limit_bytes=VMEM_BYTES),
        name="layer",
    )(clip, *vectors, tokens, wqkv, wout, wup, wdown, cot)


VMEM_BYTES = 60 << 20


def widen_kernel(a_in, b_in, s_in, down, out, up, qkv, ag, ash, qv, ob, mg, ms, ub, db):
    down[...] = a_in[pl.ds(0, 4)].astype(f32)
    out[...] = a_in[4].astype(f32)
    for j in range(4):
        up[:, pl.ds(j * 512, 512)] = b_in[j].astype(f32)
    qkv[...] = b_in[pl.ds(4, 3)].astype(f32)

    @pl.when(pl.program_id(0) == 0)
    def _():
        for ref, row in ((ag, 0), (ash, 1), (ob, 3), (mg, 4), (ms, 5), (db, 8)):
            ref[...] = s_in[pl.ds(row, 1), :]
        qv[pl.ds(0, 1), :] = s_in[pl.ds(2, 1), pl.ds(0, 512)]
        qv[pl.ds(1, 1), :] = s_in[pl.ds(2, 1), pl.ds(512, 512)]
        ub[:, pl.ds(0, 1024)] = s_in[pl.ds(6, 1), :]
        ub[:, pl.ds(1024, 1024)] = s_in[pl.ds(7, 1), :]


def widen(sum_a, sum_b, small):
    steps = 8
    a = sum_a.reshape(5, 512, 1024)
    whole = lambda *shape: pl.BlockSpec(shape, lambda i: (0,) * len(shape))
    got = pl.pallas_call(
        widen_kernel,
        grid=(steps,),
        in_specs=[
            pl.BlockSpec((5, 512 // steps, 1024), lambda i: (0, i, 0)),
            pl.BlockSpec((7, 1024 // steps, 512), lambda i: (0, i, 0)),
            whole(16, 1024),
        ],
        out_specs=[
            pl.BlockSpec((4, 512 // steps, 1024), lambda i: (0, i, 0)),
            pl.BlockSpec((512 // steps, 1024), lambda i: (i, 0)),
            pl.BlockSpec((1024 // steps, 2048), lambda i: (i, 0)),
            pl.BlockSpec((3, 1024 // steps, 512), lambda i: (0, i, 0)),
            whole(1, 1024), whole(1, 1024), whole(2, 512), whole(1, 1024),
            whole(1, 1024), whole(1, 1024), whole(1, 2048), whole(1, 1024),
        ],
        out_shape=[
            jax.ShapeDtypeStruct((4, 512, 1024), f32),
            jax.ShapeDtypeStruct((512, 1024), f32),
            jax.ShapeDtypeStruct((1024, 2048), f32),
            jax.ShapeDtypeStruct((3, 1024, 512), f32),
        ]
        + [
            jax.ShapeDtypeStruct(s, f32)
            for s in ((1, 1024), (1, 1024), (2, 512), (1, 1024), (1, 1024), (1, 1024), (1, 2048), (1, 1024))
        ],
        compiler_params=pltpu.CompilerParams(vmem_limit_bytes=56 << 20),
        name="widen",
    )(a, sum_b, small)
    down, out, up, qkv, ag, ash, qv, ob, mg, ms, ub, db = got
    flat = lambda v: v.reshape(-1)
    return (
        flat(ag), flat(ash), qkv, qv, out, flat(ob), flat(mg), flat(ms), up, flat(ub),
        down.reshape(2048, 1024), flat(db),
    )


def local(
    tokens, clip_lengths, attn_gain, attn_shift, qkv_weight, qv_bias, out_weight, out_bias,
    mlp_gain, mlp_shift, up_weight, up_bias, down_weight, down_bias, cotangent,
):
    row = lambda v: v.reshape(1, -1)
    vectors = (
        row(attn_gain), row(attn_shift), qv_bias, row(out_bias), row(mlp_gain), row(mlp_shift),
        row(up_bias), row(down_bias),
    )
    layer_output, grad_tokens, sum_a, sum_b, small = layer(
        clip_lengths, vectors, tokens, qkv_weight, out_weight, up_weight, down_weight, cotangent
    )
    groups = lax.axis_size("dp")
    if groups > CELL:
        cells = [[k * CELL + i for k in range(groups // CELL)] for i in range(CELL)]
        wide = (sum_a.astype(f32), sum_b.astype(f32), small)
        sum_a, sum_b, small = lax.psum(wide, "dp", axis_index_groups=cells)
    return (layer_output, grad_tokens, *widen(sum_a, sum_b, small))


def solution(mesh):
    placed = (
        P("dp", None), P("dp", None), P(), P(), P(None, None, "tensor"), P(None, "tensor"),
        P("tensor", None), P(), P(), P(), P(None, "tensor"), P("tensor"), P("tensor", None), P(),
        P("dp", None),
    )
    return jax.shard_map(
        local,
        mesh=mesh,
        in_specs=placed,
        out_specs=(
            P("dp", None), P("dp", None), P(), P(), P(None, None, "tensor"), P(None, "tensor"),
            P("tensor", None), P(), P(), P(), P(None, "tensor"), P("tensor"), P("tensor", None), P(),
        ),
        check_vma=False,
    )
```

```python
import jax
import jax.numpy as jnp
from jax import lax
from jax.experimental import pallas as pl
from jax.experimental.pallas import tpu as pltpu
from jax.sharding import PartitionSpec as P

MESH = pl.DeviceIdType.MESH
bf16, f32 = jnp.bfloat16, jnp.float32
CELL = 16
STAGES = 6
SIDE = 256
N_DOWN = N_UP = 16
CHUNKS = 24


def pick(low, first, second):
    if isinstance(low, bool):
        return first if low else second
    return jnp.where(low, first, second)


def place_a(i):
    return pick(i < N_DOWN, i, i + N_UP)


def place_b(i):
    return pick(i < N_UP, i + N_DOWN, i + CHUNKS)


def place():
    at = lax.axis_index("dp")
    base = (at // CELL) * CELL
    inner = at - base
    z = inner // 4
    y = (inner // 2) % 2
    core = inner % 2
    return base, z, y, core


class Summer:
    def __init__(self, loc_a, loc_b, bufs, out, sems):
        self.loc_a, self.loc_b = loc_a, loc_b
        (self.a1, self.a2, self.a3, self.b1, self.b2, self.b3) = bufs
        self.out = out
        self.as_, self.ar_, self.bs_, self.br_, self.ls_ = sems
        self.ha = loc_a.shape[1] // 2
        self.hb = loc_b.shape[1] // 2
        base, z, y, core = place()
        self.y, self.core = y, core
        self.outer = jnp.logical_or(z == 0, z == 3)
        self.mid = jnp.logical_not(self.outer)
        self.mine = jnp.where(z >= 2, 1, 0)
        across = 3 - z
        toward = jnp.where(z < 2, 1 - z, 5 - z)
        tensor = lax.axis_index("tensor")

        def dev(zz, yy, cc):
            return (base + zz * 4 + yy * 2 + cc, tensor)

        self.to_sib = dev(z, y, 1 - core)
        self.to_y = dev(z, 1 - y, core)
        self.to_mid = dev(across, y, core)
        self.to_z = dev(toward, y, core)

    def la(self, i, h):
        return self.loc_a.at[i, pl.ds(pl.multiple_of(h * self.ha, self.ha), self.ha), :]

    def lb(self, i, h):
        return self.loc_b.at[i, pl.ds(pl.multiple_of(h * self.hb, self.hb), self.hb), :]

    def oa(self, i, h, core):
        return self.out.at[
            place_a(i), core, pl.ds(pl.multiple_of(h * self.ha, self.ha), self.ha), :
        ]

    def ob(self, i, h, core):
        return self.out.at[
            place_b(i), core, pl.ds(pl.multiple_of(h * self.hb, self.hb), self.hb), :
        ]

    def ca(self, i, kind, recv, src, dst, to):
        return pltpu.make_async_remote_copy(
            src, dst, self.as_.at[i, kind], self.ar_.at[i, recv], device_id=to, device_id_type=MESH
        )

    def cb(self, i, kind, recv, src, dst, to):
        return pltpu.make_async_remote_copy(
            src, dst, self.bs_.at[i, kind], self.br_.at[i, recv], device_id=to, device_id_type=MESH
        )

    def a_y(self, i):
        return self.ca(i, 0, 0, self.la(i, 1 - self.y), self.a1.at[i], self.to_y)

    def a_in(self, i):
        return self.ca(i, 1, 1, self.la(i, self.y), self.a2.at[i], self.to_z)

    def a_mid(self, i):
        return self.ca(i, 1, 2, self.la(i, self.y), self.a3.at[i], self.to_mid)

    def a_out(self, i):
        return self.ca(i, 2, 3, self.a2.at[i], self.oa(i, self.y, self.core), self.to_z)

    def a_done(self, i, kind, recv, src, to):
        return self.ca(i, kind, recv, src, self.oa(i, self.y, self.core), to)

    def a_keep(self, i):
        return pltpu.make_async_copy(self.a2.at[i], self.oa(i, self.y, self.core), self.ls_.at[0, i])

    def a_fwd(self, i):
        o = self.oa(i, 1 - self.y, self.core)
        return self.ca(i, 5, 6, o, o, self.to_sib)

    def step_a(self, i, stage):
        y = self.y
        if stage == 0:
            self.a_y(i).start()
        elif stage == 1:
            self.a_y(i).wait_recv()
            v = self.la(i, y)
            v[...] = (v[...].astype(f32) + self.a1[i].astype(f32)).astype(bf16)

            @pl.when(self.outer)
            def _():
                self.a_in(i).start()
        elif stage == 2:
            @pl.when(self.mid)
            def _():
                self.a_in(i).wait_recv()
                v = self.la(i, y)
                v[...] = (v[...].astype(f32) + self.a2[i].astype(f32)).astype(bf16)
                self.a_mid(i).start()
        elif stage == 3:
            @pl.when(self.mid)
            def _():
                self.a_mid(i).wait_recv()
                self.a2[i] = (self.la(i, y)[...].astype(f32) + self.a3[i].astype(f32)).astype(bf16)
                self.a_out(i).start()
                src = self.a2.at[i]
                self.a_done(i, 3, 4, src, self.to_y).start()
                self.a_done(i, 4, 5, src, self.to_sib).start()
                self.a_keep(i).start()
        elif stage == 4:
            @pl.when(self.outer)
            def _():
                self.a_out(i).wait_recv()
                src = self.oa(i, y, self.core)
                self.a_done(i, 3, 4, src, self.to_y).start()
                self.a_done(i, 4, 5, src, self.to_sib).start()
        elif stage == 5:
            self.a_done(i, 3, 4, self.oa(i, y, self.core), self.to_y).wait_recv()
            self.a_fwd(i).start()

    def end_a(self, i):
        src = self.a2.at[i]
        self.a_y(i).wait_send()
        self.a_in(i).wait_send()

        @pl.when(self.mid)
        def _():
            self.a_out(i).wait_send()
            self.a_keep(i).wait()

        self.a_done(i, 3, 4, src, self.to_y).wait_send()
        self.a_done(i, 4, 5, src, self.to_sib).wait_send()
        self.a_fwd(i).wait_send()
        self.a_done(i, 4, 5, src, self.to_sib).wait_recv()
        self.a_fwd(i).wait_recv()

    def b_in(self, i):
        return self.cb(i, 0, 0, self.loc_b.at[i], self.b1.at[i], self.to_z)

    def b_mid(self, i):
        return self.cb(i, 0, 1, self.lb(i, 1 - self.mine), self.b2.at[i], self.to_mid)

    def b_y(self, i):
        return self.cb(i, 1, 2, self.lb(i, self.mine), self.b3.at[i], self.to_y)

    def fin_b(self, i):
        return self.b1.at[i, pl.ds(0, self.hb), :]

    def b_done(self, i, kind, recv, src, h, to):
        return self.cb(i, kind, recv, src, self.ob(i, h, self.core), to)

    def b_keep(self, i):
        return pltpu.make_async_copy(
            self.fin_b(i), self.ob(i, self.mine, self.core), self.ls_.at[1, i]
        )

    def step_b(self, i, stage):
        mine, core = self.mine, self.core
        if stage == 0:
            @pl.when(self.outer)
            def _():
                self.b_in(i).start()
        elif stage == 1:
            @pl.when(self.mid)
            def _():
                self.b_in(i).wait_recv()
                self.loc_b[i] = (self.loc_b[i].astype(f32) + self.b1[i].astype(f32)).astype(bf16)
                self.b_mid(i).start()
        elif stage == 2:
            @pl.when(self.mid)
            def _():
                self.b_mid(i).wait_recv()
                v = self.lb(i, mine)
                v[...] = (v[...].astype(f32) + self.b2[i].astype(f32)).astype(bf16)
                self.b_y(i).start()
        elif stage == 3:
            @pl.when(self.mid)
            def _():
                self.b_y(i).wait_recv()
                fin = self.fin_b(i)
                fin[...] = (self.lb(i, mine)[...].astype(f32) + self.b3[i].astype(f32)).astype(bf16)
                self.b_done(i, 2, 4, fin, mine, self.to_mid).start()
                self.b_done(i, 3, 3, fin, mine, self.to_z).start()
                self.b_done(i, 4, 5, fin, mine, self.to_sib).start()
                self.b_keep(i).start()
        elif stage == 4:
            @pl.when(self.mid)
            def _():
                o = self.ob(i, 1 - mine, core)
                self.b_done(i, 2, 4, o, 1 - mine, self.to_mid).wait_recv()
                self.b_done(i, 5, 4, o, 1 - mine, self.to_z).start()
                self.b_done(i, 6, 6, o, 1 - mine, self.to_sib).start()

            @pl.when(self.outer)
            def _():
                o = self.ob(i, mine, core)
                self.b_done(i, 3, 3, o, mine, self.to_z).wait_recv()
                self.b_done(i, 4, 5, o, mine, self.to_sib).start()
        elif stage == 5:
            @pl.when(self.outer)
            def _():
                o = self.ob(i, 1 - mine, core)
                self.b_done(i, 5, 4, o, 1 - mine, self.to_z).wait_recv()
                self.b_done(i, 6, 6, o, 1 - mine, self.to_sib).start()

    def end_b(self, i):
        fin = self.fin_b(i)
        mine = self.mine

        @pl.when(self.outer)
        def _():
            self.b_in(i).wait_send()

        @pl.when(self.mid)
        def _():
            self.b_mid(i).wait_send()
            self.b_y(i).wait_send()
            self.b_done(i, 2, 4, fin, mine, self.to_mid).wait_send()
            self.b_done(i, 3, 3, fin, mine, self.to_z).wait_send()
            self.b_done(i, 5, 4, fin, mine, self.to_z).wait_send()
            self.b_keep(i).wait()

        self.b_done(i, 4, 5, fin, mine, self.to_sib).wait_send()
        self.b_done(i, 6, 6, fin, mine, self.to_sib).wait_send()
        self.b_done(i, 4, 5, fin, mine, self.to_sib).wait_recv()
        self.b_done(i, 6, 6, fin, mine, self.to_sib).wait_recv()

    def step(self, t):
        for stage in (*range(STAGES), STAGES + 1):
            i = t - stage

            def run():
                if stage < STAGES:
                    self.step_a(i, stage)
                    self.step_b(i, stage)
                else:
                    self.end_a(i)
                    self.end_b(i)

            if not isinstance(t, int):
                pl.when(jnp.logical_and(i >= 0, i < CHUNKS))(run)
            elif 0 <= i < CHUNKS:
                run()

    def steps(self, lo, hi):
        def body(t, _):
            self.step(t)
            return 0

        lax.fori_loop(lo, hi, body, 0)

    def end(self):
        def body(i, _):
            self.end_a(i)
            self.end_b(i)
            return 0

        lax.fori_loop(CHUNKS - 2, CHUNKS, body, 0)


def scratch_of(n, side):
    whole, half = pltpu.VMEM((n, side, side), bf16), pltpu.VMEM((n, side // 2, side), bf16)
    return [
        whole,
        whole,
        half,
        half,
        half,
        whole,
        half,
        half,
        pltpu.SemaphoreType.DMA((n, 6)),
        pltpu.SemaphoreType.DMA((n, 7)),
        pltpu.SemaphoreType.DMA((n, 7)),
        pltpu.SemaphoreType.DMA((n, 7)),
        pltpu.SemaphoreType.DMA((2, n)),
    ]


def split_rows(value):
    rows, cols = value.shape
    return jnp.sum(value.reshape(rows // 8, 8, cols), axis=0)


def erf(value):
    x = jnp.clip(value, -4.0, 4.0)
    x2 = x * x
    top = -2.72614225801306e-10
    for c in (
        2.77068142495902e-08,
        -2.10102402082508e-06,
        -5.69250639462346e-05,
        -7.34990630326855e-04,
        -2.95459980854025e-03,
        -1.60960333262415e-02,
    ):
        top = top * x2 + c
    low = -1.45660718464996e-05
    for c in (
        -2.13374055278905e-04,
        -1.68282697438203e-03,
        -7.37332916720468e-03,
        -1.42647390514189e-02,
    ):
        low = low * x2 + c
    return x * top / low


def gelu_parts(u):
    cdf = 0.5 * (1.0 + erf(u * 0.7071067811865476))
    pdf = jnp.exp(-0.5 * u * u) * 0.3989422804014327
    return u * cdf, cdf + u * pdf


def normed(rows_in):
    centred = rows_in - jnp.mean(rows_in, axis=-1, keepdims=True)
    scale = lax.rsqrt(jnp.mean(centred * centred, axis=-1, keepdims=True) + 1e-06)
    return centred * scale, scale


def mm(left, right):
    return jnp.dot(left, right, preferred_element_type=f32)


def mm_tn(left, right):
    return lax.dot_general(left, right, (((0,), (0,)), ((), ())), preferred_element_type=f32)


def mm_nt(left, right):
    return lax.dot_general(left, right, (((1,), (1,)), ((), ())), preferred_element_type=f32)


LINKS = {
    "w": 4, "c": 1, "o": 4, "osib": 2, "h2t": 4, "act": 4, "pre": 4, "x0": 4, "x1": 4, "x2": 4,
    "dyb": 1, "h1t": 1, "dqkv": 6, "small": 5,
}
LINK_AT = {}
for _name, _count in LINKS.items():
    LINK_AT[_name] = sum(LINKS[n] for n in LINK_AT)
N_LINKS = sum(LINKS.values())


def layer_kernel(
    clip, again, ashift, qvb, outb, mgain, mshift, upb, downb,
    tok_h, wqkv_h, wout_h, wup_h, wdown_h, cot_h,
    lo_h, gt_h, out, small_h,
    tok, wqkv, wout, wup, wdown, cpair, hid, q, k, v, o_own, o_peer, o_sib, y1, h2t,
    act, pre, act_sib, pre_sib, xs0, xs1, xr0, xr1, dy1, dob, small, small_r, sums,
    loc_a, loc_b, a1, a2, a3, b1, b2, b3,
    as_, ar_, bs_, br_, ls_, lsem, ssem, rsem,
):
    rows = tok.shape[0]
    width = tok.shape[1]
    sm = Summer(loc_a, loc_b, (a1, a2, a3, b1, b2, b3), out, (as_, ar_, bs_, br_, ls_))
    base, z, y, core = place()
    t = lax.axis_index("tensor")
    to_x = (lax.axis_index("dp"), 1 - t)
    to_sib, to_y = sm.to_sib, sm.to_y

    def rc(name, i, src, dst, to):
        at = LINK_AT[name] + i
        return pltpu.make_async_remote_copy(
            src, dst, ssem.at[at], rsem.at[at], device_id=to, device_id_type=MESH
        )

    def cols(i, n=128):
        return pl.ds(pl.multiple_of(i * n, n), n)

    def loop(n, body, unroll=False):
        def wrapped(i, _):
            body(i)
            return 0

        lax.fori_loop(0, n, wrapped, 0, unroll=unroll)

    def load(i, src, dst):
        return pltpu.make_async_copy(src, dst, lsem.at[i])

    loads = [
        load(0, tok_h, tok),
        load(1, wqkv_h, wqkv),
        load(2, wout_h, wout.at[t]),
        load(3, wup_h, wup),
        load(4, cot_h, cpair.at[0]),
        load(5, wdown_h, wdown),
    ]
    quarter = 2 * y + core
    part = wout_h.shape[0] // 4

    def rows_of(i):
        return pl.ds(pl.multiple_of(i * part, part), part)

    def w_at(i):
        return wout.at[1 - t, rows_of(i), :]

    w_out = rc("w", 0, wout_h.at[rows_of(quarter), :], wout.at[t, rows_of(quarter), :], to_x)
    w_in = rc("w", 0, wout_h.at[rows_of(quarter), :], w_at(quarter), to_x)
    w_y = rc("w", 1, w_at(quarter), w_at(quarter), to_y)
    w_s0 = rc("w", 2, w_at(quarter), w_at(quarter), to_sib)
    other = 2 * (1 - y) + core
    w_s1 = rc("w", 3, w_at(other), w_at(other), to_sib)
    c_out = rc("c", 0, cot_h, cpair.at[1], to_sib)
    for item in loads:
        item.start()

    barrier = pltpu.get_barrier_semaphore()

    def greet(to):
        pl.semaphore_signal(barrier, inc=1, device_id=to, device_id_type=MESH)

    for to in (to_sib, to_x, to_y, sm.to_z):
        greet(to)

    @pl.when(sm.mid)
    def _():
        greet(sm.to_mid)

    loads[0].wait()
    tile = 64

    def norm_one(i):
        r = pl.ds(pl.multiple_of(i * tile, tile), tile)
        n1, _ = normed(tok[r, :].astype(f32))
        hid[r, :] = (n1 * again[...] + ashift[...]).astype(bf16)

    loop(rows // tile, norm_one, True)

    @pl.when(sm.mid)
    def _():
        pl.semaphore_wait(barrier, 5)

    @pl.when(sm.outer)
    def _():
        pl.semaphore_wait(barrier, 4)

    w_out.start()
    c_out.start()
    loads[1].wait()
    heads_w = q.shape[1]
    lane = lax.broadcasted_iota(jnp.int32, (1, 128), 1)

    def half_of(value, e):
        keep = (lane < 64) if e == 0 else (lane >= 64)
        return jnp.where(keep, value.astype(f32), 0.0).astype(bf16)

    end0 = clip[0, 0]
    end1 = end0 + clip[0, 1]
    end2 = end1 + clip[0, 2]

    def seg_of(index):
        one = lambda e: (index >= e).astype(jnp.int32)
        return one(end0) + one(end1) + one(end2)

    key_seg = seg_of(lax.broadcasted_iota(jnp.int32, (1, rows), 1))
    def same_clip(at, count):
        return seg_of(lax.broadcasted_iota(jnp.int32, (count, 1), 0) + at) == key_seg

    def softmax(products, same):
        s = jnp.where(same, products, -1e30)
        w = jnp.exp(s - jnp.max(s, axis=1, keepdims=True))
        return w * (1.0 / jnp.sum(w, axis=1, keepdims=True))

    def make_qkv(g):
        c4 = cols(g, 256)
        h = hid[...]
        q[:, c4] = ((mm(h, wqkv[0, :, c4]) + qvb[pl.ds(0, 1), c4]).astype(bf16) * 0.125).astype(bf16)
        k[:, c4] = mm(h, wqkv[1, :, c4]).astype(bf16)
        v[:, c4] = (mm(h, wqkv[2, :, c4]) + qvb[pl.ds(1, 1), c4]).astype(bf16)

    def o_send(pr):
        return rc("o", pr, o_own.at[:, cols(pr)], o_peer.at[:, cols(pr)], to_x)

    def osib_send(pr):
        m = lax.rem(pr, 2)
        return rc("osib", m, o_own.at[:, cols(pr)], o_sib.at[:, cols(m)], to_sib)

    def attend(pr):
        c2 = cols(pr)
        keys = k[:, c2]
        values = [half_of(v[:, c2], e) for e in range(2)]
        for at in range(0, rows, 256):
            r = pl.ds(at, 256)
            same = same_clip(at, 256)
            total = None
            for e in range(2):
                p = softmax(mm_nt(half_of(q[r, c2], e), keys), same)
                term = mm(p.astype(bf16), values[e])
                total = term if total is None else total + term
            o_own[r, c2] = total.astype(bf16)
        o_send(pr).start()

        @pl.when(pr // 2 == 1 - core)
        def _():
            osib_send(pr).start()

    def group_of_heads(g):
        make_qkv(g)
        attend(2 * g)
        attend(2 * g + 1)

    loop(heads_w // 256, group_of_heads)

    w_in.wait_recv()
    w_y.start()
    w_s0.start()
    loads[2].wait()
    nrow = 128

    def own_part(i):
        r = pl.ds(pl.multiple_of(i * nrow, nrow), nrow)
        y1[r, :] = mm(o_own[r, :], wout[t])

    loop(rows // nrow, own_part, True)
    w_y.wait_recv()
    w_s1.start()
    w_s0.wait_recv()
    w_s1.wait_recv()
    w_y.wait_send()
    w_s0.wait_send()
    w_s1.wait_send()
    for pr in range(4):
        o_send(pr).wait_recv()

    def peer_part(i):
        r = pl.ds(pl.multiple_of(i * nrow, nrow), nrow)
        dy1[r, :] = mm(o_peer[r, :], wout[1 - t])

    loop(rows // nrow, peer_part, True)

    def h2t_send(i):
        return rc("h2t", i, h2t.at[0, :, cols(i, nrow)], h2t.at[1, :, cols(i, nrow)], to_sib)

    def norm_two(i):
        r = pl.ds(pl.multiple_of(i * nrow, nrow), nrow)
        x = tok[r, :].astype(f32)
        y = x + (y1[r, :] + dy1[r, :]) + outb[...]
        y1[r, :] = y
        n2, _ = normed(y)
        h2 = (n2 * mgain[...] + mshift[...]).astype(bf16)
        hid_two[r, :] = h2
        h2t[0, :, cols(i, nrow)] = h2.T
        h2t_send(i).start()

    hid_two = xs1
    loop(rows // nrow, norm_two, True)

    loads[3].wait()
    loads[4].wait()
    loads[5].wait()
    c_out.wait_recv()

    def act_send(j):
        c4 = cols(2 * j + 1 - core, 256)
        return rc("act", j, act.at[:, c4], act_sib.at[j], to_sib)

    def pre_send(j):
        c4 = cols(2 * j + 1 - core, 256)
        return rc("pre", j, pre.at[:, c4], pre_sib.at[j], to_sib)

    def hidden(piece):
        c4 = cols(piece, 256)
        a, d = gelu_parts(mm(hid_two[...], wup[:, c4]) + upb[:, c4])
        du = (mm_nt(cpair[0], wdown[c4, :]) * d).astype(bf16)
        act[:, c4] = a.astype(bf16)
        pre[:, c4] = du
        total = split_rows(du.astype(f32))
        row = 6 + piece // 4
        small[pl.ds(row, 1), cols(lax.rem(piece, 4), 256)] = jnp.sum(total, axis=0, keepdims=True)

    def chunk(j, middle=None):
        hidden(2 * j + 1 - core)
        act_send(j).start()
        pre_send(j).start()
        hidden(2 * j + core)
        if middle is not None:
            sm.step(middle)
        mine = cols(2 * j + core, 256)
        act_send(j).wait_recv()
        for n in range(2):
            wide = pl.ds(n * 512, 512)
            block = mm_tn(act[:, mine], cpair[0, :, wide]) + mm_tn(act_sib[j], cpair[1, :, wide])
            low = block.astype(bf16)
            loc_a[4 * j + 2 * n] = low[:, :256]
            loc_a[4 * j + 2 * n + 1] = low[:, 256:]
        pre_send(j).wait_recv()
        for m in range(2):
            high = pl.ds(m * 512, 512)
            low = (mm(h2t[0, high, :], pre[:, mine]) + mm(h2t[1, high, :], pre_sib[j])).astype(bf16)
            loc_b[4 * j + 2 * m] = low[:256]
            loc_b[4 * j + 2 * m + 1] = low[256:]

    for i in range(4):
        h2t_send(i).wait_recv()
    chunk(0)
    sm.step(0)
    chunk(1, 1)
    sm.step(2)
    chunk(2, 3)
    chunk(3, 4)
    sm.step(5)

    def x_send(name, n, src, dst):
        return rc(name, n, src.at[:, cols(n, 256)], dst.at[:, cols(n, 256)], to_x)

    def back_two(n):
        xs0[:, cols(n, 256)] = mm_nt(pre[...], wup[cols(n, 256), :]).astype(bf16)
        x_send("x0", n, xs0, xr0).start()

    loop(width // 256, back_two)
    sm.step(6)

    def forward_two(n):
        xs1[:, cols(n, 256)] = mm(act[...], wdown[:, cols(n, 256)]).astype(bf16)
        x_send("x1", n, xs1, xr1).start()

    loop(width // 256, forward_two)
    sm.step(7)

    for i in range(4):
        h2t_send(i).wait_send()
    h1t = h2t

    def turn_first(i):
        r = pl.ds(pl.multiple_of(i * nrow, nrow), nrow)
        h1t[0, :, cols(i, nrow)] = hid[r, :].T

    loop(rows // nrow, turn_first, True)
    h1t_out = rc("h1t", 0, h1t.at[0], h1t.at[1], to_sib)

    def cot_sum(i, total):
        r = pl.ds(pl.multiple_of(i * tile, tile), tile)
        return total + split_rows(cpair[0, r, :].astype(f32))

    total = lax.fori_loop(0, rows // tile, cot_sum, jnp.zeros((8, width), f32), unroll=True)
    small[pl.ds(8, 1), :] = jnp.sum(total, axis=0, keepdims=True)
    sm.steps(8, 13)

    for n in range(4):
        x_send("x0", n, xs0, xr0).wait_recv()
    sums[...] = jnp.zeros_like(sums)
    back = 128
    dyb = xr0

    def norm_two_back(i):
        r = pl.ds(pl.multiple_of(i * back, back), back)
        g = xs0[r, :].astype(f32) + xr0[r, :].astype(f32)
        n2, r2 = normed(y1[r, :])
        gn = g * n2
        sums[0] += split_rows(gn)
        sums[1] += split_rows(g)
        e2 = g * mgain[...]
        m1 = jnp.mean(e2, axis=-1, keepdims=True)
        m2 = jnp.mean(e2 * n2, axis=-1, keepdims=True)
        d = cpair[0, r, :].astype(f32) + r2 * (e2 - m1 - n2 * m2)
        sums[2] += split_rows(d)
        dy1[r, :] = d
        dyb[r, :] = d.astype(bf16)

    loop(rows // back, norm_two_back)
    dyb_out = rc("dyb", 0, dyb, wout.at[1 - t], to_sib)
    dyb_out.start()
    for i, row in enumerate((4, 5, 3)):
        small[pl.ds(row, 1), :] = jnp.sum(sums[i], axis=0, keepdims=True)
    for n in range(4):
        x_send("x0", n, xs0, xr0).wait_send()

    def back_heads(n):
        dob[:, cols(n, 256)] = mm_nt(dyb[...], wout[t, cols(n, 256), :]).astype(bf16)

    loop(heads_w // 256, back_heads)
    sm.step(13)
    osib_send(0).wait_recv()
    osib_send(1).wait_recv()
    dyb_out.wait_recv()
    h1t_out.start()
    for n in range(width // 512):
        wide = pl.ds(n * 512, 512)
        low = (
            mm_tn(o_own[:, cols(core, 256)], dyb[:, wide]) + mm_tn(o_sib[...], wout[1 - t, :, wide])
        ).astype(bf16)
        loc_a[16 + 2 * n] = low[:, :256]
        loc_a[17 + 2 * n] = low[:, 256:]

    sm.step(14)

    def dqkv_send(w, m, src, pr):
        return rc("dqkv", 2 * w + m, src.at[:, cols(pr)], act_sib.at[w, :, cols(m)], to_sib)

    def attend_back(pr):
        c2 = cols(pr)
        same = same_clip(0, rows)
        dq = dk = dv = None
        for e in range(2):
            q_e, do_e = half_of(q[:, c2], e), half_of(dob[:, c2], e)
            p = softmax(mm_nt(q_e, k[:, c2]), same)
            dp = mm_nt(do_e, v[:, c2])
            ds = (p * (dp - jnp.sum(p * dp, axis=1, keepdims=True))).astype(bf16)
            terms = (
                mm(ds, half_of(k[:, c2], e)) * 0.125,
                mm_tn(ds, q_e),
                mm_tn(p.astype(bf16), do_e),
            )
            dq, dk, dv = terms if dq is None else (dq + terms[0], dk + terms[1], dv + terms[2])
        q[:, c2] = dq.astype(bf16)
        k[:, c2] = dk.astype(bf16)
        v[:, c2] = dv.astype(bf16)
        small[pl.ds(2, 1), c2] = jnp.sum(q[:, c2].astype(f32), axis=0, keepdims=True)
        small[pl.ds(2, 1), cols(pr + 4)] = jnp.sum(v[:, c2].astype(f32), axis=0, keepdims=True)

    def theirs(m):
        pr = 2 * (1 - core) + m
        attend_back(pr)
        for w, src in enumerate((q, k, v)):
            dqkv_send(w, m, src, pr).start()

    loop(2, theirs)
    sm.step(15)

    def ours(m):
        attend_back(2 * core + m)

    loop(2, ours)
    h1t_out.wait_recv()
    for w, src in enumerate((q, k, v)):
        for m in range(2):
            dqkv_send(w, m, src, m).wait_recv()
        for m in range(4):
            high = pl.ds(m * 256, 256)
            low = mm(h1t[0, high, :], src[:, cols(core, 256)]) + mm(h1t[1, high, :], act_sib[w])
            at = 3 * m + w
            if at < 4:
                loc_a[20 + at] = low.astype(bf16)
            else:
                loc_b[12 + at] = low.astype(bf16)
    sm.step(16)

    last = wup.at[pl.ds(0, rows), pl.ds(0, width)]

    def back_one(n):
        c4 = cols(n, 256)
        xs0[:, c4] = (
            mm_nt(q[...], wqkv[0, c4, :]) + mm_nt(k[...], wqkv[1, c4, :]) + mm_nt(v[...], wqkv[2, c4, :])
        ).astype(bf16)
        x_send("x2", n, xs0, last).start()

    loop(width // 256, back_one)
    sm.steps(17, 20)

    for n in range(4):
        x_send("x1", n, xs1, xr1).wait_recv()

    def finish(i):
        r = pl.ds(pl.multiple_of(i * tile, tile), tile)
        hid[r, :] = (
            y1[r, :] + (xs1[r, :].astype(f32) + xr1[r, :].astype(f32)) + downb[...]
        ).astype(bf16)

    loop(rows // tile, finish, True)
    lo_out = load(6, hid, lo_h)
    lo_out.start()

    sm.steps(20, 23)
    for n in range(4):
        x_send("x2", n, xs0, last).wait_recv()
    sums[...] = jnp.zeros_like(sums)

    def norm_one_back(i):
        r = pl.ds(pl.multiple_of(i * back, back), back)
        g = xs0[r, :].astype(f32) + last[r, :].astype(f32)
        n1, r1 = normed(tok[r, :].astype(f32))
        gn = g * n1
        sums[0] += split_rows(gn)
        sums[1] += split_rows(g)
        e1 = g * again[...]
        m1 = jnp.mean(e1, axis=-1, keepdims=True)
        m2 = jnp.mean(e1 * n1, axis=-1, keepdims=True)
        tok[r, :] = (dy1[r, :] + r1 * (e1 - m1 - n1 * m2)).astype(bf16)

    loop(rows // back, norm_one_back)
    gt_out = load(7, tok, gt_h)
    gt_out.start()
    for i, row in enumerate((0, 1)):
        small[pl.ds(row, 1), :] = jnp.sum(sums[i], axis=0, keepdims=True)

    def small_rc(i, src, to):
        return rc("small", i, src, small_r.at[i], to)

    small_sib = small_rc(0, small, to_sib)
    small_y = small_rc(1, small_r.at[0], to_y)
    small_in = small_rc(2, small_r.at[1], sm.to_z)
    small_mid = small_rc(3, small_r.at[2], sm.to_mid)
    small_out = small_rc(4, small_r.at[3], sm.to_z)
    small_sib.start()
    sm.step(23)
    small_sib.wait_recv()
    small_r[0] += small[...]
    small_y.start()
    sm.step(24)
    small_y.wait_recv()
    small_r[1] += small_r[0]

    @pl.when(sm.outer)
    def _():
        small_in.start()

    sm.step(25)

    @pl.when(sm.mid)
    def _():
        small_in.wait_recv()
        small_r[2] += small_r[1]
        small_mid.start()

    sm.step(26)

    @pl.when(sm.mid)
    def _():
        small_mid.wait_recv()
        small_r[3] += small_r[2]
        small_out.start()

    sm.steps(27, CHUNKS + STAGES - 1)

    @pl.when(sm.outer)
    def _():
        small_out.wait_recv()

    keep = load(8, small_r.at[jnp.where(sm.outer, 4, 3)], small_h)
    keep.start()

    sm.end()
    w_out.wait_send()
    c_out.wait_send()
    h1t_out.wait_send()
    dyb_out.wait_send()
    for i in range(4):
        o_send(i).wait_send()
        act_send(i).wait_send()
        pre_send(i).wait_send()
        x_send("x1", i, xs1, xr1).wait_send()
        x_send("x2", i, xs0, last).wait_send()
    for m in range(2):
        osib_send(m).wait_send()
        for w, src in enumerate((q, k, v)):
            dqkv_send(w, m, src, m).wait_send()
    small_sib.wait_send()
    small_y.wait_send()

    @pl.when(sm.outer)
    def _():
        small_in.wait_send()

    @pl.when(sm.mid)
    def _():
        small_mid.wait_send()
        small_out.wait_send()

    lo_out.wait()
    gt_out.wait()
    keep.wait()


def layer(clip, vectors, tokens, wqkv, wout, wup, wdown, cot):
    rows, width = tokens.shape
    heads_w = wqkv.shape[2]
    hidden = wup.shape[1]
    big = pl.BlockSpec(memory_space=pl.ANY)
    small = pl.BlockSpec(memory_space=pltpu.VMEM)
    vm = lambda *shape: pltpu.VMEM(shape, bf16)
    vf = lambda *shape: pltpu.VMEM(shape, f32)
    return pl.pallas_call(
        layer_kernel,
        out_shape=(
            jax.ShapeDtypeStruct((rows, width), bf16),
            jax.ShapeDtypeStruct((rows, width), bf16),
            jax.ShapeDtypeStruct((2 * CHUNKS, 2, SIDE, SIDE), bf16),
            jax.ShapeDtypeStruct((16, width), f32),
        ),
        in_specs=[pl.BlockSpec(memory_space=pltpu.SMEM)] + [small] * len(vectors) + [big] * 6,
        out_specs=[big] * 4,
        scratch_shapes=[
            vm(rows, width),
            vm(*wqkv.shape),
            vm(2, *wout.shape),
            vm(*wup.shape),
            vm(*wdown.shape),
            vm(2, rows, width),
            vm(rows, width),
            vm(rows, heads_w),
            vm(rows, heads_w),
            vm(rows, heads_w),
            vm(rows, heads_w),
            vm(rows, heads_w),
            vm(rows, 256),
            vf(rows, width),
            vm(2, width, rows),
            vm(rows, hidden),
            vm(rows, hidden),
            vm(4, rows, 256),
            vm(4, rows, 256),
            vm(rows, width),
            vm(rows, width),
            vm(rows, width),
            vm(rows, width),
            vf(rows, width),
            vm(rows, heads_w),
            vf(16, width),
            vf(5, 16, width),
            vf(3, 8, width),
        ]
        + scratch_of(CHUNKS, SIDE)
        + [
            pltpu.SemaphoreType.DMA((9,)),
            pltpu.SemaphoreType.DMA((N_LINKS,)),
            pltpu.SemaphoreType.DMA((N_LINKS,)),
        ],
        compiler_params=pltpu.CompilerParams(
            has_side_effects=True, collective_id=0, vmem_limit_bytes=VMEM_BYTES
        ),
        name="layer",
    )(clip, *vectors, tokens, wqkv, wout, wup, wdown, cot)


VMEM_BYTES = 60 << 20


STEPS = 8


def widen_kernel(
    down_in, up_in, out_in, qkv_in, s_in, lo_in, gt_in,
    lo, gt, down, out, up, qkv, ag, ash, qv, ob, mg, ms, ub, db,
):
    lo[...] = lo_in[...]
    gt[...] = gt_in[...]
    for n in range(4):
        c = pl.ds(n * SIDE, SIDE)
        down[:, c] = down_in[n, 0].astype(f32)
        out[:, c] = out_in[n, 0].astype(f32)
        up[c, :] = up_in[n, 0].astype(f32)
    for w in range(3):
        for core in range(2):
            qkv[w, :, pl.ds(core * SIDE, SIDE)] = qkv_in[w, core].astype(f32)

    @pl.when(pl.program_id(0) == STEPS - 1)
    def _():
        for ref, row in ((ag, 0), (ash, 1), (ob, 3), (mg, 4), (ms, 5), (db, 8)):
            ref[...] = s_in[pl.ds(row, 1), :]
        qv[pl.ds(0, 1), :] = s_in[pl.ds(2, 1), pl.ds(0, 512)]
        qv[pl.ds(1, 1), :] = s_in[pl.ds(2, 1), pl.ds(512, 512)]
        ub[:, pl.ds(0, 1024)] = s_in[pl.ds(6, 1), :]
        ub[:, pl.ds(1024, 1024)] = s_in[pl.ds(7, 1), :]


def widen(sums, small, lo, gt):
    whole = lambda *shape: pl.BlockSpec(shape, lambda i: (0,) * len(shape))
    rows_in = pl.BlockSpec((lo.shape[0] // STEPS, lo.shape[1]), lambda i: (i, 0))
    vectors = ((1, 1024), (1, 1024), (2, 512), (1, 1024), (1, 1024), (1, 1024), (1, 2048), (1, 1024))
    got = pl.pallas_call(
        widen_kernel,
        grid=(STEPS,),
        in_specs=[
            pl.BlockSpec((4, 1, SIDE, SIDE), lambda i: (i // 2, i % 2, 0, 0)),
            pl.BlockSpec((4, 1, SIDE, SIDE), lambda i: (4 + i // 2, i % 2, 0, 0)),
            pl.BlockSpec((4, 1, SIDE // 4, SIDE), lambda i: (8, i // 4, i % 4, 0)),
            pl.BlockSpec((3, 2, SIDE // 2, SIDE), lambda i: (12 + i // 2, 0, i % 2, 0)),
            whole(16, 1024),
            rows_in,
            rows_in,
        ],
        out_specs=[
            rows_in,
            rows_in,
            pl.BlockSpec((SIDE, 1024), lambda i: (i, 0)),
            pl.BlockSpec((SIDE // 4, 1024), lambda i: (i, 0)),
            pl.BlockSpec((1024, SIDE), lambda i: (0, i)),
            pl.BlockSpec((3, SIDE // 2, 512), lambda i: (0, i, 0)),
        ]
        + [whole(*shape) for shape in vectors],
        out_shape=[
            jax.ShapeDtypeStruct(lo.shape, bf16),
            jax.ShapeDtypeStruct(gt.shape, bf16),
            jax.ShapeDtypeStruct((2048, 1024), f32),
            jax.ShapeDtypeStruct((512, 1024), f32),
            jax.ShapeDtypeStruct((1024, 2048), f32),
            jax.ShapeDtypeStruct((3, 1024, 512), f32),
        ]
        + [jax.ShapeDtypeStruct(shape, f32) for shape in vectors],
        compiler_params=pltpu.CompilerParams(vmem_limit_bytes=56 << 20),
        name="widen",
    )(sums, sums, sums, sums, small, lo, gt)
    lo, gt, down, out, up, qkv, ag, ash, qv, ob, mg, ms, ub, db = got
    flat = lambda v: v.reshape(-1)
    return (
        lo, gt, flat(ag), flat(ash), qkv, qv, out, flat(ob), flat(mg), flat(ms), up, flat(ub),
        down, flat(db),
    )


def local(
    tokens, clip_lengths, attn_gain, attn_shift, qkv_weight, qv_bias, out_weight, out_bias,
    mlp_gain, mlp_shift, up_weight, up_bias, down_weight, down_bias, cotangent,
):
    row = lambda v: v.reshape(1, -1)
    vectors = (
        row(attn_gain), row(attn_shift), qv_bias, row(out_bias), row(mlp_gain), row(mlp_shift),
        row(up_bias), row(down_bias),
    )
    layer_output, grad_tokens, sums, small = layer(
        clip_lengths, vectors, tokens, qkv_weight, out_weight, up_weight, down_weight, cotangent
    )
    groups = lax.axis_size("dp")
    if groups > CELL:
        cells = [[k * CELL + i for k in range(groups // CELL)] for i in range(CELL)]
        sums, small = lax.psum((sums.astype(f32), small), "dp", axis_index_groups=cells)
    return widen(sums, small, layer_output, grad_tokens)


def solution(mesh):
    placed = (
        P("dp", None), P("dp", None), P(), P(), P(None, None, "tensor"), P(None, "tensor"),
        P("tensor", None), P(), P(), P(), P(None, "tensor"), P("tensor"), P("tensor", None), P(),
        P("dp", None),
    )
    return jax.shard_map(
        local,
        mesh=mesh,
        in_specs=placed,
        out_specs=(
            P("dp", None), P("dp", None), P(), P(), P(None, None, "tensor"), P(None, "tensor"),
            P("tensor", None), P(), P(), P(), P(None, "tensor"), P("tensor"), P("tensor", None), P(),
        ),
        check_vma=False,
    )
```

```python
import jax
import jax.numpy as jnp
from jax import lax
from jax.experimental import pallas as pl
from jax.experimental.pallas import tpu as pltpu
from jax.sharding import PartitionSpec as P

MESH = pl.DeviceIdType.MESH
bf16, f32 = jnp.bfloat16, jnp.float32
CELL = 16
LAGS = (0, 2, 4, 6, 8, 10)
LAST = LAGS[-1] + 2
STAGES = len(LAGS)
SIDE = 256
N_DOWN = N_UP = 16
CHUNKS = 24
END = CHUNKS + LAGS[-1]


def pick(low, first, second):
    if isinstance(low, bool):
        return first if low else second
    return jnp.where(low, first, second)


def place_a(i):
    return pick(i < N_DOWN, i, i + N_UP)


def place_b(i):
    return pick(i < N_UP, i + N_DOWN, i + CHUNKS)


def place():
    at = lax.axis_index("dp")
    base = (at // CELL) * CELL
    inner = at - base
    z = inner // 4
    y = (inner // 2) % 2
    core = inner % 2
    return base, z, y, core


class Summer:
    def __init__(self, loc_a, loc_b, bufs, out, sems):
        self.loc_a, self.loc_b = loc_a, loc_b
        (self.a1, self.a2, self.a3, self.b1, self.b2, self.b3) = bufs
        self.out = out
        self.as_, self.ar_, self.bs_, self.br_, self.ls_ = sems
        self.ha = loc_a.shape[1] // 2
        self.hb = loc_b.shape[1] // 2
        base, z, y, core = place()
        self.y, self.core = y, core
        self.outer = jnp.logical_or(z == 0, z == 3)
        self.mid = jnp.logical_not(self.outer)
        self.mine = jnp.where(z >= 2, 1, 0)
        across = 3 - z
        toward = jnp.where(z < 2, 1 - z, 5 - z)
        tensor = lax.axis_index("tensor")

        def dev(zz, yy, cc):
            return (base + zz * 4 + yy * 2 + cc, tensor)

        self.to_sib = dev(z, y, 1 - core)
        self.to_y = dev(z, 1 - y, core)
        self.to_mid = dev(across, y, core)
        self.to_z = dev(toward, y, core)

    def la(self, i, h):
        return self.loc_a.at[i, pl.ds(pl.multiple_of(h * self.ha, self.ha), self.ha), :]

    def lb(self, i, h):
        return self.loc_b.at[i, pl.ds(pl.multiple_of(h * self.hb, self.hb), self.hb), :]

    def oa(self, i, h, core):
        return self.out.at[
            place_a(i), core, pl.ds(pl.multiple_of(h * self.ha, self.ha), self.ha), :
        ]

    def ob(self, i, h, core):
        return self.out.at[
            place_b(i), core, pl.ds(pl.multiple_of(h * self.hb, self.hb), self.hb), :
        ]

    def ca(self, i, kind, recv, src, dst, to):
        return pltpu.make_async_remote_copy(
            src, dst, self.as_.at[i, kind], self.ar_.at[i, recv], device_id=to, device_id_type=MESH
        )

    def cb(self, i, kind, recv, src, dst, to):
        return pltpu.make_async_remote_copy(
            src, dst, self.bs_.at[i, kind], self.br_.at[i, recv], device_id=to, device_id_type=MESH
        )

    def a_y(self, i):
        return self.ca(i, 0, 0, self.la(i, 1 - self.y), self.a1.at[i], self.to_y)

    def a_in(self, i):
        return self.ca(i, 1, 1, self.la(i, self.y), self.a2.at[i], self.to_z)

    def a_mid(self, i):
        return self.ca(i, 1, 2, self.la(i, self.y), self.a3.at[i], self.to_mid)

    def a_out(self, i):
        return self.ca(i, 2, 3, self.a2.at[i], self.oa(i, self.y, self.core), self.to_z)

    def a_done(self, i, kind, recv, src, to):
        return self.ca(i, kind, recv, src, self.oa(i, self.y, self.core), to)

    def a_keep(self, i):
        return pltpu.make_async_copy(self.a2.at[i], self.oa(i, self.y, self.core), self.ls_.at[0, i])

    def a_fwd(self, i):
        o = self.oa(i, 1 - self.y, self.core)
        return self.ca(i, 5, 6, o, o, self.to_sib)

    def step_a(self, i, stage):
        y = self.y
        if stage == 0:
            self.a_y(i).start()
        elif stage == 1:
            self.a_y(i).wait_recv()
            v = self.la(i, y)
            v[...] = (v[...].astype(f32) + self.a1[i].astype(f32)).astype(bf16)

            @pl.when(self.outer)
            def _():
                self.a_in(i).start()
        elif stage == 2:
            @pl.when(self.mid)
            def _():
                self.a_in(i).wait_recv()
                v = self.la(i, y)
                v[...] = (v[...].astype(f32) + self.a2[i].astype(f32)).astype(bf16)
                self.a_mid(i).start()
        elif stage == 3:
            @pl.when(self.mid)
            def _():
                self.a_mid(i).wait_recv()
                self.a2[i] = (self.la(i, y)[...].astype(f32) + self.a3[i].astype(f32)).astype(bf16)
                self.a_out(i).start()
                src = self.a2.at[i]
                self.a_done(i, 3, 4, src, self.to_y).start()
                self.a_done(i, 4, 5, src, self.to_sib).start()
                self.a_keep(i).start()
        elif stage == 4:
            @pl.when(self.outer)
            def _():
                self.a_out(i).wait_recv()
                src = self.oa(i, y, self.core)
                self.a_done(i, 3, 4, src, self.to_y).start()
                self.a_done(i, 4, 5, src, self.to_sib).start()
        elif stage == 5:
            self.a_done(i, 3, 4, self.oa(i, y, self.core), self.to_y).wait_recv()
            self.a_fwd(i).start()

    def end_a(self, i):
        src = self.a2.at[i]
        self.a_y(i).wait_send()
        self.a_in(i).wait_send()

        @pl.when(self.mid)
        def _():
            self.a_out(i).wait_send()
            self.a_keep(i).wait()

        self.a_done(i, 3, 4, src, self.to_y).wait_send()
        self.a_done(i, 4, 5, src, self.to_sib).wait_send()
        self.a_fwd(i).wait_send()
        self.a_done(i, 4, 5, src, self.to_sib).wait_recv()
        self.a_fwd(i).wait_recv()

    def b_in(self, i):
        return self.cb(i, 0, 0, self.loc_b.at[i], self.b1.at[i], self.to_z)

    def b_mid(self, i):
        return self.cb(i, 0, 1, self.lb(i, 1 - self.mine), self.b2.at[i], self.to_mid)

    def b_y(self, i):
        return self.cb(i, 1, 2, self.lb(i, self.mine), self.b3.at[i], self.to_y)

    def fin_b(self, i):
        return self.b1.at[i, pl.ds(0, self.hb), :]

    def b_done(self, i, kind, recv, src, h, to):
        return self.cb(i, kind, recv, src, self.ob(i, h, self.core), to)

    def b_keep(self, i):
        return pltpu.make_async_copy(
            self.fin_b(i), self.ob(i, self.mine, self.core), self.ls_.at[1, i]
        )

    def step_b(self, i, stage):
        mine, core = self.mine, self.core
        if stage == 0:
            @pl.when(self.outer)
            def _():
                self.b_in(i).start()
        elif stage == 1:
            @pl.when(self.mid)
            def _():
                self.b_in(i).wait_recv()
                self.loc_b[i] = (self.loc_b[i].astype(f32) + self.b1[i].astype(f32)).astype(bf16)
                self.b_mid(i).start()
        elif stage == 2:
            @pl.when(self.mid)
            def _():
                self.b_mid(i).wait_recv()
                v = self.lb(i, mine)
                v[...] = (v[...].astype(f32) + self.b2[i].astype(f32)).astype(bf16)
                self.b_y(i).start()
        elif stage == 3:
            @pl.when(self.mid)
            def _():
                self.b_y(i).wait_recv()
                fin = self.fin_b(i)
                fin[...] = (self.lb(i, mine)[...].astype(f32) + self.b3[i].astype(f32)).astype(bf16)
                self.b_done(i, 2, 4, fin, mine, self.to_mid).start()
                self.b_done(i, 3, 3, fin, mine, self.to_z).start()
                self.b_done(i, 4, 5, fin, mine, self.to_sib).start()
                self.b_keep(i).start()
        elif stage == 4:
            @pl.when(self.mid)
            def _():
                o = self.ob(i, 1 - mine, core)
                self.b_done(i, 2, 4, o, 1 - mine, self.to_mid).wait_recv()
                self.b_done(i, 5, 4, o, 1 - mine, self.to_z).start()
                self.b_done(i, 6, 6, o, 1 - mine, self.to_sib).start()

            @pl.when(self.outer)
            def _():
                o = self.ob(i, mine, core)
                self.b_done(i, 3, 3, o, mine, self.to_z).wait_recv()
                self.b_done(i, 4, 5, o, mine, self.to_sib).start()
        elif stage == 5:
            @pl.when(self.outer)
            def _():
                o = self.ob(i, 1 - mine, core)
                self.b_done(i, 5, 4, o, 1 - mine, self.to_z).wait_recv()
                self.b_done(i, 6, 6, o, 1 - mine, self.to_sib).start()

    def end_b(self, i):
        fin = self.fin_b(i)
        mine = self.mine

        @pl.when(self.outer)
        def _():
            self.b_in(i).wait_send()

        @pl.when(self.mid)
        def _():
            self.b_mid(i).wait_send()
            self.b_y(i).wait_send()
            self.b_done(i, 2, 4, fin, mine, self.to_mid).wait_send()
            self.b_done(i, 3, 3, fin, mine, self.to_z).wait_send()
            self.b_done(i, 5, 4, fin, mine, self.to_z).wait_send()
            self.b_keep(i).wait()

        self.b_done(i, 4, 5, fin, mine, self.to_sib).wait_send()
        self.b_done(i, 6, 6, fin, mine, self.to_sib).wait_send()
        self.b_done(i, 4, 5, fin, mine, self.to_sib).wait_recv()
        self.b_done(i, 6, 6, fin, mine, self.to_sib).wait_recv()

    def step(self, t):
        for stage in range(STAGES + 1):
            i = t - (*LAGS, LAST)[stage]

            def run():
                if stage < STAGES:
                    self.step_a(i, stage)
                    self.step_b(i, stage)
                else:
                    self.end_a(i)
                    self.end_b(i)

            if not isinstance(t, int):
                pl.when(jnp.logical_and(i >= 0, i < CHUNKS))(run)
            elif 0 <= i < CHUNKS:
                run()

    def steps(self, lo, hi):
        def body(t, _):
            self.step(t)
            return 0

        lax.fori_loop(lo, hi, body, 0)

    def end(self):
        def body(i, _):
            self.end_a(i)
            self.end_b(i)
            return 0

        lax.fori_loop(END - LAST, CHUNKS, body, 0)


def scratch_of(n, side):
    whole, half = pltpu.VMEM((n, side, side), bf16), pltpu.VMEM((n, side // 2, side), bf16)
    return [
        whole,
        whole,
        half,
        half,
        half,
        whole,
        half,
        half,
        pltpu.SemaphoreType.DMA((n, 6)),
        pltpu.SemaphoreType.DMA((n, 7)),
        pltpu.SemaphoreType.DMA((n, 7)),
        pltpu.SemaphoreType.DMA((n, 7)),
        pltpu.SemaphoreType.DMA((2, n)),
    ]


def split_rows(value):
    rows, cols = value.shape
    return jnp.sum(value.reshape(rows // 8, 8, cols), axis=0)


def erf(value):
    x = jnp.clip(value, -4.0, 4.0)
    x2 = x * x
    top = -2.72614225801306e-10
    for c in (
        2.77068142495902e-08,
        -2.10102402082508e-06,
        -5.69250639462346e-05,
        -7.34990630326855e-04,
        -2.95459980854025e-03,
        -1.60960333262415e-02,
    ):
        top = top * x2 + c
    low = -1.45660718464996e-05
    for c in (
        -2.13374055278905e-04,
        -1.68282697438203e-03,
        -7.37332916720468e-03,
        -1.42647390514189e-02,
    ):
        low = low * x2 + c
    return x * top / low


def gelu_parts(u):
    cdf = 0.5 * (1.0 + erf(u * 0.7071067811865476))
    pdf = jnp.exp(-0.5 * u * u) * 0.3989422804014327
    return u * cdf, cdf + u * pdf


def normed(rows_in):
    centred = rows_in - jnp.mean(rows_in, axis=-1, keepdims=True)
    scale = lax.rsqrt(jnp.mean(centred * centred, axis=-1, keepdims=True) + 1e-06)
    return centred * scale, scale


def mm(left, right):
    return jnp.dot(left, right, preferred_element_type=f32)


def mm_tn(left, right):
    return lax.dot_general(left, right, (((0,), (0,)), ((), ())), preferred_element_type=f32)


def mm_nt(left, right):
    return lax.dot_general(left, right, (((1,), (1,)), ((), ())), preferred_element_type=f32)


LINKS = {
    "w": 4, "c": 1, "o": 4, "osib": 2, "h2t": 4, "act": 4, "pre": 4, "x0": 4, "x1": 4, "x2": 4,
    "dyb": 1, "h1t": 1, "dqkv": 6, "small": 5,
}
LINK_AT = {}
for _name, _count in LINKS.items():
    LINK_AT[_name] = sum(LINKS[n] for n in LINK_AT)
N_LINKS = sum(LINKS.values())


def layer_kernel(
    clip, again, ashift, qvb, outb, mgain, mshift, upb, downb,
    tok_h, wqkv_h, wout_h, wup_h, wdown_h, cot_h,
    lo_h, gt_h, out, small_h,
    tok, wqkv, wout, wup, wdown, cpair, hid, q, k, v, o_own, o_peer, o_sib, y1, h2t,
    act, pre, act_sib, pre_sib, xs0, xs1, xr0, xr1, dy1, dob, small, small_r, sums,
    loc_a, loc_b, a1, a2, a3, b1, b2, b3,
    as_, ar_, bs_, br_, ls_, lsem, ssem, rsem,
):
    rows = tok.shape[0]
    width = tok.shape[1]
    sm = Summer(loc_a, loc_b, (a1, a2, a3, b1, b2, b3), out, (as_, ar_, bs_, br_, ls_))
    base, z, y, core = place()
    t = lax.axis_index("tensor")
    to_x = (lax.axis_index("dp"), 1 - t)
    to_sib, to_y = sm.to_sib, sm.to_y

    def rc(name, i, src, dst, to):
        at = LINK_AT[name] + i
        return pltpu.make_async_remote_copy(
            src, dst, ssem.at[at], rsem.at[at], device_id=to, device_id_type=MESH
        )

    def cols(i, n=128):
        return pl.ds(pl.multiple_of(i * n, n), n)

    def loop(n, body, unroll=False):
        def wrapped(i, _):
            body(i)
            return 0

        lax.fori_loop(0, n, wrapped, 0, unroll=unroll)

    def load(i, src, dst):
        return pltpu.make_async_copy(src, dst, lsem.at[i])

    loads = [
        load(0, tok_h, tok),
        load(1, wqkv_h, wqkv),
        load(2, wout_h, wout.at[t]),
        load(3, wup_h, wup),
        load(4, cot_h, cpair.at[0]),
        load(5, wdown_h, wdown),
    ]
    quarter = 2 * y + core
    part = wout_h.shape[0] // 4

    def rows_of(i):
        return pl.ds(pl.multiple_of(i * part, part), part)

    def w_at(i):
        return wout.at[1 - t, rows_of(i), :]

    w_out = rc("w", 0, wout_h.at[rows_of(quarter), :], wout.at[t, rows_of(quarter), :], to_x)
    w_in = rc("w", 0, wout_h.at[rows_of(quarter), :], w_at(quarter), to_x)
    w_y = rc("w", 1, w_at(quarter), w_at(quarter), to_y)
    w_s0 = rc("w", 2, w_at(quarter), w_at(quarter), to_sib)
    other = 2 * (1 - y) + core
    w_s1 = rc("w", 3, w_at(other), w_at(other), to_sib)
    c_out = rc("c", 0, cot_h, cpair.at[1], to_sib)
    for item in loads:
        item.start()

    barrier = pltpu.get_barrier_semaphore()

    def greet(to):
        pl.semaphore_signal(barrier, inc=1, device_id=to, device_id_type=MESH)

    for to in (to_sib, to_x, to_y, sm.to_z):
        greet(to)

    @pl.when(sm.mid)
    def _():
        greet(sm.to_mid)

    loads[0].wait()
    tile = 64

    def norm_one(i):
        r = pl.ds(pl.multiple_of(i * tile, tile), tile)
        n1, _ = normed(tok[r, :].astype(f32))
        hid[r, :] = (n1 * again[...] + ashift[...]).astype(bf16)

    loop(rows // tile, norm_one, True)

    @pl.when(sm.mid)
    def _():
        pl.semaphore_wait(barrier, 5)

    @pl.when(sm.outer)
    def _():
        pl.semaphore_wait(barrier, 4)

    w_out.start()
    c_out.start()
    loads[1].wait()
    heads_w = q.shape[1]
    lane = lax.broadcasted_iota(jnp.int32, (1, 128), 1)

    def half_of(value, e):
        keep = (lane < 64) if e == 0 else (lane >= 64)
        return jnp.where(keep, value.astype(f32), 0.0).astype(bf16)

    end0 = clip[0, 0]
    end1 = end0 + clip[0, 1]
    end2 = end1 + clip[0, 2]

    def seg_of(index):
        one = lambda e: (index >= e).astype(jnp.int32)
        return one(end0) + one(end1) + one(end2)

    key_seg = seg_of(lax.broadcasted_iota(jnp.int32, (1, rows), 1))
    def same_clip(at, count):
        return seg_of(lax.broadcasted_iota(jnp.int32, (count, 1), 0) + at) == key_seg

    def softmax(products, same):
        s = jnp.where(same, products, -1e30)
        w = jnp.exp(s - jnp.max(s, axis=1, keepdims=True))
        return w * (1.0 / jnp.sum(w, axis=1, keepdims=True))

    def make_qkv(g):
        c4 = cols(g, 256)
        h = hid[...]
        q[:, c4] = ((mm(h, wqkv[0, :, c4]) + qvb[pl.ds(0, 1), c4]).astype(bf16) * 0.125).astype(bf16)
        k[:, c4] = mm(h, wqkv[1, :, c4]).astype(bf16)
        v[:, c4] = (mm(h, wqkv[2, :, c4]) + qvb[pl.ds(1, 1), c4]).astype(bf16)

    def o_send(pr):
        return rc("o", pr, o_own.at[:, cols(pr)], o_peer.at[:, cols(pr)], to_x)

    def osib_send(pr):
        m = lax.rem(pr, 2)
        return rc("osib", m, o_own.at[:, cols(pr)], o_sib.at[:, cols(m)], to_sib)

    def attend(pr):
        c2 = cols(pr)
        keys = k[:, c2]
        values = [half_of(v[:, c2], e) for e in range(2)]
        for at in range(0, rows, 256):
            r = pl.ds(at, 256)
            same = same_clip(at, 256)
            total = None
            for e in range(2):
                p = softmax(mm_nt(half_of(q[r, c2], e), keys), same)
                term = mm(p.astype(bf16), values[e])
                total = term if total is None else total + term
            o_own[r, c2] = total.astype(bf16)
        o_send(pr).start()

        @pl.when(pr // 2 == 1 - core)
        def _():
            osib_send(pr).start()

    def group_of_heads(g):
        make_qkv(g)
        attend(2 * g)
        attend(2 * g + 1)

    loop(heads_w // 256, group_of_heads)

    w_in.wait_recv()
    w_y.start()
    w_s0.start()
    loads[2].wait()
    nrow = 128

    def own_part(i):
        r = pl.ds(pl.multiple_of(i * nrow, nrow), nrow)
        y1[r, :] = mm(o_own[r, :], wout[t])

    loop(rows // nrow, own_part, True)
    w_y.wait_recv()
    w_s1.start()
    w_s0.wait_recv()
    w_s1.wait_recv()
    w_y.wait_send()
    w_s0.wait_send()
    w_s1.wait_send()
    for pr in range(4):
        o_send(pr).wait_recv()

    def peer_part(i):
        r = pl.ds(pl.multiple_of(i * nrow, nrow), nrow)
        dy1[r, :] = mm(o_peer[r, :], wout[1 - t])

    loop(rows // nrow, peer_part, True)

    def h2t_send(i):
        return rc("h2t", i, h2t.at[0, :, cols(i, nrow)], h2t.at[1, :, cols(i, nrow)], to_sib)

    def norm_two(i):
        r = pl.ds(pl.multiple_of(i * nrow, nrow), nrow)
        x = tok[r, :].astype(f32)
        y = x + (y1[r, :] + dy1[r, :]) + outb[...]
        y1[r, :] = y
        n2, _ = normed(y)
        h2 = (n2 * mgain[...] + mshift[...]).astype(bf16)
        hid_two[r, :] = h2
        h2t[0, :, cols(i, nrow)] = h2.T
        h2t_send(i).start()

    hid_two = xs1
    loop(rows // nrow, norm_two, True)

    loads[3].wait()
    loads[4].wait()
    loads[5].wait()
    c_out.wait_recv()

    def act_send(j):
        c4 = cols(2 * j + 1 - core, 256)
        return rc("act", j, act.at[:, c4], act_sib.at[j], to_sib)

    def pre_send(j):
        c4 = cols(2 * j + 1 - core, 256)
        return rc("pre", j, pre.at[:, c4], pre_sib.at[j], to_sib)

    def hidden(piece):
        c4 = cols(piece, 256)
        a, d = gelu_parts(mm(hid_two[...], wup[:, c4]) + upb[:, c4])
        du = (mm_nt(cpair[0], wdown[c4, :]) * d).astype(bf16)
        act[:, c4] = a.astype(bf16)
        pre[:, c4] = du
        total = split_rows(du.astype(f32))
        row = 6 + piece // 4
        small[pl.ds(row, 1), cols(lax.rem(piece, 4), 256)] = jnp.sum(total, axis=0, keepdims=True)

    def hidden_pair(j):
        hidden(2 * j + 1 - core)
        act_send(j).start()
        pre_send(j).start()
        hidden(2 * j + core)

    def chunk(j):
        mine = cols(2 * j + core, 256)
        act_send(j).wait_recv()
        for n in range(2):
            wide = pl.ds(n * 512, 512)
            block = mm_tn(act[:, mine], cpair[0, :, wide]) + mm_tn(act_sib[j], cpair[1, :, wide])
            low = block.astype(bf16)
            loc_a[4 * j + 2 * n] = low[:, :256]
            loc_a[4 * j + 2 * n + 1] = low[:, 256:]
        pre_send(j).wait_recv()
        for m in range(2):
            high = pl.ds(m * 512, 512)
            low = (mm(h2t[0, high, :], pre[:, mine]) + mm(h2t[1, high, :], pre_sib[j])).astype(bf16)
            loc_b[4 * j + 2 * m] = low[:256]
            loc_b[4 * j + 2 * m + 1] = low[256:]

    for i in range(4):
        h2t_send(i).wait_recv()
    hidden_pair(0)
    chunk(0)
    for j in range(1, 4):
        sm.step(j - 1)
        hidden_pair(j)
    sm.step(3)

    def x_send(name, n, src, dst):
        return rc(name, n, src.at[:, cols(n, 256)], dst.at[:, cols(n, 256)], to_x)

    def back_two(n):
        xs0[:, cols(n, 256)] = mm_nt(pre[...], wup[cols(n, 256), :]).astype(bf16)
        x_send("x0", n, xs0, xr0).start()

    loop(width // 256, back_two)
    chunk(1)
    sm.step(4)

    def forward_two(n):
        xs1[:, cols(n, 256)] = mm(act[...], wdown[:, cols(n, 256)]).astype(bf16)
        x_send("x1", n, xs1, xr1).start()

    loop(width // 256, forward_two)
    sm.step(5)
    chunk(2)
    sm.step(6)
    chunk(3)
    sm.step(7)

    for i in range(4):
        h2t_send(i).wait_send()
    h1t = h2t

    def turn_first(i):
        r = pl.ds(pl.multiple_of(i * nrow, nrow), nrow)
        h1t[0, :, cols(i, nrow)] = hid[r, :].T

    loop(rows // nrow, turn_first, True)
    h1t_out = rc("h1t", 0, h1t.at[0], h1t.at[1], to_sib)

    def cot_sum(i, total):
        r = pl.ds(pl.multiple_of(i * tile, tile), tile)
        return total + split_rows(cpair[0, r, :].astype(f32))

    total = lax.fori_loop(0, rows // tile, cot_sum, jnp.zeros((8, width), f32), unroll=True)
    small[pl.ds(8, 1), :] = jnp.sum(total, axis=0, keepdims=True)
    sm.steps(8, 10)

    for n in range(4):
        x_send("x0", n, xs0, xr0).wait_recv()
    sums[...] = jnp.zeros_like(sums)
    back = 128
    dyb = xr0

    def norm_two_back(i):
        r = pl.ds(pl.multiple_of(i * back, back), back)
        g = xs0[r, :].astype(f32) + xr0[r, :].astype(f32)
        n2, r2 = normed(y1[r, :])
        gn = g * n2
        sums[0] += split_rows(gn)
        sums[1] += split_rows(g)
        e2 = g * mgain[...]
        m1 = jnp.mean(e2, axis=-1, keepdims=True)
        m2 = jnp.mean(e2 * n2, axis=-1, keepdims=True)
        d = cpair[0, r, :].astype(f32) + r2 * (e2 - m1 - n2 * m2)
        sums[2] += split_rows(d)
        dy1[r, :] = d
        dyb[r, :] = d.astype(bf16)

    loop(rows // back, norm_two_back)
    dyb_out = rc("dyb", 0, dyb, wout.at[1 - t], to_sib)
    dyb_out.start()
    for i, row in enumerate((4, 5, 3)):
        small[pl.ds(row, 1), :] = jnp.sum(sums[i], axis=0, keepdims=True)
    for n in range(4):
        x_send("x0", n, xs0, xr0).wait_send()

    def back_heads(n):
        dob[:, cols(n, 256)] = mm_nt(dyb[...], wout[t, cols(n, 256), :]).astype(bf16)

    sm.step(10)
    loop(heads_w // 256, back_heads)
    osib_send(0).wait_recv()
    osib_send(1).wait_recv()
    dyb_out.wait_recv()
    h1t_out.start()
    for n in range(width // 512):
        wide = pl.ds(n * 512, 512)
        low = (
            mm_tn(o_own[:, cols(core, 256)], dyb[:, wide]) + mm_tn(o_sib[...], wout[1 - t, :, wide])
        ).astype(bf16)
        loc_a[16 + 2 * n] = low[:, :256]
        loc_a[17 + 2 * n] = low[:, 256:]

    sm.step(11)

    def dqkv_send(w, m, src, pr):
        return rc("dqkv", 2 * w + m, src.at[:, cols(pr)], act_sib.at[w, :, cols(m)], to_sib)

    def attend_back(pr):
        c2 = cols(pr)
        same = same_clip(0, rows)
        dq = dk = dv = None
        for e in range(2):
            q_e, do_e = half_of(q[:, c2], e), half_of(dob[:, c2], e)
            p = softmax(mm_nt(q_e, k[:, c2]), same)
            dp = mm_nt(do_e, v[:, c2])
            ds = (p * (dp - jnp.sum(p * dp, axis=1, keepdims=True))).astype(bf16)
            terms = (
                mm(ds, half_of(k[:, c2], e)) * 0.125,
                mm_tn(ds, q_e),
                mm_tn(p.astype(bf16), do_e),
            )
            dq, dk, dv = terms if dq is None else (dq + terms[0], dk + terms[1], dv + terms[2])
        q[:, c2] = dq.astype(bf16)
        k[:, c2] = dk.astype(bf16)
        v[:, c2] = dv.astype(bf16)
        small[pl.ds(2, 1), c2] = jnp.sum(q[:, c2].astype(f32), axis=0, keepdims=True)
        small[pl.ds(2, 1), cols(pr + 4)] = jnp.sum(v[:, c2].astype(f32), axis=0, keepdims=True)

    def theirs(m):
        pr = 2 * (1 - core) + m
        attend_back(pr)
        for w, src in enumerate((q, k, v)):
            dqkv_send(w, m, src, pr).start()

    loop(2, theirs)
    sm.step(12)

    def ours(m):
        attend_back(2 * core + m)

    loop(2, ours)
    sm.step(13)
    h1t_out.wait_recv()
    for w, src in enumerate((q, k, v)):
        for m in range(2):
            dqkv_send(w, m, src, m).wait_recv()
        for m in range(4):
            high = pl.ds(m * 256, 256)
            low = mm(h1t[0, high, :], src[:, cols(core, 256)]) + mm(h1t[1, high, :], act_sib[w])
            at = 3 * m + w
            if at < 4:
                loc_a[20 + at] = low.astype(bf16)
            else:
                loc_b[12 + at] = low.astype(bf16)
    sm.step(14)

    last = wup.at[pl.ds(0, rows), pl.ds(0, width)]

    def back_one(n):
        c4 = cols(n, 256)
        xs0[:, c4] = (
            mm_nt(q[...], wqkv[0, c4, :]) + mm_nt(k[...], wqkv[1, c4, :]) + mm_nt(v[...], wqkv[2, c4, :])
        ).astype(bf16)
        x_send("x2", n, xs0, last).start()

    loop(width // 256, back_one)
    sm.steps(15, 18)

    for n in range(4):
        x_send("x1", n, xs1, xr1).wait_recv()

    def finish(i):
        r = pl.ds(pl.multiple_of(i * tile, tile), tile)
        hid[r, :] = (
            y1[r, :] + (xs1[r, :].astype(f32) + xr1[r, :].astype(f32)) + downb[...]
        ).astype(bf16)

    loop(rows // tile, finish, True)
    lo_out = load(6, hid, lo_h)
    lo_out.start()

    sm.steps(18, 20)
    for n in range(4):
        x_send("x2", n, xs0, last).wait_recv()
    sums[...] = jnp.zeros_like(sums)

    def norm_one_back(i):
        r = pl.ds(pl.multiple_of(i * back, back), back)
        g = xs0[r, :].astype(f32) + last[r, :].astype(f32)
        n1, r1 = normed(tok[r, :].astype(f32))
        gn = g * n1
        sums[0] += split_rows(gn)
        sums[1] += split_rows(g)
        e1 = g * again[...]
        m1 = jnp.mean(e1, axis=-1, keepdims=True)
        m2 = jnp.mean(e1 * n1, axis=-1, keepdims=True)
        tok[r, :] = (dy1[r, :] + r1 * (e1 - m1 - n1 * m2)).astype(bf16)

    loop(rows // back, norm_one_back)
    gt_out = load(7, tok, gt_h)
    gt_out.start()
    for i, row in enumerate((0, 1)):
        small[pl.ds(row, 1), :] = jnp.sum(sums[i], axis=0, keepdims=True)

    def small_rc(i, src, to):
        return rc("small", i, src, small_r.at[i], to)

    small_sib = small_rc(0, small, to_sib)
    small_y = small_rc(1, small_r.at[0], to_y)
    small_in = small_rc(2, small_r.at[1], sm.to_z)
    small_mid = small_rc(3, small_r.at[2], sm.to_mid)
    small_out = small_rc(4, small_r.at[3], sm.to_z)
    small_sib.start()
    sm.step(20)
    small_sib.wait_recv()
    small_r[0] += small[...]
    small_y.start()
    sm.step(21)
    small_y.wait_recv()
    small_r[1] += small_r[0]

    @pl.when(sm.outer)
    def _():
        small_in.start()

    sm.step(22)

    @pl.when(sm.mid)
    def _():
        small_in.wait_recv()
        small_r[2] += small_r[1]
        small_mid.start()

    sm.step(23)

    @pl.when(sm.mid)
    def _():
        small_mid.wait_recv()
        small_r[3] += small_r[2]
        small_out.start()

    sm.steps(24, END)

    @pl.when(sm.outer)
    def _():
        small_out.wait_recv()

    keep = load(8, small_r.at[jnp.where(sm.outer, 4, 3)], small_h)
    keep.start()

    sm.end()
    w_out.wait_send()
    c_out.wait_send()
    h1t_out.wait_send()
    dyb_out.wait_send()
    for i in range(4):
        o_send(i).wait_send()
        act_send(i).wait_send()
        pre_send(i).wait_send()
        x_send("x1", i, xs1, xr1).wait_send()
        x_send("x2", i, xs0, last).wait_send()
    for m in range(2):
        osib_send(m).wait_send()
        for w, src in enumerate((q, k, v)):
            dqkv_send(w, m, src, m).wait_send()
    small_sib.wait_send()
    small_y.wait_send()

    @pl.when(sm.outer)
    def _():
        small_in.wait_send()

    @pl.when(sm.mid)
    def _():
        small_mid.wait_send()
        small_out.wait_send()

    lo_out.wait()
    gt_out.wait()
    keep.wait()


def layer(clip, vectors, tokens, wqkv, wout, wup, wdown, cot):
    rows, width = tokens.shape
    heads_w = wqkv.shape[2]
    hidden = wup.shape[1]
    big = pl.BlockSpec(memory_space=pl.ANY)
    small = pl.BlockSpec(memory_space=pltpu.VMEM)
    vm = lambda *shape: pltpu.VMEM(shape, bf16)
    vf = lambda *shape: pltpu.VMEM(shape, f32)
    return pl.pallas_call(
        layer_kernel,
        out_shape=(
            jax.ShapeDtypeStruct((rows, width), bf16),
            jax.ShapeDtypeStruct((rows, width), bf16),
            jax.ShapeDtypeStruct((2 * CHUNKS, 2, SIDE, SIDE), bf16),
            jax.ShapeDtypeStruct((16, width), f32),
        ),
        in_specs=[pl.BlockSpec(memory_space=pltpu.SMEM)] + [small] * len(vectors) + [big] * 6,
        out_specs=[big] * 4,
        scratch_shapes=[
            vm(rows, width),
            vm(*wqkv.shape),
            vm(2, *wout.shape),
            vm(*wup.shape),
            vm(*wdown.shape),
            vm(2, rows, width),
            vm(rows, width),
            vm(rows, heads_w),
            vm(rows, heads_w),
            vm(rows, heads_w),
            vm(rows, heads_w),
            vm(rows, heads_w),
            vm(rows, 256),
            vf(rows, width),
            vm(2, width, rows),
            vm(rows, hidden),
            vm(rows, hidden),
            vm(4, rows, 256),
            vm(4, rows, 256),
            vm(rows, width),
            vm(rows, width),
            vm(rows, width),
            vm(rows, width),
            vf(rows, width),
            vm(rows, heads_w),
            vf(16, width),
            vf(5, 16, width),
            vf(3, 8, width),
        ]
        + scratch_of(CHUNKS, SIDE)
        + [
            pltpu.SemaphoreType.DMA((9,)),
            pltpu.SemaphoreType.DMA((N_LINKS,)),
            pltpu.SemaphoreType.DMA((N_LINKS,)),
        ],
        compiler_params=pltpu.CompilerParams(
            has_side_effects=True, collective_id=0, vmem_limit_bytes=VMEM_BYTES
        ),
        name="layer",
    )(clip, *vectors, tokens, wqkv, wout, wup, wdown, cot)


VMEM_BYTES = 60 << 20


STEPS = 8


def widen_kernel(
    down_in, up_in, out_in, qkv_in, s_in, lo_in, gt_in,
    lo, gt, down, out, up, qkv, ag, ash, qv, ob, mg, ms, ub, db,
):
    lo[...] = lo_in[...]
    gt[...] = gt_in[...]
    for n in range(4):
        c = pl.ds(n * SIDE, SIDE)
        down[:, c] = down_in[n, 0].astype(f32)
        out[:, c] = out_in[n, 0].astype(f32)
        up[c, :] = up_in[n, 0].astype(f32)
    for w in range(3):
        for core in range(2):
            qkv[w, :, pl.ds(core * SIDE, SIDE)] = qkv_in[w, core].astype(f32)

    @pl.when(pl.program_id(0) == STEPS - 1)
    def _():
        for ref, row in ((ag, 0), (ash, 1), (ob, 3), (mg, 4), (ms, 5), (db, 8)):
            ref[...] = s_in[pl.ds(row, 1), :]
        qv[pl.ds(0, 1), :] = s_in[pl.ds(2, 1), pl.ds(0, 512)]
        qv[pl.ds(1, 1), :] = s_in[pl.ds(2, 1), pl.ds(512, 512)]
        ub[:, pl.ds(0, 1024)] = s_in[pl.ds(6, 1), :]
        ub[:, pl.ds(1024, 1024)] = s_in[pl.ds(7, 1), :]


def widen(sums, small, lo, gt):
    whole = lambda *shape: pl.BlockSpec(shape, lambda i: (0,) * len(shape))
    rows_in = pl.BlockSpec((lo.shape[0] // STEPS, lo.shape[1]), lambda i: (i, 0))
    vectors = ((1, 1024), (1, 1024), (2, 512), (1, 1024), (1, 1024), (1, 1024), (1, 2048), (1, 1024))
    got = pl.pallas_call(
        widen_kernel,
        grid=(STEPS,),
        in_specs=[
            pl.BlockSpec((4, 1, SIDE, SIDE), lambda i: (i // 2, i % 2, 0, 0)),
            pl.BlockSpec((4, 1, SIDE, SIDE), lambda i: (4 + i // 2, i % 2, 0, 0)),
            pl.BlockSpec((4, 1, SIDE // 4, SIDE), lambda i: (8, i // 4, i % 4, 0)),
            pl.BlockSpec((3, 2, SIDE // 2, SIDE), lambda i: (12 + i // 2, 0, i % 2, 0)),
            whole(16, 1024),
            rows_in,
            rows_in,
        ],
        out_specs=[
            rows_in,
            rows_in,
            pl.BlockSpec((SIDE, 1024), lambda i: (i, 0)),
            pl.BlockSpec((SIDE // 4, 1024), lambda i: (i, 0)),
            pl.BlockSpec((1024, SIDE), lambda i: (0, i)),
            pl.BlockSpec((3, SIDE // 2, 512), lambda i: (0, i, 0)),
        ]
        + [whole(*shape) for shape in vectors],
        out_shape=[
            jax.ShapeDtypeStruct(lo.shape, bf16),
            jax.ShapeDtypeStruct(gt.shape, bf16),
            jax.ShapeDtypeStruct((2048, 1024), f32),
            jax.ShapeDtypeStruct((512, 1024), f32),
            jax.ShapeDtypeStruct((1024, 2048), f32),
            jax.ShapeDtypeStruct((3, 1024, 512), f32),
        ]
        + [jax.ShapeDtypeStruct(shape, f32) for shape in vectors],
        compiler_params=pltpu.CompilerParams(vmem_limit_bytes=56 << 20),
        name="widen",
    )(sums, sums, sums, sums, small, lo, gt)
    lo, gt, down, out, up, qkv, ag, ash, qv, ob, mg, ms, ub, db = got
    flat = lambda v: v.reshape(-1)
    return (
        lo, gt, flat(ag), flat(ash), qkv, qv, out, flat(ob), flat(mg), flat(ms), up, flat(ub),
        down, flat(db),
    )


def local(
    tokens, clip_lengths, attn_gain, attn_shift, qkv_weight, qv_bias, out_weight, out_bias,
    mlp_gain, mlp_shift, up_weight, up_bias, down_weight, down_bias, cotangent,
):
    row = lambda v: v.reshape(1, -1)
    vectors = (
        row(attn_gain), row(attn_shift), qv_bias, row(out_bias), row(mlp_gain), row(mlp_shift),
        row(up_bias), row(down_bias),
    )
    layer_output, grad_tokens, sums, small = layer(
        clip_lengths, vectors, tokens, qkv_weight, out_weight, up_weight, down_weight, cotangent
    )
    groups = lax.axis_size("dp")
    if groups > CELL:
        cells = [[k * CELL + i for k in range(groups // CELL)] for i in range(CELL)]
        sums, small = lax.psum((sums.astype(f32), small), "dp", axis_index_groups=cells)
    return widen(sums, small, layer_output, grad_tokens)


def solution(mesh):
    placed = (
        P("dp", None), P("dp", None), P(), P(), P(None, None, "tensor"), P(None, "tensor"),
        P("tensor", None), P(), P(), P(), P(None, "tensor"), P("tensor"), P("tensor", None), P(),
        P("dp", None),
    )
    return jax.shard_map(
        local,
        mesh=mesh,
        in_specs=placed,
        out_specs=(
            P("dp", None), P("dp", None), P(), P(), P(None, None, "tensor"), P(None, "tensor"),
            P("tensor", None), P(), P(), P(), P(None, "tensor"), P("tensor"), P("tensor", None), P(),
        ),
        check_vma=False,
    )
```

```python
import jax
import jax.numpy as jnp
from jax import lax
from jax.experimental import pallas as pl
from jax.experimental.pallas import tpu as pltpu
from jax.sharding import PartitionSpec as P

MESH = pl.DeviceIdType.MESH
bf16, f32 = jnp.bfloat16, jnp.float32
CELL = 16
LAGS = (0, 2, 4, 6, 8, 10)
LAST = LAGS[-1] + 2
STAGES = len(LAGS)
SIDE = 256
N_DOWN = N_UP = 16
CHUNKS = 24
END = CHUNKS + LAGS[-1]


def pick(low, first, second):
    if isinstance(low, bool):
        return first if low else second
    return jnp.where(low, first, second)


def place_a(i):
    return pick(i < N_DOWN, i, i + N_UP)


def place_b(i):
    return pick(i < N_UP, i + N_DOWN, i + CHUNKS)


def place():
    at = lax.axis_index("dp")
    base = (at // CELL) * CELL
    inner = at - base
    z = inner // 4
    y = (inner // 2) % 2
    core = inner % 2
    return base, z, y, core


class Summer:
    def __init__(self, loc_a, loc_b, bufs, out, sems):
        self.loc_a, self.loc_b = loc_a, loc_b
        (self.a1, self.a2, self.a3, self.b1, self.b2, self.b3) = bufs
        self.out = out
        self.as_, self.ar_, self.bs_, self.br_, self.ls_ = sems
        self.ha = loc_a.shape[1] // 2
        self.hb = loc_b.shape[1] // 2
        base, z, y, core = place()
        self.y, self.core = y, core
        self.outer = jnp.logical_or(z == 0, z == 3)
        self.mid = jnp.logical_not(self.outer)
        self.mine = jnp.where(z >= 2, 1, 0)
        across = 3 - z
        toward = jnp.where(z < 2, 1 - z, 5 - z)
        tensor = lax.axis_index("tensor")

        def dev(zz, yy, cc):
            return (base + zz * 4 + yy * 2 + cc, tensor)

        self.to_sib = dev(z, y, 1 - core)
        self.to_y = dev(z, 1 - y, core)
        self.to_mid = dev(across, y, core)
        self.to_z = dev(toward, y, core)

    def la(self, i, h):
        return self.loc_a.at[i, pl.ds(pl.multiple_of(h * self.ha, self.ha), self.ha), :]

    def lb(self, i, h):
        return self.loc_b.at[i, pl.ds(pl.multiple_of(h * self.hb, self.hb), self.hb), :]

    def oa(self, i, h, core):
        return self.out.at[
            place_a(i), core, pl.ds(pl.multiple_of(h * self.ha, self.ha), self.ha), :
        ]

    def ob(self, i, h, core):
        return self.out.at[
            place_b(i), core, pl.ds(pl.multiple_of(h * self.hb, self.hb), self.hb), :
        ]

    def ca(self, i, kind, recv, src, dst, to):
        return pltpu.make_async_remote_copy(
            src, dst, self.as_.at[i, kind], self.ar_.at[i, recv], device_id=to, device_id_type=MESH
        )

    def cb(self, i, kind, recv, src, dst, to):
        return pltpu.make_async_remote_copy(
            src, dst, self.bs_.at[i, kind], self.br_.at[i, recv], device_id=to, device_id_type=MESH
        )

    def a_y(self, i):
        return self.ca(i, 0, 0, self.la(i, 1 - self.y), self.a1.at[i], self.to_y)

    def a_in(self, i):
        return self.ca(i, 1, 1, self.la(i, self.y), self.a2.at[i], self.to_z)

    def a_mid(self, i):
        return self.ca(i, 1, 2, self.la(i, self.y), self.a3.at[i], self.to_mid)

    def a_out(self, i):
        return self.ca(i, 2, 3, self.a2.at[i], self.oa(i, self.y, self.core), self.to_z)

    def a_done(self, i, kind, recv, src, to):
        return self.ca(i, kind, recv, src, self.oa(i, self.y, self.core), to)

    def a_keep(self, i):
        return pltpu.make_async_copy(self.a2.at[i], self.oa(i, self.y, self.core), self.ls_.at[0, i])

    def a_fwd(self, i):
        o = self.oa(i, 1 - self.y, self.core)
        return self.ca(i, 5, 6, o, o, self.to_sib)

    def step_a(self, i, stage):
        y = self.y
        if stage == 0:
            self.a_y(i).start()
        elif stage == 1:
            self.a_y(i).wait_recv()
            v = self.la(i, y)
            v[...] = (v[...].astype(f32) + self.a1[i].astype(f32)).astype(bf16)

            @pl.when(self.outer)
            def _():
                self.a_in(i).start()
        elif stage == 2:
            @pl.when(self.mid)
            def _():
                self.a_in(i).wait_recv()
                v = self.la(i, y)
                v[...] = (v[...].astype(f32) + self.a2[i].astype(f32)).astype(bf16)
                self.a_mid(i).start()
        elif stage == 3:
            @pl.when(self.mid)
            def _():
                self.a_mid(i).wait_recv()
                self.a2[i] = (self.la(i, y)[...].astype(f32) + self.a3[i].astype(f32)).astype(bf16)
                self.a_out(i).start()
                src = self.a2.at[i]
                self.a_done(i, 3, 4, src, self.to_y).start()
                self.a_done(i, 4, 5, src, self.to_sib).start()
                self.a_keep(i).start()
        elif stage == 4:
            @pl.when(self.outer)
            def _():
                self.a_out(i).wait_recv()
                src = self.oa(i, y, self.core)
                self.a_done(i, 3, 4, src, self.to_y).start()
                self.a_done(i, 4, 5, src, self.to_sib).start()
        elif stage == 5:
            self.a_done(i, 3, 4, self.oa(i, y, self.core), self.to_y).wait_recv()
            self.a_fwd(i).start()

    def end_a(self, i):
        src = self.a2.at[i]
        self.a_y(i).wait_send()
        self.a_in(i).wait_send()

        @pl.when(self.mid)
        def _():
            self.a_out(i).wait_send()
            self.a_keep(i).wait()

        self.a_done(i, 3, 4, src, self.to_y).wait_send()
        self.a_done(i, 4, 5, src, self.to_sib).wait_send()
        self.a_fwd(i).wait_send()
        self.a_done(i, 4, 5, src, self.to_sib).wait_recv()
        self.a_fwd(i).wait_recv()

    def b_in(self, i):
        return self.cb(i, 0, 0, self.loc_b.at[i], self.b1.at[i], self.to_z)

    def b_mid(self, i):
        return self.cb(i, 0, 1, self.lb(i, 1 - self.mine), self.b2.at[i], self.to_mid)

    def b_y(self, i):
        return self.cb(i, 1, 2, self.lb(i, self.mine), self.b3.at[i], self.to_y)

    def fin_b(self, i):
        return self.b1.at[i, pl.ds(0, self.hb), :]

    def b_done(self, i, kind, recv, src, h, to):
        return self.cb(i, kind, recv, src, self.ob(i, h, self.core), to)

    def b_keep(self, i):
        return pltpu.make_async_copy(
            self.fin_b(i), self.ob(i, self.mine, self.core), self.ls_.at[1, i]
        )

    def step_b(self, i, stage):
        mine, core = self.mine, self.core
        if stage == 0:
            @pl.when(self.outer)
            def _():
                self.b_in(i).start()
        elif stage == 1:
            @pl.when(self.mid)
            def _():
                self.b_in(i).wait_recv()
                self.loc_b[i] = (self.loc_b[i].astype(f32) + self.b1[i].astype(f32)).astype(bf16)
                self.b_mid(i).start()
        elif stage == 2:
            @pl.when(self.mid)
            def _():
                self.b_mid(i).wait_recv()
                v = self.lb(i, mine)
                v[...] = (v[...].astype(f32) + self.b2[i].astype(f32)).astype(bf16)
                self.b_y(i).start()
        elif stage == 3:
            @pl.when(self.mid)
            def _():
                self.b_y(i).wait_recv()
                fin = self.fin_b(i)
                fin[...] = (self.lb(i, mine)[...].astype(f32) + self.b3[i].astype(f32)).astype(bf16)
                self.b_done(i, 2, 4, fin, mine, self.to_mid).start()
                self.b_done(i, 3, 3, fin, mine, self.to_z).start()
                self.b_done(i, 4, 5, fin, mine, self.to_sib).start()
                self.b_keep(i).start()
        elif stage == 4:
            @pl.when(self.mid)
            def _():
                o = self.ob(i, 1 - mine, core)
                self.b_done(i, 2, 4, o, 1 - mine, self.to_mid).wait_recv()
                self.b_done(i, 5, 4, o, 1 - mine, self.to_z).start()
                self.b_done(i, 6, 6, o, 1 - mine, self.to_sib).start()

            @pl.when(self.outer)
            def _():
                o = self.ob(i, mine, core)
                self.b_done(i, 3, 3, o, mine, self.to_z).wait_recv()
                self.b_done(i, 4, 5, o, mine, self.to_sib).start()
        elif stage == 5:
            @pl.when(self.outer)
            def _():
                o = self.ob(i, 1 - mine, core)
                self.b_done(i, 5, 4, o, 1 - mine, self.to_z).wait_recv()
                self.b_done(i, 6, 6, o, 1 - mine, self.to_sib).start()

    def end_b(self, i):
        fin = self.fin_b(i)
        mine = self.mine

        @pl.when(self.outer)
        def _():
            self.b_in(i).wait_send()

        @pl.when(self.mid)
        def _():
            self.b_mid(i).wait_send()
            self.b_y(i).wait_send()
            self.b_done(i, 2, 4, fin, mine, self.to_mid).wait_send()
            self.b_done(i, 3, 3, fin, mine, self.to_z).wait_send()
            self.b_done(i, 5, 4, fin, mine, self.to_z).wait_send()
            self.b_keep(i).wait()

        self.b_done(i, 4, 5, fin, mine, self.to_sib).wait_send()
        self.b_done(i, 6, 6, fin, mine, self.to_sib).wait_send()
        self.b_done(i, 4, 5, fin, mine, self.to_sib).wait_recv()
        self.b_done(i, 6, 6, fin, mine, self.to_sib).wait_recv()

    def step(self, t):
        for stage in range(STAGES + 1):
            i = t - (*LAGS, LAST)[stage]

            def run():
                if stage < STAGES:
                    self.step_a(i, stage)
                    self.step_b(i, stage)
                else:
                    self.end_a(i)
                    self.end_b(i)

            if not isinstance(t, int):
                pl.when(jnp.logical_and(i >= 0, i < CHUNKS))(run)
            elif 0 <= i < CHUNKS:
                run()

    def steps(self, lo, hi):
        def body(t, _):
            self.step(t)
            return 0

        lax.fori_loop(lo, hi, body, 0)

    def end(self):
        def body(i, _):
            self.end_a(i)
            self.end_b(i)
            return 0

        lax.fori_loop(END - LAST, CHUNKS, body, 0)


def scratch_of(n, side):
    whole, half = pltpu.VMEM((n, side, side), bf16), pltpu.VMEM((n, side // 2, side), bf16)
    return [
        whole,
        whole,
        half,
        half,
        half,
        whole,
        half,
        half,
        pltpu.SemaphoreType.DMA((n, 6)),
        pltpu.SemaphoreType.DMA((n, 7)),
        pltpu.SemaphoreType.DMA((n, 7)),
        pltpu.SemaphoreType.DMA((n, 7)),
        pltpu.SemaphoreType.DMA((2, n)),
    ]


def split_rows(value):
    rows, cols = value.shape
    return jnp.sum(value.reshape(rows // 8, 8, cols), axis=0)


def erf(value):
    x = jnp.clip(value, -4.0, 4.0)
    x2 = x * x
    top = -2.72614225801306e-10
    for c in (
        2.77068142495902e-08,
        -2.10102402082508e-06,
        -5.69250639462346e-05,
        -7.34990630326855e-04,
        -2.95459980854025e-03,
        -1.60960333262415e-02,
    ):
        top = top * x2 + c
    low = -1.45660718464996e-05
    for c in (
        -2.13374055278905e-04,
        -1.68282697438203e-03,
        -7.37332916720468e-03,
        -1.42647390514189e-02,
    ):
        low = low * x2 + c
    return x * top / low


def gelu_parts(u):
    cdf = 0.5 * (1.0 + erf(u * 0.7071067811865476))
    pdf = jnp.exp(-0.5 * u * u) * 0.3989422804014327
    return u * cdf, cdf + u * pdf


def normed(rows_in):
    centred = rows_in - jnp.mean(rows_in, axis=-1, keepdims=True)
    scale = lax.rsqrt(jnp.mean(centred * centred, axis=-1, keepdims=True) + 1e-06)
    return centred * scale, scale


def mm(left, right):
    return jnp.dot(left, right, preferred_element_type=f32)


def mm_tn(left, right):
    return lax.dot_general(left, right, (((0,), (0,)), ((), ())), preferred_element_type=f32)


def mm_nt(left, right):
    return lax.dot_general(left, right, (((1,), (1,)), ((), ())), preferred_element_type=f32)


LINKS = {
    "w": 4, "c": 1, "o": 4, "osib": 2, "h2t": 4, "act": 4, "pre": 4, "x0": 4, "x1": 4, "x2": 4,
    "dyb": 1, "h1t": 1, "dqkv": 6, "small": 5,
}
LINK_AT = {}
for _name, _count in LINKS.items():
    LINK_AT[_name] = sum(LINKS[n] for n in LINK_AT)
N_LINKS = sum(LINKS.values())


def layer_kernel(
    clip, again, ashift, qvb, outb, mgain, mshift, upb, downb,
    tok_h, wqkv_h, wout_h, wup_h, wdown_h, cot_h,
    lo_h, gt_h, out, small_h,
    tok, wqkv, wout, wup, wdown, cpair, hid, q, k, v, o_own, o_peer, o_sib, y1, h2t,
    act, pre, act_sib, pre_sib, xs0, xs1, xr0, xr1, dy1, dob, small, small_r, sums,
    loc_a, loc_b, a1, a2, a3, b1, b2, b3,
    as_, ar_, bs_, br_, ls_, lsem, ssem, rsem,
):
    rows = tok.shape[0]
    width = tok.shape[1]
    sm = Summer(loc_a, loc_b, (a1, a2, a3, b1, b2, b3), out, (as_, ar_, bs_, br_, ls_))
    base, z, y, core = place()
    t = lax.axis_index("tensor")
    to_x = (lax.axis_index("dp"), 1 - t)
    to_sib, to_y = sm.to_sib, sm.to_y

    def rc(name, i, src, dst, to):
        at = LINK_AT[name] + i
        return pltpu.make_async_remote_copy(
            src, dst, ssem.at[at], rsem.at[at], device_id=to, device_id_type=MESH
        )

    def cols(i, n=128):
        return pl.ds(pl.multiple_of(i * n, n), n)

    def loop(n, body, unroll=False):
        def wrapped(i, _):
            body(i)
            return 0

        lax.fori_loop(0, n, wrapped, 0, unroll=unroll)

    def load(i, src, dst):
        return pltpu.make_async_copy(src, dst, lsem.at[i])

    loads = [
        load(0, tok_h, tok),
        load(1, wqkv_h, wqkv),
        load(2, wout_h, wout.at[t]),
        load(3, wup_h, wup),
        load(4, cot_h, cpair.at[0]),
        load(5, wdown_h, wdown),
    ]
    quarter = 2 * y + core
    part = wout_h.shape[0] // 4

    def rows_of(i):
        return pl.ds(pl.multiple_of(i * part, part), part)

    def w_at(i):
        return wout.at[1 - t, rows_of(i), :]

    w_out = rc("w", 0, wout_h.at[rows_of(quarter), :], wout.at[t, rows_of(quarter), :], to_x)
    w_in = rc("w", 0, wout_h.at[rows_of(quarter), :], w_at(quarter), to_x)
    w_y = rc("w", 1, w_at(quarter), w_at(quarter), to_y)
    w_s0 = rc("w", 2, w_at(quarter), w_at(quarter), to_sib)
    other = 2 * (1 - y) + core
    w_s1 = rc("w", 3, w_at(other), w_at(other), to_sib)
    c_out = rc("c", 0, cot_h, cpair.at[1], to_sib)
    for item in loads:
        item.start()

    barrier = pltpu.get_barrier_semaphore()

    def greet(to):
        pl.semaphore_signal(barrier, inc=1, device_id=to, device_id_type=MESH)

    for to in (to_sib, to_x, to_y, sm.to_z):
        greet(to)

    @pl.when(sm.mid)
    def _():
        greet(sm.to_mid)

    loads[0].wait()
    tile = 64

    def norm_one(i):
        r = pl.ds(pl.multiple_of(i * tile, tile), tile)
        n1, _ = normed(tok[r, :].astype(f32))
        hid[r, :] = (n1 * again[...] + ashift[...]).astype(bf16)

    loop(rows // tile, norm_one, True)

    @pl.when(sm.mid)
    def _():
        pl.semaphore_wait(barrier, 5)

    @pl.when(sm.outer)
    def _():
        pl.semaphore_wait(barrier, 4)

    w_out.start()
    c_out.start()
    loads[1].wait()
    heads_w = q.shape[1]
    lane = lax.broadcasted_iota(jnp.int32, (1, 128), 1)

    def half_of(value, e):
        keep = (lane < 64) if e == 0 else (lane >= 64)
        return jnp.where(keep, value.astype(f32), 0.0).astype(bf16)

    end0 = clip[0, 0]
    end1 = end0 + clip[0, 1]
    end2 = end1 + clip[0, 2]

    def seg_of(index):
        one = lambda e: (index >= e).astype(jnp.int32)
        return one(end0) + one(end1) + one(end2)

    key_seg = seg_of(lax.broadcasted_iota(jnp.int32, (1, rows), 1))
    def same_clip(at, count):
        return seg_of(lax.broadcasted_iota(jnp.int32, (count, 1), 0) + at) == key_seg

    def softmax(products, same):
        s = jnp.where(same, products, -1e30)
        w = jnp.exp(s - jnp.max(s, axis=1, keepdims=True))
        return w * (1.0 / jnp.sum(w, axis=1, keepdims=True))

    def make_qkv(g):
        c4 = cols(g, 256)
        h = hid[...]
        q[:, c4] = ((mm(h, wqkv[0, :, c4]) + qvb[pl.ds(0, 1), c4]).astype(bf16) * 0.125).astype(bf16)
        k[:, c4] = mm(h, wqkv[1, :, c4]).astype(bf16)
        v[:, c4] = (mm(h, wqkv[2, :, c4]) + qvb[pl.ds(1, 1), c4]).astype(bf16)

    def o_send(pr):
        return rc("o", pr, o_own.at[:, cols(pr)], o_peer.at[:, cols(pr)], to_x)

    def osib_send(pr):
        m = lax.rem(pr, 2)
        return rc("osib", m, o_own.at[:, cols(pr)], o_sib.at[:, cols(m)], to_sib)

    def attend(pr):
        c2 = cols(pr)
        keys = k[:, c2]
        values = [half_of(v[:, c2], e) for e in range(2)]
        for at in range(0, rows, 256):
            r = pl.ds(at, 256)
            same = same_clip(at, 256)
            total = None
            for e in range(2):
                p = softmax(mm_nt(half_of(q[r, c2], e), keys), same)
                term = mm(p.astype(bf16), values[e])
                total = term if total is None else total + term
            o_own[r, c2] = total.astype(bf16)
        o_send(pr).start()

        @pl.when(pr // 2 == 1 - core)
        def _():
            osib_send(pr).start()

    def group_of_heads(g):
        make_qkv(g)
        attend(2 * g)
        attend(2 * g + 1)

    loop(heads_w // 256, group_of_heads)

    w_in.wait_recv()
    w_y.start()
    w_s0.start()
    loads[2].wait()
    nrow = 128

    def own_part(i):
        r = pl.ds(pl.multiple_of(i * nrow, nrow), nrow)
        y1[r, :] = mm(o_own[r, :], wout[t])

    loop(rows // nrow, own_part, True)
    w_y.wait_recv()
    w_s1.start()
    w_s0.wait_recv()
    w_s1.wait_recv()
    w_y.wait_send()
    w_s0.wait_send()
    w_s1.wait_send()
    for pr in range(4):
        o_send(pr).wait_recv()

    def peer_part(i):
        r = pl.ds(pl.multiple_of(i * nrow, nrow), nrow)
        dy1[r, :] = mm(o_peer[r, :], wout[1 - t])

    loop(rows // nrow, peer_part, True)

    def h2t_send(i):
        return rc("h2t", i, h2t.at[0, :, cols(i, nrow)], h2t.at[1, :, cols(i, nrow)], to_sib)

    def norm_two(i):
        r = pl.ds(pl.multiple_of(i * nrow, nrow), nrow)
        x = tok[r, :].astype(f32)
        y = x + (y1[r, :] + dy1[r, :]) + outb[...]
        y1[r, :] = y
        n2, _ = normed(y)
        h2 = (n2 * mgain[...] + mshift[...]).astype(bf16)
        hid_two[r, :] = h2
        h2t[0, :, cols(i, nrow)] = h2.T
        h2t_send(i).start()

    hid_two = xs1
    loop(rows // nrow, norm_two, True)

    loads[3].wait()
    loads[4].wait()
    loads[5].wait()
    c_out.wait_recv()

    def act_send(j):
        c4 = cols(2 * j + 1 - core, 256)
        return rc("act", j, act.at[:, c4], act_sib.at[j], to_sib)

    def pre_send(j):
        c4 = cols(2 * j + 1 - core, 256)
        return rc("pre", j, pre.at[:, c4], pre_sib.at[j], to_sib)

    def hidden(piece):
        c4 = cols(piece, 256)
        a, d = gelu_parts(mm(hid_two[...], wup[:, c4]) + upb[:, c4])
        du = (mm_nt(cpair[0], wdown[c4, :]) * d).astype(bf16)
        act[:, c4] = a.astype(bf16)
        pre[:, c4] = du
        total = split_rows(du.astype(f32))
        row = 6 + piece // 4
        small[pl.ds(row, 1), cols(lax.rem(piece, 4), 256)] = jnp.sum(total, axis=0, keepdims=True)

    def hidden_pair(j):
        hidden(2 * j + 1 - core)
        act_send(j).start()
        pre_send(j).start()
        hidden(2 * j + core)

    def chunk(j):
        mine = cols(2 * j + core, 256)
        act_send(j).wait_recv()
        for n in range(2):
            wide = pl.ds(n * 512, 512)
            block = mm_tn(act[:, mine], cpair[0, :, wide]) + mm_tn(act_sib[j], cpair[1, :, wide])
            low = block.astype(bf16)
            loc_a[4 * j + 2 * n] = low[:, :256]
            loc_a[4 * j + 2 * n + 1] = low[:, 256:]
        pre_send(j).wait_recv()
        for m in range(2):
            high = pl.ds(m * 512, 512)
            low = (mm(h2t[0, high, :], pre[:, mine]) + mm(h2t[1, high, :], pre_sib[j])).astype(bf16)
            loc_b[4 * j + 2 * m] = low[:256]
            loc_b[4 * j + 2 * m + 1] = low[256:]

    for i in range(4):
        h2t_send(i).wait_recv()
    hidden_pair(0)
    chunk(0)
    for j in range(1, 4):
        sm.step(j - 1)
        hidden_pair(j)
    sm.step(3)

    def x_send(name, n, src, dst):
        return rc(name, n, src.at[:, cols(n, 256)], dst.at[:, cols(n, 256)], to_x)

    def back_two(n):
        xs0[:, cols(n, 256)] = mm_nt(pre[...], wup[cols(n, 256), :]).astype(bf16)
        x_send("x0", n, xs0, xr0).start()

    loop(width // 256, back_two)
    chunk(1)
    sm.step(4)

    def forward_two(n):
        xs1[:, cols(n, 256)] = mm(act[...], wdown[:, cols(n, 256)]).astype(bf16)
        x_send("x1", n, xs1, xr1).start()

    loop(width // 256, forward_two)
    sm.step(5)
    chunk(2)
    sm.step(6)
    chunk(3)
    sm.step(7)

    for i in range(4):
        h2t_send(i).wait_send()
    h1t = h2t

    def turn_first(i):
        r = pl.ds(pl.multiple_of(i * nrow, nrow), nrow)
        h1t[0, :, cols(i, nrow)] = hid[r, :].T

    loop(rows // nrow, turn_first, True)
    h1t_out = rc("h1t", 0, h1t.at[0], h1t.at[1], to_sib)

    def cot_sum(i, total):
        r = pl.ds(pl.multiple_of(i * tile, tile), tile)
        return total + split_rows(cpair[0, r, :].astype(f32))

    total = lax.fori_loop(0, rows // tile, cot_sum, jnp.zeros((8, width), f32), unroll=True)
    small[pl.ds(8, 1), :] = jnp.sum(total, axis=0, keepdims=True)
    sm.steps(8, 10)

    for n in range(4):
        x_send("x0", n, xs0, xr0).wait_recv()
    sums[...] = jnp.zeros_like(sums)
    back = 128
    dyb = xr0

    def norm_two_back(i):
        r = pl.ds(pl.multiple_of(i * back, back), back)
        g = xs0[r, :].astype(f32) + xr0[r, :].astype(f32)
        n2, r2 = normed(y1[r, :])
        gn = g * n2
        sums[0] += split_rows(gn)
        sums[1] += split_rows(g)
        e2 = g * mgain[...]
        m1 = jnp.mean(e2, axis=-1, keepdims=True)
        m2 = jnp.mean(e2 * n2, axis=-1, keepdims=True)
        d = cpair[0, r, :].astype(f32) + r2 * (e2 - m1 - n2 * m2)
        sums[2] += split_rows(d)
        dy1[r, :] = d
        dyb[r, :] = d.astype(bf16)

    loop(rows // back, norm_two_back)
    dyb_out = rc("dyb", 0, dyb, wout.at[1 - t], to_sib)
    dyb_out.start()
    for i, row in enumerate((4, 5, 3)):
        small[pl.ds(row, 1), :] = jnp.sum(sums[i], axis=0, keepdims=True)
    for n in range(4):
        x_send("x0", n, xs0, xr0).wait_send()

    def back_heads(n):
        dob[:, cols(n, 256)] = mm_nt(dyb[...], wout[t, cols(n, 256), :]).astype(bf16)

    sm.step(10)
    loop(heads_w // 256, back_heads)
    osib_send(0).wait_recv()
    osib_send(1).wait_recv()
    dyb_out.wait_recv()
    h1t_out.start()
    for n in range(width // 512):
        wide = pl.ds(n * 512, 512)
        low = (
            mm_tn(o_own[:, cols(core, 256)], dyb[:, wide]) + mm_tn(o_sib[...], wout[1 - t, :, wide])
        ).astype(bf16)
        loc_a[16 + 2 * n] = low[:, :256]
        loc_a[17 + 2 * n] = low[:, 256:]

    sm.step(11)

    def dqkv_send(w, m, src, pr):
        return rc("dqkv", 2 * w + m, src.at[:, cols(pr)], act_sib.at[w, :, cols(m)], to_sib)

    def attend_back(pr):
        c2 = cols(pr)
        same = same_clip(0, rows)
        dq = dk = dv = None
        for e in range(2):
            q_e, do_e = half_of(q[:, c2], e), half_of(dob[:, c2], e)
            p = softmax(mm_nt(q_e, k[:, c2]), same)
            dp = mm_nt(do_e, v[:, c2])
            ds = (p * (dp - jnp.sum(p * dp, axis=1, keepdims=True))).astype(bf16)
            terms = (
                mm(ds, half_of(k[:, c2], e)) * 0.125,
                mm_tn(ds, q_e),
                mm_tn(p.astype(bf16), do_e),
            )
            dq, dk, dv = terms if dq is None else (dq + terms[0], dk + terms[1], dv + terms[2])
        q[:, c2] = dq.astype(bf16)
        k[:, c2] = dk.astype(bf16)
        v[:, c2] = dv.astype(bf16)
        small[pl.ds(2, 1), c2] = jnp.sum(q[:, c2].astype(f32), axis=0, keepdims=True)
        small[pl.ds(2, 1), cols(pr + 4)] = jnp.sum(v[:, c2].astype(f32), axis=0, keepdims=True)

    def theirs(m):
        pr = 2 * (1 - core) + m
        attend_back(pr)
        for w, src in enumerate((q, k, v)):
            dqkv_send(w, m, src, pr).start()

    loop(2, theirs)
    sm.step(12)

    def ours(m):
        attend_back(2 * core + m)

    loop(2, ours)
    sm.step(13)
    h1t_out.wait_recv()
    for w, src in enumerate((q, k, v)):
        for m in range(2):
            dqkv_send(w, m, src, m).wait_recv()
        for m in range(4):
            high = pl.ds(m * 256, 256)
            low = mm(h1t[0, high, :], src[:, cols(core, 256)]) + mm(h1t[1, high, :], act_sib[w])
            at = 3 * m + w
            if at < 4:
                loc_a[20 + at] = low.astype(bf16)
            else:
                loc_b[12 + at] = low.astype(bf16)
    sm.step(14)

    last = wup.at[pl.ds(0, rows), pl.ds(0, width)]

    def back_one(n):
        c4 = cols(n, 256)
        xs0[:, c4] = (
            mm_nt(q[...], wqkv[0, c4, :]) + mm_nt(k[...], wqkv[1, c4, :]) + mm_nt(v[...], wqkv[2, c4, :])
        ).astype(bf16)
        x_send("x2", n, xs0, last).start()

    loop(width // 256, back_one)
    sm.steps(15, 18)

    for n in range(4):
        x_send("x1", n, xs1, xr1).wait_recv()

    def finish(i):
        r = pl.ds(pl.multiple_of(i * tile, tile), tile)
        hid[r, :] = (
            y1[r, :] + (xs1[r, :].astype(f32) + xr1[r, :].astype(f32)) + downb[...]
        ).astype(bf16)

    loop(rows // tile, finish, True)
    lo_out = load(6, hid, lo_h)
    lo_out.start()

    sm.steps(18, 27)
    for n in range(4):
        x_send("x2", n, xs0, last).wait_recv()
    sums[...] = jnp.zeros_like(sums)

    def norm_one_back(i):
        r = pl.ds(pl.multiple_of(i * back, back), back)
        g = xs0[r, :].astype(f32) + last[r, :].astype(f32)
        n1, r1 = normed(tok[r, :].astype(f32))
        gn = g * n1
        sums[0] += split_rows(gn)
        sums[1] += split_rows(g)
        e1 = g * again[...]
        m1 = jnp.mean(e1, axis=-1, keepdims=True)
        m2 = jnp.mean(e1 * n1, axis=-1, keepdims=True)
        tok[r, :] = (dy1[r, :] + r1 * (e1 - m1 - n1 * m2)).astype(bf16)

    loop(rows // back, norm_one_back)
    gt_out = load(7, tok, gt_h)
    gt_out.start()
    for i, row in enumerate((0, 1)):
        small[pl.ds(row, 1), :] = jnp.sum(sums[i], axis=0, keepdims=True)

    def small_rc(i, src, to):
        return rc("small", i, src, small_r.at[i], to)

    small_sib = small_rc(0, small, to_sib)
    small_y = small_rc(1, small_r.at[0], to_y)
    small_in = small_rc(2, small_r.at[1], sm.to_z)
    small_mid = small_rc(3, small_r.at[2], sm.to_mid)
    small_out = small_rc(4, small_r.at[3], sm.to_z)
    small_sib.start()
    sm.step(27)
    small_sib.wait_recv()
    small_r[0] += small[...]
    small_y.start()
    sm.step(28)
    small_y.wait_recv()
    small_r[1] += small_r[0]

    @pl.when(sm.outer)
    def _():
        small_in.start()

    sm.step(29)

    @pl.when(sm.mid)
    def _():
        small_in.wait_recv()
        small_r[2] += small_r[1]
        small_mid.start()

    sm.step(30)

    @pl.when(sm.mid)
    def _():
        small_mid.wait_recv()
        small_r[3] += small_r[2]
        small_out.start()

    sm.steps(31, END)

    @pl.when(sm.outer)
    def _():
        small_out.wait_recv()

    keep = load(8, small_r.at[jnp.where(sm.outer, 4, 3)], small_h)
    keep.start()

    sm.end()
    w_out.wait_send()
    c_out.wait_send()
    h1t_out.wait_send()
    dyb_out.wait_send()
    for i in range(4):
        o_send(i).wait_send()
        act_send(i).wait_send()
        pre_send(i).wait_send()
        x_send("x1", i, xs1, xr1).wait_send()
        x_send("x2", i, xs0, last).wait_send()
    for m in range(2):
        osib_send(m).wait_send()
        for w, src in enumerate((q, k, v)):
            dqkv_send(w, m, src, m).wait_send()
    small_sib.wait_send()
    small_y.wait_send()

    @pl.when(sm.outer)
    def _():
        small_in.wait_send()

    @pl.when(sm.mid)
    def _():
        small_mid.wait_send()
        small_out.wait_send()

    lo_out.wait()
    gt_out.wait()
    keep.wait()


def layer(clip, vectors, tokens, wqkv, wout, wup, wdown, cot):
    rows, width = tokens.shape
    heads_w = wqkv.shape[2]
    hidden = wup.shape[1]
    big = pl.BlockSpec(memory_space=pl.ANY)
    small = pl.BlockSpec(memory_space=pltpu.VMEM)
    vm = lambda *shape: pltpu.VMEM(shape, bf16)
    vf = lambda *shape: pltpu.VMEM(shape, f32)
    return pl.pallas_call(
        layer_kernel,
        out_shape=(
            jax.ShapeDtypeStruct((rows, width), bf16),
            jax.ShapeDtypeStruct((rows, width), bf16),
            jax.ShapeDtypeStruct((2 * CHUNKS, 2, SIDE, SIDE), bf16),
            jax.ShapeDtypeStruct((16, width), f32),
        ),
        in_specs=[pl.BlockSpec(memory_space=pltpu.SMEM)] + [small] * len(vectors) + [big] * 6,
        out_specs=[big] * 4,
        scratch_shapes=[
            vm(rows, width),
            vm(*wqkv.shape),
            vm(2, *wout.shape),
            vm(*wup.shape),
            vm(*wdown.shape),
            vm(2, rows, width),
            vm(rows, width),
            vm(rows, heads_w),
            vm(rows, heads_w),
            vm(rows, heads_w),
            vm(rows, heads_w),
            vm(rows, heads_w),
            vm(rows, 256),
            vf(rows, width),
            vm(2, width, rows),
            vm(rows, hidden),
            vm(rows, hidden),
            vm(4, rows, 256),
            vm(4, rows, 256),
            vm(rows, width),
            vm(rows, width),
            vm(rows, width),
            vm(rows, width),
            vf(rows, width),
            vm(rows, heads_w),
            vf(16, width),
            vf(5, 16, width),
            vf(3, 8, width),
        ]
        + scratch_of(CHUNKS, SIDE)
        + [
            pltpu.SemaphoreType.DMA((9,)),
            pltpu.SemaphoreType.DMA((N_LINKS,)),
            pltpu.SemaphoreType.DMA((N_LINKS,)),
        ],
        compiler_params=pltpu.CompilerParams(
            has_side_effects=True, collective_id=0, vmem_limit_bytes=VMEM_BYTES
        ),
        name="layer",
    )(clip, *vectors, tokens, wqkv, wout, wup, wdown, cot)


VMEM_BYTES = 60 << 20


STEPS = 8


def widen_kernel(
    down_in, up_in, out_in, qkv_in, s_in, lo_in, gt_in,
    lo, gt, down, out, up, qkv, ag, ash, qv, ob, mg, ms, ub, db,
):
    lo[...] = lo_in[...]
    gt[...] = gt_in[...]
    for n in range(4):
        c = pl.ds(n * SIDE, SIDE)
        down[:, c] = down_in[n, 0].astype(f32)
        out[:, c] = out_in[n, 0].astype(f32)
        up[c, :] = up_in[n, 0].astype(f32)
    for w in range(3):
        for core in range(2):
            qkv[w, :, pl.ds(core * SIDE, SIDE)] = qkv_in[w, core].astype(f32)

    @pl.when(pl.program_id(0) == STEPS - 1)
    def _():
        for ref, row in ((ag, 0), (ash, 1), (ob, 3), (mg, 4), (ms, 5), (db, 8)):
            ref[...] = s_in[pl.ds(row, 1), :]
        qv[pl.ds(0, 1), :] = s_in[pl.ds(2, 1), pl.ds(0, 512)]
        qv[pl.ds(1, 1), :] = s_in[pl.ds(2, 1), pl.ds(512, 512)]
        ub[:, pl.ds(0, 1024)] = s_in[pl.ds(6, 1), :]
        ub[:, pl.ds(1024, 1024)] = s_in[pl.ds(7, 1), :]


def widen(sums, small, lo, gt):
    whole = lambda *shape: pl.BlockSpec(shape, lambda i: (0,) * len(shape))
    rows_in = pl.BlockSpec((lo.shape[0] // STEPS, lo.shape[1]), lambda i: (i, 0))
    vectors = ((1, 1024), (1, 1024), (2, 512), (1, 1024), (1, 1024), (1, 1024), (1, 2048), (1, 1024))
    got = pl.pallas_call(
        widen_kernel,
        grid=(STEPS,),
        in_specs=[
            pl.BlockSpec((4, 1, SIDE, SIDE), lambda i: (i // 2, i % 2, 0, 0)),
            pl.BlockSpec((4, 1, SIDE, SIDE), lambda i: (4 + i // 2, i % 2, 0, 0)),
            pl.BlockSpec((4, 1, SIDE // 4, SIDE), lambda i: (8, i // 4, i % 4, 0)),
            pl.BlockSpec((3, 2, SIDE // 2, SIDE), lambda i: (12 + i // 2, 0, i % 2, 0)),
            whole(16, 1024),
            rows_in,
            rows_in,
        ],
        out_specs=[
            rows_in,
            rows_in,
            pl.BlockSpec((SIDE, 1024), lambda i: (i, 0)),
            pl.BlockSpec((SIDE // 4, 1024), lambda i: (i, 0)),
            pl.BlockSpec((1024, SIDE), lambda i: (0, i)),
            pl.BlockSpec((3, SIDE // 2, 512), lambda i: (0, i, 0)),
        ]
        + [whole(*shape) for shape in vectors],
        out_shape=[
            jax.ShapeDtypeStruct(lo.shape, bf16),
            jax.ShapeDtypeStruct(gt.shape, bf16),
            jax.ShapeDtypeStruct((2048, 1024), f32),
            jax.ShapeDtypeStruct((512, 1024), f32),
            jax.ShapeDtypeStruct((1024, 2048), f32),
            jax.ShapeDtypeStruct((3, 1024, 512), f32),
        ]
        + [jax.ShapeDtypeStruct(shape, f32) for shape in vectors],
        compiler_params=pltpu.CompilerParams(vmem_limit_bytes=56 << 20),
        name="widen",
    )(sums, sums, sums, sums, small, lo, gt)
    lo, gt, down, out, up, qkv, ag, ash, qv, ob, mg, ms, ub, db = got
    flat = lambda v: v.reshape(-1)
    return (
        lo, gt, flat(ag), flat(ash), qkv, qv, out, flat(ob), flat(mg), flat(ms), up, flat(ub),
        down, flat(db),
    )


def local(
    tokens, clip_lengths, attn_gain, attn_shift, qkv_weight, qv_bias, out_weight, out_bias,
    mlp_gain, mlp_shift, up_weight, up_bias, down_weight, down_bias, cotangent,
):
    row = lambda v: v.reshape(1, -1)
    vectors = (
        row(attn_gain), row(attn_shift), qv_bias, row(out_bias), row(mlp_gain), row(mlp_shift),
        row(up_bias), row(down_bias),
    )
    layer_output, grad_tokens, sums, small = layer(
        clip_lengths, vectors, tokens, qkv_weight, out_weight, up_weight, down_weight, cotangent
    )
    groups = lax.axis_size("dp")
    if groups > CELL:
        cells = [[k * CELL + i for k in range(groups // CELL)] for i in range(CELL)]
        sums, small = lax.psum((sums.astype(f32), small), "dp", axis_index_groups=cells)
    return widen(sums, small, layer_output, grad_tokens)


def solution(mesh):
    placed = (
        P("dp", None), P("dp", None), P(), P(), P(None, None, "tensor"), P(None, "tensor"),
        P("tensor", None), P(), P(), P(), P(None, "tensor"), P("tensor"), P("tensor", None), P(),
        P("dp", None),
    )
    return jax.shard_map(
        local,
        mesh=mesh,
        in_specs=placed,
        out_specs=(
            P("dp", None), P("dp", None), P(), P(), P(None, None, "tensor"), P(None, "tensor"),
            P("tensor", None), P(), P(), P(), P(None, "tensor"), P("tensor"), P("tensor", None), P(),
        ),
        check_vma=False,
    )
```

```python
import jax
import jax.numpy as jnp
from jax import lax
from jax.experimental import pallas as pl
from jax.experimental.pallas import tpu as pltpu
from jax.sharding import PartitionSpec as P

MESH = pl.DeviceIdType.MESH
bf16, f32 = jnp.bfloat16, jnp.float32
CELL = 16
LAGS = (0, 2, 4, 6, 8, 10)
LAST = LAGS[-1] + 2
STAGES = len(LAGS)
SIDE = 256
N_DOWN = N_UP = 16
CHUNKS = 24
END = CHUNKS + LAGS[-1]


def pick(low, first, second):
    if isinstance(low, bool):
        return first if low else second
    return jnp.where(low, first, second)


def place_a(i):
    return pick(i < N_DOWN, i, i + N_UP)


def place_b(i):
    return pick(i < N_UP, i + N_DOWN, i + CHUNKS)


def place():
    at = lax.axis_index("dp")
    base = (at // CELL) * CELL
    inner = at - base
    z = inner // 4
    y = (inner // 2) % 2
    core = inner % 2
    return base, z, y, core


class Summer:
    def __init__(self, loc_a, loc_b, bufs, out, sems):
        self.loc_a, self.loc_b = loc_a, loc_b
        (self.a1, self.a2, self.a3, self.b1, self.b2, self.b3) = bufs
        self.out = out
        self.as_, self.ar_, self.bs_, self.br_, self.ls_ = sems
        self.ha = loc_a.shape[1] // 2
        self.hb = loc_b.shape[1] // 2
        base, z, y, core = place()
        self.y, self.core = y, core
        self.outer = jnp.logical_or(z == 0, z == 3)
        self.mid = jnp.logical_not(self.outer)
        self.mine = jnp.where(z >= 2, 1, 0)
        across = 3 - z
        toward = jnp.where(z < 2, 1 - z, 5 - z)
        tensor = lax.axis_index("tensor")

        def dev(zz, yy, cc):
            return (base + zz * 4 + yy * 2 + cc, tensor)

        self.to_sib = dev(z, y, 1 - core)
        self.to_y = dev(z, 1 - y, core)
        self.to_mid = dev(across, y, core)
        self.to_z = dev(toward, y, core)

    def la(self, i, h):
        return self.loc_a.at[i, pl.ds(pl.multiple_of(h * self.ha, self.ha), self.ha), :]

    def lb(self, i, h):
        return self.loc_b.at[i, pl.ds(pl.multiple_of(h * self.hb, self.hb), self.hb), :]

    def oa(self, i, h, core):
        return self.out.at[
            place_a(i), core, pl.ds(pl.multiple_of(h * self.ha, self.ha), self.ha), :
        ]

    def ob(self, i, h, core):
        return self.out.at[
            place_b(i), core, pl.ds(pl.multiple_of(h * self.hb, self.hb), self.hb), :
        ]

    def ca(self, i, kind, recv, src, dst, to):
        return pltpu.make_async_remote_copy(
            src, dst, self.as_.at[i, kind], self.ar_.at[i, recv], device_id=to, device_id_type=MESH
        )

    def cb(self, i, kind, recv, src, dst, to):
        return pltpu.make_async_remote_copy(
            src, dst, self.bs_.at[i, kind], self.br_.at[i, recv], device_id=to, device_id_type=MESH
        )

    def a_y(self, i):
        return self.ca(i, 0, 0, self.la(i, 1 - self.y), self.a1.at[i], self.to_y)

    def a_in(self, i):
        return self.ca(i, 1, 1, self.la(i, self.y), self.a2.at[i], self.to_z)

    def a_mid(self, i):
        return self.ca(i, 1, 2, self.la(i, self.y), self.a3.at[i], self.to_mid)

    def a_out(self, i):
        return self.ca(i, 2, 3, self.a2.at[i], self.oa(i, self.y, self.core), self.to_z)

    def a_done(self, i, kind, recv, src, to):
        return self.ca(i, kind, recv, src, self.oa(i, self.y, self.core), to)

    def a_keep(self, i):
        return pltpu.make_async_copy(self.a2.at[i], self.oa(i, self.y, self.core), self.ls_.at[0, i])

    def a_fwd(self, i):
        o = self.oa(i, 1 - self.y, self.core)
        return self.ca(i, 5, 6, o, o, self.to_sib)

    def step_a(self, i, stage):
        y = self.y
        if stage == 0:
            self.a_y(i).start()
        elif stage == 1:
            self.a_y(i).wait_recv()
            v = self.la(i, y)
            v[...] = (v[...].astype(f32) + self.a1[i].astype(f32)).astype(bf16)

            @pl.when(self.outer)
            def _():
                self.a_in(i).start()
        elif stage == 2:
            @pl.when(self.mid)
            def _():
                self.a_in(i).wait_recv()
                v = self.la(i, y)
                v[...] = (v[...].astype(f32) + self.a2[i].astype(f32)).astype(bf16)
                self.a_mid(i).start()
        elif stage == 3:
            @pl.when(self.mid)
            def _():
                self.a_mid(i).wait_recv()
                self.a2[i] = (self.la(i, y)[...].astype(f32) + self.a3[i].astype(f32)).astype(bf16)
                self.a_out(i).start()
                src = self.a2.at[i]
                self.a_done(i, 3, 4, src, self.to_y).start()
                self.a_done(i, 4, 5, src, self.to_sib).start()
                self.a_keep(i).start()
        elif stage == 4:
            @pl.when(self.outer)
            def _():
                self.a_out(i).wait_recv()
                src = self.oa(i, y, self.core)
                self.a_done(i, 3, 4, src, self.to_y).start()
                self.a_done(i, 4, 5, src, self.to_sib).start()
        elif stage == 5:
            self.a_done(i, 3, 4, self.oa(i, y, self.core), self.to_y).wait_recv()
            self.a_fwd(i).start()

    def end_a(self, i):
        src = self.a2.at[i]
        self.a_y(i).wait_send()
        self.a_in(i).wait_send()

        @pl.when(self.mid)
        def _():
            self.a_out(i).wait_send()
            self.a_keep(i).wait()

        self.a_done(i, 3, 4, src, self.to_y).wait_send()
        self.a_done(i, 4, 5, src, self.to_sib).wait_send()
        self.a_fwd(i).wait_send()
        self.a_done(i, 4, 5, src, self.to_sib).wait_recv()
        self.a_fwd(i).wait_recv()

    def b_in(self, i):
        return self.cb(i, 0, 0, self.loc_b.at[i], self.b1.at[i], self.to_z)

    def b_mid(self, i):
        return self.cb(i, 0, 1, self.lb(i, 1 - self.mine), self.b2.at[i], self.to_mid)

    def b_y(self, i):
        return self.cb(i, 1, 2, self.lb(i, self.mine), self.b3.at[i], self.to_y)

    def fin_b(self, i):
        return self.b1.at[i, pl.ds(0, self.hb), :]

    def b_done(self, i, kind, recv, src, h, to):
        return self.cb(i, kind, recv, src, self.ob(i, h, self.core), to)

    def b_keep(self, i):
        return pltpu.make_async_copy(
            self.fin_b(i), self.ob(i, self.mine, self.core), self.ls_.at[1, i]
        )

    def step_b(self, i, stage):
        mine, core = self.mine, self.core
        if stage == 0:
            @pl.when(self.outer)
            def _():
                self.b_in(i).start()
        elif stage == 1:
            @pl.when(self.mid)
            def _():
                self.b_in(i).wait_recv()
                self.loc_b[i] = (self.loc_b[i].astype(f32) + self.b1[i].astype(f32)).astype(bf16)
                self.b_mid(i).start()
        elif stage == 2:
            @pl.when(self.mid)
            def _():
                self.b_mid(i).wait_recv()
                v = self.lb(i, mine)
                v[...] = (v[...].astype(f32) + self.b2[i].astype(f32)).astype(bf16)
                self.b_y(i).start()
        elif stage == 3:
            @pl.when(self.mid)
            def _():
                self.b_y(i).wait_recv()
                fin = self.fin_b(i)
                fin[...] = (self.lb(i, mine)[...].astype(f32) + self.b3[i].astype(f32)).astype(bf16)
                self.b_done(i, 2, 4, fin, mine, self.to_mid).start()
                self.b_done(i, 3, 3, fin, mine, self.to_z).start()
                self.b_done(i, 4, 5, fin, mine, self.to_sib).start()
                self.b_keep(i).start()
        elif stage == 4:
            @pl.when(self.mid)
            def _():
                o = self.ob(i, 1 - mine, core)
                self.b_done(i, 2, 4, o, 1 - mine, self.to_mid).wait_recv()
                self.b_done(i, 5, 4, o, 1 - mine, self.to_z).start()
                self.b_done(i, 6, 6, o, 1 - mine, self.to_sib).start()

            @pl.when(self.outer)
            def _():
                o = self.ob(i, mine, core)
                self.b_done(i, 3, 3, o, mine, self.to_z).wait_recv()
                self.b_done(i, 4, 5, o, mine, self.to_sib).start()
        elif stage == 5:
            @pl.when(self.outer)
            def _():
                o = self.ob(i, 1 - mine, core)
                self.b_done(i, 5, 4, o, 1 - mine, self.to_z).wait_recv()
                self.b_done(i, 6, 6, o, 1 - mine, self.to_sib).start()

    def end_b(self, i):
        fin = self.fin_b(i)
        mine = self.mine

        @pl.when(self.outer)
        def _():
            self.b_in(i).wait_send()

        @pl.when(self.mid)
        def _():
            self.b_mid(i).wait_send()
            self.b_y(i).wait_send()
            self.b_done(i, 2, 4, fin, mine, self.to_mid).wait_send()
            self.b_done(i, 3, 3, fin, mine, self.to_z).wait_send()
            self.b_done(i, 5, 4, fin, mine, self.to_z).wait_send()
            self.b_keep(i).wait()

        self.b_done(i, 4, 5, fin, mine, self.to_sib).wait_send()
        self.b_done(i, 6, 6, fin, mine, self.to_sib).wait_send()
        self.b_done(i, 4, 5, fin, mine, self.to_sib).wait_recv()
        self.b_done(i, 6, 6, fin, mine, self.to_sib).wait_recv()

    def step(self, t):
        for stage in range(STAGES + 1):
            i = t - (*LAGS, LAST)[stage]

            def run():
                if stage < STAGES:
                    self.step_a(i, stage)
                    self.step_b(i, stage)
                else:
                    self.end_a(i)
                    self.end_b(i)

            if not isinstance(t, int):
                pl.when(jnp.logical_and(i >= 0, i < CHUNKS))(run)
            elif 0 <= i < CHUNKS:
                run()

    def steps(self, lo, hi):
        def body(t, _):
            self.step(t)
            return 0

        lax.fori_loop(lo, hi, body, 0)

    def end(self):
        def body(i, _):
            self.end_a(i)
            self.end_b(i)
            return 0

        lax.fori_loop(END - LAST, CHUNKS, body, 0)


def scratch_of(n, side):
    whole, half = pltpu.VMEM((n, side, side), bf16), pltpu.VMEM((n, side // 2, side), bf16)
    return [
        whole,
        whole,
        half,
        half,
        half,
        whole,
        half,
        half,
        pltpu.SemaphoreType.DMA((n, 6)),
        pltpu.SemaphoreType.DMA((n, 7)),
        pltpu.SemaphoreType.DMA((n, 7)),
        pltpu.SemaphoreType.DMA((n, 7)),
        pltpu.SemaphoreType.DMA((2, n)),
    ]


def split_rows(value):
    rows, cols = value.shape
    return jnp.sum(value.reshape(rows // 8, 8, cols), axis=0)


def erf(value):
    x = jnp.clip(value, -4.0, 4.0)
    x2 = x * x
    top = -2.72614225801306e-10
    for c in (
        2.77068142495902e-08,
        -2.10102402082508e-06,
        -5.69250639462346e-05,
        -7.34990630326855e-04,
        -2.95459980854025e-03,
        -1.60960333262415e-02,
    ):
        top = top * x2 + c
    low = -1.45660718464996e-05
    for c in (
        -2.13374055278905e-04,
        -1.68282697438203e-03,
        -7.37332916720468e-03,
        -1.42647390514189e-02,
    ):
        low = low * x2 + c
    return x * top / low


def gelu_parts(u):
    cdf = 0.5 * (1.0 + erf(u * 0.7071067811865476))
    pdf = jnp.exp(-0.5 * u * u) * 0.3989422804014327
    return u * cdf, cdf + u * pdf


def normed(rows_in):
    centred = rows_in - jnp.mean(rows_in, axis=-1, keepdims=True)
    scale = lax.rsqrt(jnp.mean(centred * centred, axis=-1, keepdims=True) + 1e-06)
    return centred * scale, scale


def mm(left, right):
    return jnp.dot(left, right, preferred_element_type=f32)


def mm_tn(left, right):
    return lax.dot_general(left, right, (((0,), (0,)), ((), ())), preferred_element_type=f32)


def mm_nt(left, right):
    return lax.dot_general(left, right, (((1,), (1,)), ((), ())), preferred_element_type=f32)


LINKS = {
    "w": 4, "c": 1, "o": 4, "osib": 2, "h2t": 4, "act": 4, "pre": 4, "x0": 4, "x1": 4, "x2": 4,
    "dyb": 1, "h1t": 1, "dqkv": 6, "small": 5,
}
LINK_AT = {}
for _name, _count in LINKS.items():
    LINK_AT[_name] = sum(LINKS[n] for n in LINK_AT)
N_LINKS = sum(LINKS.values())


def layer_kernel(
    clip, again, ashift, qvb, outb, mgain, mshift, upb, downb,
    tok_h, wqkv_h, wout_h, wup_h, wdown_h, cot_h,
    lo_h, gt_h, out, small_h,
    tok, wqkv, wout, wup, wdown, cpair, hid, q, k, v, o_own, o_peer, o_sib, y1, h2t,
    act, pre, act_sib, pre_sib, xs0, xs1, xr0, xr1, dy1, dob, small, small_r, sums,
    loc_a, loc_b, a1, a2, a3, b1, b2, b3,
    as_, ar_, bs_, br_, ls_, lsem, ssem, rsem,
):
    rows = tok.shape[0]
    width = tok.shape[1]
    sm = Summer(loc_a, loc_b, (a1, a2, a3, b1, b2, b3), out, (as_, ar_, bs_, br_, ls_))
    base, z, y, core = place()
    t = lax.axis_index("tensor")
    to_x = (lax.axis_index("dp"), 1 - t)
    to_sib, to_y = sm.to_sib, sm.to_y

    def rc(name, i, src, dst, to):
        at = LINK_AT[name] + i
        return pltpu.make_async_remote_copy(
            src, dst, ssem.at[at], rsem.at[at], device_id=to, device_id_type=MESH
        )

    def cols(i, n=128):
        return pl.ds(pl.multiple_of(i * n, n), n)

    def loop(n, body, unroll=False):
        def wrapped(i, _):
            body(i)
            return 0

        lax.fori_loop(0, n, wrapped, 0, unroll=unroll)

    def load(i, src, dst):
        return pltpu.make_async_copy(src, dst, lsem.at[i])

    loads = [
        load(0, tok_h, tok),
        load(1, wqkv_h, wqkv),
        load(2, wout_h, wout.at[t]),
        load(3, wup_h, wup),
        load(4, cot_h, cpair.at[0]),
        load(5, wdown_h, wdown),
    ]
    quarter = 2 * y + core
    part = wout_h.shape[0] // 4

    def rows_of(i):
        return pl.ds(pl.multiple_of(i * part, part), part)

    def w_at(i):
        return wout.at[1 - t, rows_of(i), :]

    w_out = rc("w", 0, wout_h.at[rows_of(quarter), :], wout.at[t, rows_of(quarter), :], to_x)
    w_in = rc("w", 0, wout_h.at[rows_of(quarter), :], w_at(quarter), to_x)
    w_y = rc("w", 1, w_at(quarter), w_at(quarter), to_y)
    w_s0 = rc("w", 2, w_at(quarter), w_at(quarter), to_sib)
    other = 2 * (1 - y) + core
    w_s1 = rc("w", 3, w_at(other), w_at(other), to_sib)
    c_out = rc("c", 0, cot_h, cpair.at[1], to_sib)
    for item in loads:
        item.start()

    barrier = pltpu.get_barrier_semaphore()

    def greet(to):
        pl.semaphore_signal(barrier, inc=1, device_id=to, device_id_type=MESH)

    for to in (to_sib, to_x, to_y, sm.to_z):
        greet(to)

    @pl.when(sm.mid)
    def _():
        greet(sm.to_mid)

    loads[0].wait()
    tile = 64

    def norm_one(i):
        r = pl.ds(pl.multiple_of(i * tile, tile), tile)
        n1, _ = normed(tok[r, :].astype(f32))
        hid[r, :] = (n1 * again[...] + ashift[...]).astype(bf16)

    loop(rows // tile, norm_one, True)

    @pl.when(sm.mid)
    def _():
        pl.semaphore_wait(barrier, 5)

    @pl.when(sm.outer)
    def _():
        pl.semaphore_wait(barrier, 4)

    w_out.start()
    c_out.start()
    loads[1].wait()
    heads_w = q.shape[1]
    lane = lax.broadcasted_iota(jnp.int32, (1, 128), 1)

    def half_of(value, e):
        keep = (lane < 64) if e == 0 else (lane >= 64)
        return jnp.where(keep, value.astype(f32), 0.0).astype(bf16)

    end0 = clip[0, 0]
    end1 = end0 + clip[0, 1]
    end2 = end1 + clip[0, 2]

    def seg_of(index):
        one = lambda e: (index >= e).astype(jnp.int32)
        return one(end0) + one(end1) + one(end2)

    key_seg = seg_of(lax.broadcasted_iota(jnp.int32, (1, rows), 1))
    def same_clip(at, count):
        return seg_of(lax.broadcasted_iota(jnp.int32, (count, 1), 0) + at) == key_seg

    def softmax(products, same):
        s = jnp.where(same, products, -1e30)
        w = jnp.exp(s - jnp.max(s, axis=1, keepdims=True))
        return w * (1.0 / jnp.sum(w, axis=1, keepdims=True))

    def make_qkv(g):
        c4 = cols(g, 256)
        h = hid[...]
        q[:, c4] = ((mm(h, wqkv[0, :, c4]) + qvb[pl.ds(0, 1), c4]).astype(bf16) * 0.125).astype(bf16)
        k[:, c4] = mm(h, wqkv[1, :, c4]).astype(bf16)
        v[:, c4] = (mm(h, wqkv[2, :, c4]) + qvb[pl.ds(1, 1), c4]).astype(bf16)

    def o_send(pr):
        return rc("o", pr, o_own.at[:, cols(pr)], o_peer.at[:, cols(pr)], to_x)

    def osib_send(pr):
        m = lax.rem(pr, 2)
        return rc("osib", m, o_own.at[:, cols(pr)], o_sib.at[:, cols(m)], to_sib)

    def attend(pr):
        c2 = cols(pr)
        keys = k[:, c2]
        values = [half_of(v[:, c2], e) for e in range(2)]
        for at in range(0, rows, 256):
            r = pl.ds(at, 256)
            same = same_clip(at, 256)
            total = None
            for e in range(2):
                p = softmax(mm_nt(half_of(q[r, c2], e), keys), same)
                term = mm(p.astype(bf16), values[e])
                total = term if total is None else total + term
            o_own[r, c2] = total.astype(bf16)
        o_send(pr).start()

        @pl.when(pr // 2 == 1 - core)
        def _():
            osib_send(pr).start()

    def group_of_heads(g):
        make_qkv(g)
        attend(2 * g)
        attend(2 * g + 1)

    loop(heads_w // 256, group_of_heads)

    w_in.wait_recv()
    w_y.start()
    w_s0.start()
    loads[2].wait()
    nrow = 128

    def own_part(i):
        r = pl.ds(pl.multiple_of(i * nrow, nrow), nrow)
        y1[r, :] = mm(o_own[r, :], wout[t])

    loop(rows // nrow, own_part, True)
    w_y.wait_recv()
    w_s1.start()
    w_s0.wait_recv()
    w_s1.wait_recv()
    w_y.wait_send()
    w_s0.wait_send()
    w_s1.wait_send()
    for pr in range(4):
        o_send(pr).wait_recv()

    def peer_part(i):
        r = pl.ds(pl.multiple_of(i * nrow, nrow), nrow)
        dy1[r, :] = mm(o_peer[r, :], wout[1 - t])

    loop(rows // nrow, peer_part, True)

    def h2t_send(i):
        return rc("h2t", i, h2t.at[0, :, cols(i, nrow)], h2t.at[1, :, cols(i, nrow)], to_sib)

    def norm_two(i):
        r = pl.ds(pl.multiple_of(i * nrow, nrow), nrow)
        x = tok[r, :].astype(f32)
        y = x + (y1[r, :] + dy1[r, :]) + outb[...]
        y1[r, :] = y
        n2, _ = normed(y)
        h2 = (n2 * mgain[...] + mshift[...]).astype(bf16)
        hid_two[r, :] = h2
        h2t[0, :, cols(i, nrow)] = h2.T
        h2t_send(i).start()

    hid_two = xs1
    loop(rows // nrow, norm_two, True)

    loads[3].wait()
    loads[4].wait()
    loads[5].wait()
    c_out.wait_recv()

    def act_send(j):
        c4 = cols(2 * j + 1 - core, 256)
        return rc("act", j, act.at[:, c4], act_sib.at[j], to_sib)

    def pre_send(j):
        c4 = cols(2 * j + 1 - core, 256)
        return rc("pre", j, pre.at[:, c4], pre_sib.at[j], to_sib)

    def hidden(piece):
        c4 = cols(piece, 256)
        a, d = gelu_parts(mm(hid_two[...], wup[:, c4]) + upb[:, c4])
        du = (mm_nt(cpair[0], wdown[c4, :]) * d).astype(bf16)
        act[:, c4] = a.astype(bf16)
        pre[:, c4] = du
        total = split_rows(du.astype(f32))
        row = 6 + piece // 4
        small[pl.ds(row, 1), cols(lax.rem(piece, 4), 256)] = jnp.sum(total, axis=0, keepdims=True)

    def hidden_pair(j):
        hidden(2 * j + 1 - core)
        act_send(j).start()
        pre_send(j).start()
        hidden(2 * j + core)

    def chunk(j):
        mine = cols(2 * j + core, 256)
        act_send(j).wait_recv()
        for n in range(2):
            wide = pl.ds(n * 512, 512)
            block = mm_tn(act[:, mine], cpair[0, :, wide]) + mm_tn(act_sib[j], cpair[1, :, wide])
            low = block.astype(bf16)
            loc_a[4 * j + 2 * n] = low[:, :256]
            loc_a[4 * j + 2 * n + 1] = low[:, 256:]
        pre_send(j).wait_recv()
        for m in range(2):
            high = pl.ds(m * 512, 512)
            low = (mm(h2t[0, high, :], pre[:, mine]) + mm(h2t[1, high, :], pre_sib[j])).astype(bf16)
            loc_b[4 * j + 2 * m] = low[:256]
            loc_b[4 * j + 2 * m + 1] = low[256:]

    for i in range(4):
        h2t_send(i).wait_recv()
    hidden_pair(0)
    chunk(0)
    for j in range(1, 4):
        sm.step(j - 1)
        hidden_pair(j)
    sm.step(3)

    def x_send(name, n, src, dst):
        return rc(name, n, src.at[:, cols(n, 256)], dst.at[:, cols(n, 256)], to_x)

    def back_two(n):
        xs0[:, cols(n, 512)] = mm_nt(pre[...], wup[cols(n, 512), :]).astype(bf16)
        x_send("x0", 2 * n, xs0, xr0).start()
        x_send("x0", 2 * n + 1, xs0, xr0).start()

    loop(width // 512, back_two)
    chunk(1)
    sm.step(4)

    def forward_two(n):
        xs1[:, cols(n, 512)] = mm(act[...], wdown[:, cols(n, 512)]).astype(bf16)
        x_send("x1", 2 * n, xs1, xr1).start()
        x_send("x1", 2 * n + 1, xs1, xr1).start()

    loop(width // 512, forward_two)
    sm.step(5)
    chunk(2)
    sm.step(6)
    chunk(3)
    sm.step(7)

    for i in range(4):
        h2t_send(i).wait_send()
    h1t = h2t

    def turn_first(i):
        r = pl.ds(pl.multiple_of(i * nrow, nrow), nrow)
        h1t[0, :, cols(i, nrow)] = hid[r, :].T

    loop(rows // nrow, turn_first, True)
    h1t_out = rc("h1t", 0, h1t.at[0], h1t.at[1], to_sib)

    def cot_sum(i, total):
        r = pl.ds(pl.multiple_of(i * tile, tile), tile)
        return total + split_rows(cpair[0, r, :].astype(f32))

    total = lax.fori_loop(0, rows // tile, cot_sum, jnp.zeros((8, width), f32), unroll=True)
    small[pl.ds(8, 1), :] = jnp.sum(total, axis=0, keepdims=True)
    sm.steps(8, 10)

    for n in range(4):
        x_send("x0", n, xs0, xr0).wait_recv()
    sums[...] = jnp.zeros_like(sums)
    back = 256
    dyb = xr0

    def norm_two_back(i):
        r = pl.ds(pl.multiple_of(i * back, back), back)
        g = xs0[r, :].astype(f32) + xr0[r, :].astype(f32)
        n2, r2 = normed(y1[r, :])
        gn = g * n2
        sums[0] += split_rows(gn)
        sums[1] += split_rows(g)
        e2 = g * mgain[...]
        m1 = jnp.mean(e2, axis=-1, keepdims=True)
        m2 = jnp.mean(e2 * n2, axis=-1, keepdims=True)
        d = cpair[0, r, :].astype(f32) + r2 * (e2 - m1 - n2 * m2)
        sums[2] += split_rows(d)
        dy1[r, :] = d
        dyb[r, :] = d.astype(bf16)

    loop(rows // back, norm_two_back)
    dyb_out = rc("dyb", 0, dyb, wout.at[1 - t], to_sib)
    dyb_out.start()
    for i, row in enumerate((4, 5, 3)):
        small[pl.ds(row, 1), :] = jnp.sum(sums[i], axis=0, keepdims=True)
    for n in range(4):
        x_send("x0", n, xs0, xr0).wait_send()

    def back_heads(n):
        dob[:, cols(n, 256)] = mm_nt(dyb[...], wout[t, cols(n, 256), :]).astype(bf16)

    sm.step(10)
    loop(heads_w // 256, back_heads)
    osib_send(0).wait_recv()
    osib_send(1).wait_recv()
    dyb_out.wait_recv()
    h1t_out.start()
    for n in range(width // 512):
        wide = pl.ds(n * 512, 512)
        low = (
            mm_tn(o_own[:, cols(core, 256)], dyb[:, wide]) + mm_tn(o_sib[...], wout[1 - t, :, wide])
        ).astype(bf16)
        loc_a[16 + 2 * n] = low[:, :256]
        loc_a[17 + 2 * n] = low[:, 256:]

    sm.step(11)

    def dqkv_send(w, m, src, pr):
        return rc("dqkv", 2 * w + m, src.at[:, cols(pr)], act_sib.at[w, :, cols(m)], to_sib)

    def attend_back(pr):
        c2 = cols(pr)
        same = same_clip(0, rows)
        dq = dk = dv = None
        for e in range(2):
            q_e, do_e = half_of(q[:, c2], e), half_of(dob[:, c2], e)
            p = softmax(mm_nt(q_e, k[:, c2]), same)
            dp = mm_nt(do_e, v[:, c2])
            ds = (p * (dp - jnp.sum(p * dp, axis=1, keepdims=True))).astype(bf16)
            terms = (
                mm(ds, half_of(k[:, c2], e)) * 0.125,
                mm_tn(ds, q_e),
                mm_tn(p.astype(bf16), do_e),
            )
            dq, dk, dv = terms if dq is None else (dq + terms[0], dk + terms[1], dv + terms[2])
        q[:, c2] = dq.astype(bf16)
        k[:, c2] = dk.astype(bf16)
        v[:, c2] = dv.astype(bf16)
        small[pl.ds(2, 1), c2] = jnp.sum(q[:, c2].astype(f32), axis=0, keepdims=True)
        small[pl.ds(2, 1), cols(pr + 4)] = jnp.sum(v[:, c2].astype(f32), axis=0, keepdims=True)

    def theirs(m):
        pr = 2 * (1 - core) + m
        attend_back(pr)
        for w, src in enumerate((q, k, v)):
            dqkv_send(w, m, src, pr).start()

    loop(2, theirs)
    sm.step(12)

    def ours(m):
        attend_back(2 * core + m)

    loop(2, ours)
    sm.step(13)
    h1t_out.wait_recv()
    for w, src in enumerate((q, k, v)):
        for m in range(2):
            dqkv_send(w, m, src, m).wait_recv()
        for m in range(4):
            high = pl.ds(m * 256, 256)
            low = mm(h1t[0, high, :], src[:, cols(core, 256)]) + mm(h1t[1, high, :], act_sib[w])
            at = 3 * m + w
            if at < 4:
                loc_a[20 + at] = low.astype(bf16)
            else:
                loc_b[12 + at] = low.astype(bf16)
    sm.step(14)

    last = wup.at[pl.ds(0, rows), pl.ds(0, width)]

    def back_one(n):
        c4 = cols(n, 256)
        xs0[:, c4] = (
            mm_nt(q[...], wqkv[0, c4, :]) + mm_nt(k[...], wqkv[1, c4, :]) + mm_nt(v[...], wqkv[2, c4, :])
        ).astype(bf16)
        x_send("x2", n, xs0, last).start()

    loop(width // 256, back_one)
    sm.steps(15, 18)

    for n in range(4):
        x_send("x1", n, xs1, xr1).wait_recv()

    def finish(i):
        r = pl.ds(pl.multiple_of(i * tile, tile), tile)
        hid[r, :] = (
            y1[r, :] + (xs1[r, :].astype(f32) + xr1[r, :].astype(f32)) + downb[...]
        ).astype(bf16)

    loop(rows // tile, finish, True)
    lo_out = load(6, hid, lo_h)
    lo_out.start()

    sm.steps(18, 27)
    for n in range(4):
        x_send("x2", n, xs0, last).wait_recv()
    sums[...] = jnp.zeros_like(sums)

    def norm_one_back(i):
        r = pl.ds(pl.multiple_of(i * back, back), back)
        g = xs0[r, :].astype(f32) + last[r, :].astype(f32)
        n1, r1 = normed(tok[r, :].astype(f32))
        gn = g * n1
        sums[0] += split_rows(gn)
        sums[1] += split_rows(g)
        e1 = g * again[...]
        m1 = jnp.mean(e1, axis=-1, keepdims=True)
        m2 = jnp.mean(e1 * n1, axis=-1, keepdims=True)
        tok[r, :] = (dy1[r, :] + r1 * (e1 - m1 - n1 * m2)).astype(bf16)

    loop(rows // back, norm_one_back)
    gt_out = load(7, tok, gt_h)
    gt_out.start()
    for i, row in enumerate((0, 1)):
        small[pl.ds(row, 1), :] = jnp.sum(sums[i], axis=0, keepdims=True)

    def small_rc(i, src, to):
        return rc("small", i, src, small_r.at[i], to)

    small_sib = small_rc(0, small, to_sib)
    small_y = small_rc(1, small_r.at[0], to_y)
    small_in = small_rc(2, small_r.at[1], sm.to_z)
    small_mid = small_rc(3, small_r.at[2], sm.to_mid)
    small_out = small_rc(4, small_r.at[3], sm.to_z)
    small_sib.start()
    sm.step(27)
    small_sib.wait_recv()
    small_r[0] += small[...]
    small_y.start()
    sm.step(28)
    small_y.wait_recv()
    small_r[1] += small_r[0]

    @pl.when(sm.outer)
    def _():
        small_in.start()

    sm.step(29)

    @pl.when(sm.mid)
    def _():
        small_in.wait_recv()
        small_r[2] += small_r[1]
        small_mid.start()

    sm.step(30)

    @pl.when(sm.mid)
    def _():
        small_mid.wait_recv()
        small_r[3] += small_r[2]
        small_out.start()

    sm.steps(31, END)

    @pl.when(sm.outer)
    def _():
        small_out.wait_recv()

    keep = load(8, small_r.at[jnp.where(sm.outer, 4, 3)], small_h)
    keep.start()

    sm.end()
    w_out.wait_send()
    c_out.wait_send()
    h1t_out.wait_send()
    dyb_out.wait_send()
    for i in range(4):
        o_send(i).wait_send()
        act_send(i).wait_send()
        pre_send(i).wait_send()
        x_send("x1", i, xs1, xr1).wait_send()
        x_send("x2", i, xs0, last).wait_send()
    for m in range(2):
        osib_send(m).wait_send()
        for w, src in enumerate((q, k, v)):
            dqkv_send(w, m, src, m).wait_send()
    small_sib.wait_send()
    small_y.wait_send()

    @pl.when(sm.outer)
    def _():
        small_in.wait_send()

    @pl.when(sm.mid)
    def _():
        small_mid.wait_send()
        small_out.wait_send()

    lo_out.wait()
    gt_out.wait()
    keep.wait()


def layer(clip, vectors, tokens, wqkv, wout, wup, wdown, cot):
    rows, width = tokens.shape
    heads_w = wqkv.shape[2]
    hidden = wup.shape[1]
    big = pl.BlockSpec(memory_space=pl.ANY)
    small = pl.BlockSpec(memory_space=pltpu.VMEM)
    vm = lambda *shape: pltpu.VMEM(shape, bf16)
    vf = lambda *shape: pltpu.VMEM(shape, f32)
    return pl.pallas_call(
        layer_kernel,
        out_shape=(
            jax.ShapeDtypeStruct((rows, width), bf16),
            jax.ShapeDtypeStruct((rows, width), bf16),
            jax.ShapeDtypeStruct((2 * CHUNKS, 2, SIDE, SIDE), bf16),
            jax.ShapeDtypeStruct((16, width), f32),
        ),
        in_specs=[pl.BlockSpec(memory_space=pltpu.SMEM)] + [small] * len(vectors) + [big] * 6,
        out_specs=[big] * 4,
        scratch_shapes=[
            vm(rows, width),
            vm(*wqkv.shape),
            vm(2, *wout.shape),
            vm(*wup.shape),
            vm(*wdown.shape),
            vm(2, rows, width),
            vm(rows, width),
            vm(rows, heads_w),
            vm(rows, heads_w),
            vm(rows, heads_w),
            vm(rows, heads_w),
            vm(rows, heads_w),
            vm(rows, 256),
            vf(rows, width),
            vm(2, width, rows),
            vm(rows, hidden),
            vm(rows, hidden),
            vm(4, rows, 256),
            vm(4, rows, 256),
            vm(rows, width),
            vm(rows, width),
            vm(rows, width),
            vm(rows, width),
            vf(rows, width),
            vm(rows, heads_w),
            vf(16, width),
            vf(5, 16, width),
            vf(3, 8, width),
        ]
        + scratch_of(CHUNKS, SIDE)
        + [
            pltpu.SemaphoreType.DMA((9,)),
            pltpu.SemaphoreType.DMA((N_LINKS,)),
            pltpu.SemaphoreType.DMA((N_LINKS,)),
        ],
        compiler_params=pltpu.CompilerParams(
            has_side_effects=True, collective_id=0, vmem_limit_bytes=VMEM_BYTES
        ),
        name="layer",
    )(clip, *vectors, tokens, wqkv, wout, wup, wdown, cot)


VMEM_BYTES = 60 << 20


STEPS = 8


def widen_kernel(
    down_in, up_in, out_in, qkv_in, s_in, lo_in, gt_in,
    lo, gt, down, out, up, qkv, ag, ash, qv, ob, mg, ms, ub, db,
):
    lo[...] = lo_in[...]
    gt[...] = gt_in[...]
    for n in range(4):
        c = pl.ds(n * SIDE, SIDE)
        down[:, c] = down_in[n, 0].astype(f32)
        out[:, c] = out_in[n, 0].astype(f32)
        up[c, :] = up_in[n, 0].astype(f32)
    for w in range(3):
        for core in range(2):
            qkv[w, :, pl.ds(core * SIDE, SIDE)] = qkv_in[w, core].astype(f32)

    @pl.when(pl.program_id(0) == STEPS - 1)
    def _():
        for ref, row in ((ag, 0), (ash, 1), (ob, 3), (mg, 4), (ms, 5), (db, 8)):
            ref[...] = s_in[pl.ds(row, 1), :]
        qv[pl.ds(0, 1), :] = s_in[pl.ds(2, 1), pl.ds(0, 512)]
        qv[pl.ds(1, 1), :] = s_in[pl.ds(2, 1), pl.ds(512, 512)]
        ub[:, pl.ds(0, 1024)] = s_in[pl.ds(6, 1), :]
        ub[:, pl.ds(1024, 1024)] = s_in[pl.ds(7, 1), :]


def widen(sums, small, lo, gt):
    whole = lambda *shape: pl.BlockSpec(shape, lambda i: (0,) * len(shape))
    rows_in = pl.BlockSpec((lo.shape[0] // STEPS, lo.shape[1]), lambda i: (i, 0))
    vectors = ((1, 1024), (1, 1024), (2, 512), (1, 1024), (1, 1024), (1, 1024), (1, 2048), (1, 1024))
    got = pl.pallas_call(
        widen_kernel,
        grid=(STEPS,),
        in_specs=[
            pl.BlockSpec((4, 1, SIDE, SIDE), lambda i: (i // 2, i % 2, 0, 0)),
            pl.BlockSpec((4, 1, SIDE, SIDE), lambda i: (4 + i // 2, i % 2, 0, 0)),
            pl.BlockSpec((4, 1, SIDE // 4, SIDE), lambda i: (8, i // 4, i % 4, 0)),
            pl.BlockSpec((3, 2, SIDE // 2, SIDE), lambda i: (12 + i // 2, 0, i % 2, 0)),
            whole(16, 1024),
            rows_in,
            rows_in,
        ],
        out_specs=[
            rows_in,
            rows_in,
            pl.BlockSpec((SIDE, 1024), lambda i: (i, 0)),
            pl.BlockSpec((SIDE // 4, 1024), lambda i: (i, 0)),
            pl.BlockSpec((1024, SIDE), lambda i: (0, i)),
            pl.BlockSpec((3, SIDE // 2, 512), lambda i: (0, i, 0)),
        ]
        + [whole(*shape) for shape in vectors],
        out_shape=[
            jax.ShapeDtypeStruct(lo.shape, bf16),
            jax.ShapeDtypeStruct(gt.shape, bf16),
            jax.ShapeDtypeStruct((2048, 1024), f32),
            jax.ShapeDtypeStruct((512, 1024), f32),
            jax.ShapeDtypeStruct((1024, 2048), f32),
            jax.ShapeDtypeStruct((3, 1024, 512), f32),
        ]
        + [jax.ShapeDtypeStruct(shape, f32) for shape in vectors],
        compiler_params=pltpu.CompilerParams(vmem_limit_bytes=56 << 20),
        name="widen",
    )(sums, sums, sums, sums, small, lo, gt)
    lo, gt, down, out, up, qkv, ag, ash, qv, ob, mg, ms, ub, db = got
    flat = lambda v: v.reshape(-1)
    return (
        lo, gt, flat(ag), flat(ash), qkv, qv, out, flat(ob), flat(mg), flat(ms), up, flat(ub),
        down, flat(db),
    )


def local(
    tokens, clip_lengths, attn_gain, attn_shift, qkv_weight, qv_bias, out_weight, out_bias,
    mlp_gain, mlp_shift, up_weight, up_bias, down_weight, down_bias, cotangent,
):
    row = lambda v: v.reshape(1, -1)
    vectors = (
        row(attn_gain), row(attn_shift), qv_bias, row(out_bias), row(mlp_gain), row(mlp_shift),
        row(up_bias), row(down_bias),
    )
    layer_output, grad_tokens, sums, small = layer(
        clip_lengths, vectors, tokens, qkv_weight, out_weight, up_weight, down_weight, cotangent
    )
    groups = lax.axis_size("dp")
    if groups > CELL:
        cells = [[k * CELL + i for k in range(groups // CELL)] for i in range(CELL)]
        sums, small = lax.psum((sums.astype(f32), small), "dp", axis_index_groups=cells)
    return widen(sums, small, layer_output, grad_tokens)


def solution(mesh):
    placed = (
        P("dp", None), P("dp", None), P(), P(), P(None, None, "tensor"), P(None, "tensor"),
        P("tensor", None), P(), P(), P(), P(None, "tensor"), P("tensor"), P("tensor", None), P(),
        P("dp", None),
    )
    return jax.shard_map(
        local,
        mesh=mesh,
        in_specs=placed,
        out_specs=(
            P("dp", None), P("dp", None), P(), P(), P(None, None, "tensor"), P(None, "tensor"),
            P("tensor", None), P(), P(), P(), P(None, "tensor"), P("tensor"), P("tensor", None), P(),
        ),
        check_vma=False,
    )
```
